32 devices in a mesh: dom: 8 (over z, x), slab: 4 (over y, core).
Axes of the slice: x: 2, y: 2, z: 4, core: 2. Of those that a mesh axis runs over, the one named last changes fastest.
Arguments:
- images: bfloat16 [512, 65536], P(('dom', 'slab')), may hold values from -11 to 11
- references: bfloat16 [16, 65536], P('dom'), may hold values from -6 to 6
- offsets: int32 [512, 2], P(('dom', 'slab')), may hold values from -8 to 8
- orientations: int32 [512, 2], P(('dom', 'slab')), may hold values from 0 to 15, as said below
- interp_mats: bfloat16 [8, 128, 128], replicated, may hold values from -0.5 to 0.5
- interp_index: int32 [512, 2], P(('dom', 'slab')), may hold values from 0 to 7
- owners: int32 [512, 512, 1], P(('dom', 'slab')), may hold values from 0 to 31; in each aligned block of 8192 rows (0 to 8191, 8192 to 16383, ..., all dimensions but the last counted through in order) at most 448 rows name the same one
- line_index: int32 [512, 512], P(('dom', 'slab')), may hold values from 0 to 2047
- volume_in: float32 [65536, 256], P(('dom', 'slab')), may hold values from -6 to 6
Outputs:
- volume: float32 [65536, 256], P(('dom', 'slab'))
- evidence: float32 [512], P(('dom', 'slab'))
The draws below stay inside these ranges and needn't reach their ends.
Inputs may be any that keep to these rules, and one draw needn't show every extreme that they name: `orientations`: each particle lists 2 different projections. `owners`: among the rows of one device no owner is named more than 448 times, a bound that some block reaches.
All inputs are finite; a program needn't handle non-finite values.
Results may differ from the reference program's by a relative error of at most 0.0039.
Values may be sent and summed in bfloat16 or wider, within the bound.
No kernel may reach another device: no remote copies, remote signals or barrier semaphores. Data moves between devices by JAX's collectives and lax.ppermute only.
A program may use at most 192 MiB of HBM per device.

```python
import math
import jax
import jax.numpy as jnp
import numpy as np
from jax import lax

FY = 256
FX = 128
VLINES = 65536
TX = 4
TY = 4
OFF = 8
LIST = 2
NQ = 8
IMG_DEV = 16
PARTICLES = 512
PROJ = 16
LINES_DEV = 2048
CAP = 448
DEVICES = 32


def rotate_rows(flat_rows, chosen):
    count = flat_rows.shape[0]
    planes = flat_rows.reshape(count, FY, 2, FX)
    positions = jnp.arange(FY, dtype=jnp.int32)
    freq_rows = jnp.where(positions >= FY // 2, positions - FY, positions)[None, :, None]
    freq_cols = jnp.arange(FX, dtype=jnp.int32)[None, None, :]
    phase_units = jnp.mod(freq_cols * chosen[:, 0][:, None, None] + freq_rows * chosen[:, 1][:, None, None], FY)
    angles = 2.0 * math.pi / FY * phase_units.astype(jnp.float32)
    cosine = jnp.cos(angles)
    sine_part = jnp.sin(angles)
    real_new = planes[:, :, 0] * cosine - planes[:, :, 1] * sine_part
    imag_new = planes[:, :, 0] * sine_part + planes[:, :, 1] * cosine
    return jnp.stack([real_new, imag_new], axis=2).reshape(count, FY * 2 * FX)


def shared_draw(key):
    key_refs = jax.random.fold_in(key, 101)
    key_offsets = jax.random.fold_in(key, 102)
    key_orient = jax.random.fold_in(key, 103)
    key_images = jax.random.fold_in(key, 104)
    key_strength = jax.random.fold_in(key, 106)
    width = FY * 2 * FX
    offsets = jax.random.randint(key_offsets, (PARTICLES, 2), -OFF, OFF + 1, dtype=jnp.int32)
    ranking = jax.random.randint(key_orient, (PARTICLES, PROJ), 0, 1 << 20, dtype=jnp.int32) * PROJ + jnp.arange(PROJ, dtype=jnp.int32)[None, :]
    orientations = jax.lax.top_k(ranking, LIST)[1].astype(jnp.int32)
    strength = (math.log(PROJ * TX * TY) + jax.random.uniform(key_strength, (PARTICLES, LIST), jnp.float32, -1.5, 1.5)) / math.sqrt(width)
    references = jnp.clip(jax.random.normal(key_refs, (PROJ, width), jnp.float32), -6.0, 6.0)
    background = jnp.clip(jax.random.normal(key_images, (PARTICLES, width), jnp.float32), -6.0, 6.0)

    def signal_block(block_args):
        orient_block, offset_block, strength_block = block_args
        combined = references[orient_block[:, 0]] * strength_block[:, 0:1]
        for listed in range(1, LIST):
            combined = combined + references[orient_block[:, listed]] * strength_block[:, listed:listed + 1]
        return rotate_rows(combined, offset_block)
    signal = lax.map(signal_block, (orientations.reshape(-1, 32, LIST), offsets.reshape(-1, 32, 2), strength.reshape(-1, 32, LIST)))
    images = background + signal.reshape(PARTICLES, width)
    return (references, offsets, orientations, images)


def draw_images(key, part):
    return shared_draw(key)[3].astype(jnp.bfloat16)


def draw_references(key, part):
    return shared_draw(key)[0].astype(jnp.bfloat16)


def draw_offsets(key, part):
    return shared_draw(key)[1]


def draw_orientations(key, part):
    return shared_draw(key)[2]


def with_ends(values, own_key, smallest, top_value):
    longest = values.shape.index(max(values.shape))
    spots = []
    for shift in (0, 1):
        where = [jax.random.randint(jax.random.fold_in(own_key, axis), (), 0, length) for axis, length in enumerate(values.shape)]
        where[longest] = (where[longest] + shift) % values.shape[longest]
        spots.append(tuple(where))
    return values.at[spots[0]].set(smallest).at[spots[1]].set(top_value)


def block_scale(stream_key, extent, pieces, low, top_value):
    level = 1.0
    for axis_at, blocks in pieces:
        heights = jax.random.uniform(jax.random.fold_in(jax.random.fold_in(stream_key, 6), axis_at), (blocks,), jnp.float32, low / len(pieces), top_value / len(pieces))
        level = level * jnp.repeat(jnp.exp(heights), extent[axis_at] // blocks).reshape((-1,) + (1,) * (len(extent) - 1 - axis_at))
    return level


def shared_out(own_key, own, number, rows, amount, top, most, skew):
    order = jax.random.permutation(own_key, amount)
    crowded, ordinary = shares(amount, rows * top, most, skew, True), shares(amount, rows * top, most, skew, False)
    places = jnp.arange(amount)

    def named(sizes, turn):
        used = int((sizes > 0).sum())
        fixed = max(1, used // 4)
        passed = fixed + (places - fixed + turn * (used - fixed)) % max(1, amount - fixed)
        return jnp.zeros((amount,), jnp.int32).at[order[jnp.where(places < fixed, places, passed)]].set(jnp.asarray(sizes, jnp.int32))

    sizes = jnp.where(number % 4 == 0, named(crowded, number // 4), named(ordinary, number - number // 4 - 1))
    mixed = jax.random.permutation(jax.random.fold_in(own, 3), amount)
    source_of, sink = mixed[0:amount // 2 * 2:2], mixed[1:amount // 2 * 2:2]
    slack = jnp.minimum(sizes[source_of] - 1, most - sizes[sink]) // 2
    slack = jnp.where((source_of == order[0]) | (sink == order[0]) | (sizes[sink] == 0), 0, jnp.maximum(slack, 0))
    passed = jax.random.randint(jax.random.fold_in(own, 4), (amount // 2,), 0, 1 << 20) % (slack + 1)
    sizes = sizes.at[source_of].add(-passed).at[sink].add(passed)
    items = jnp.searchsorted(jnp.cumsum(sizes), jnp.arange(rows * top), side="right").astype(jnp.int32)
    grid = items.reshape(top, rows).T
    grid = grid[jax.random.permutation(jax.random.fold_in(own, 1), rows)]
    turn = jax.random.randint(jax.random.fold_in(own, 2), (rows, 1), 0, top)
    return jnp.take_along_axis(grid, (jnp.arange(top)[None, :] + turn) % top, axis=1)


def shares(amount, total, reach, lean, full):
    portions = [(1 << 20) // math.isqrt(rank ** lean) + 1 for rank in range(1, amount + 1)]
    largest = reach if full else min(reach, max(-(-total // amount), total * portions[0] // sum(portions)))
    least = 1 if total - largest >= amount - 1 else 0
    holding, spare = [largest] + [least] * (amount - 1), total - largest - least * (amount - 1)
    while spare > 0:
        candidates = [i for i in range(1, amount) if holding[i] < largest] or [i for i in range(1, amount) if holding[i] < reach]
        whole, budget = sum([portions[i] for i in candidates]), spare
        for i in candidates:
            more = min(reach - holding[i], max(1, budget * portions[i] // whole), spare)
            holding[i] = holding[i] + more
            spare = spare - more
    return np.array(holding)


def gaussian(rng, extent, scale, reach, shards=(), held_as=jnp.bfloat16):
    values = jax.random.normal(rng, extent, jnp.float32) * scale
    if len(shards) > 0:
        values = block_scale(rng, extent, shards, -0.22, 0.18) * values
    return jnp.clip(values, min=-reach, max=reach).astype(held_as)


def setup_inputs(seed: int = 0) -> dict:
    key_of = jax.random.split(jax.random.key(seed), 10)
    images = draw_images(jax.random.fold_in(key_of[9], 71), 0)
    references = draw_references(jax.random.fold_in(key_of[9], 71), 0)
    offsets = draw_offsets(jax.random.fold_in(key_of[9], 71), 0)
    orientations = draw_orientations(jax.random.fold_in(key_of[9], 71), 0)
    interp_mats = gaussian(key_of[4], (NQ, FX, FX), FX ** -0.5, 0.5)
    interp_index = with_ends(jax.random.randint(key_of[5], (PARTICLES, LIST), 0, NQ), jax.random.fold_in(key_of[5], 1), 0, NQ - 1).astype(jnp.int32)
    owners_keys = jax.random.split(jax.random.fold_in(key_of[6], 1), PARTICLES * (LIST * FY) // (IMG_DEV * LIST * FY))
    owners_turns = jax.random.permutation(jax.random.fold_in(key_of[6], 3), PARTICLES * (LIST * FY) // (IMG_DEV * LIST * FY))
    owners = jax.vmap(lambda own, number: shared_out(jax.random.fold_in(key_of[6], 2), own, number, IMG_DEV * LIST * FY, DEVICES, 1, CAP, 1))(owners_keys, owners_turns).reshape((PARTICLES, LIST * FY, 1))
    line_index = with_ends(jax.random.randint(key_of[7], (PARTICLES, LIST * FY), 0, LINES_DEV), jax.random.fold_in(key_of[7], 1), 0, LINES_DEV - 1).astype(jnp.int32)
    volume_in = gaussian(key_of[8], (VLINES, 2 * FX), 1.0, 6.0, ((0, 32),), jnp.float32)
    return {"images": images, "references": references, "offsets": offsets, "orientations": orientations, "interp_mats": interp_mats, "interp_index": interp_index, "owners": owners, "line_index": line_index, "volume_in": volume_in}


def signed_rows(number):
    positions = jnp.arange(number, dtype=jnp.int32)
    return jnp.where(positions >= number // 2, positions - number, positions)

def turn_angle(phase_units, period):
    return 2.0 * math.pi / period * jnp.mod(phase_units, period).astype(jnp.float32)

def grid_tables():
    shift_cols = jnp.arange(TX, dtype=jnp.int32) - TX // 2
    shift_rows = jnp.arange(TY, dtype=jnp.int32) - TY // 2
    col_angle = turn_angle(shift_cols[:, None] * jnp.arange(FX, dtype=jnp.int32)[None, :], FY)
    row_angle = turn_angle(shift_rows[:, None] * signed_rows(FY)[None, :], FY)
    return (jnp.cos(col_angle), jnp.sin(col_angle), jnp.cos(row_angle), jnp.sin(row_angle))

def offset_images(images, offsets):
    number = images.shape[0]
    planes = images.astype(jnp.float32).reshape(number, FY, 2, FX)
    freq_rows = signed_rows(FY)[None, :, None]
    freq_cols = jnp.arange(FX, dtype=jnp.int32)[None, None, :]
    angles = -turn_angle(freq_cols * offsets[:, 0][:, None, None] + freq_rows * offsets[:, 1][:, None, None], FY)
    cosine = jnp.cos(angles)
    sine_part = jnp.sin(angles)
    real_part = planes[:, :, 0] * cosine - planes[:, :, 1] * sine_part
    imag_part = planes[:, :, 0] * sine_part + planes[:, :, 1] * cosine
    return (real_part, imag_part)

def search_images(real_part, imag_part, row_cos, row_sin):
    number = real_part.shape[0]
    rot_cos = row_cos[None, :, :, None]
    rot_sin = row_sin[None, :, :, None]
    real_new = real_part[:, None] * rot_cos - imag_part[:, None] * rot_sin
    imag_new = real_part[:, None] * rot_sin + imag_part[:, None] * rot_cos
    stacked = jnp.stack([real_new, imag_new], axis=3)
    return stacked.astype(jnp.bfloat16).reshape(number * TY, FY * 2 * FX)

def shifted_refs(refs, col_cos, col_sin):
    number = refs.shape[0]
    planes = refs.astype(jnp.float32).reshape(number, 1, FY, 2, FX)
    col_cosine = col_cos[None, :, None, :]
    col_sine = col_sin[None, :, None, :]
    real_new = planes[:, :, :, 0] * col_cosine + planes[:, :, :, 1] * col_sine
    imag_new = planes[:, :, :, 1] * col_cosine - planes[:, :, :, 0] * col_sine
    stacked = jnp.stack([real_new, imag_new], axis=3)
    return stacked.astype(jnp.bfloat16).reshape(number * TX, FY * 2 * FX)

def soft_weights(score_grid, orientations):
    number = score_grid.shape[0]
    flat = score_grid.reshape(number, -1)
    row_max = lax.optimization_barrier(jnp.max(flat, axis=1))
    evidence = row_max + jnp.log(lax.optimization_barrier(jnp.sum(jnp.exp(flat - row_max[:, None]), axis=1)))
    one_hot_pick = jax.nn.one_hot(orientations, score_grid.shape[2], dtype=jnp.float32)
    picked = jnp.einsum('ilj,ibja->ilba', one_hot_pick, score_grid, precision=lax.Precision.HIGHEST)
    weights = jnp.exp(picked - evidence[:, None, None, None])
    return (evidence, weights)

def weighted_slices(real_part, imag_part, weights, tables):
    col_cos, col_sin, row_cos, row_sin = tables
    high = lax.Precision.HIGHEST
    gate_real = jnp.einsum('ilba,ac->ilbc', weights, col_cos, precision=high)
    gate_imag = jnp.einsum('ilba,ac->ilbc', weights, col_sin, precision=high)
    phase_real = jnp.einsum('br,ilbc->ilrc', row_cos, gate_real, precision=high) - jnp.einsum('br,ilbc->ilrc', row_sin, gate_imag, precision=high)
    phase_imag = jnp.einsum('br,ilbc->ilrc', row_cos, gate_imag, precision=high) + jnp.einsum('br,ilbc->ilrc', row_sin, gate_real, precision=high)
    image_real = real_part[:, None]
    image_imag = imag_part[:, None]
    slice_real = image_real * phase_real - image_imag * phase_imag
    slice_imag = image_real * phase_imag + image_imag * phase_real
    return jnp.stack([slice_real, slice_imag], axis=3).astype(jnp.bfloat16)

def project_rows(slices, matrices):
    number = slices.shape[0]
    mixed = jnp.einsum('ilrpc,ilcd->ilrpd', slices.astype(jnp.float32), matrices.astype(jnp.float32), precision=lax.Precision.HIGHEST)
    return mixed.astype(jnp.bfloat16).reshape(number, LIST * FY, 2 * FX)

def reference(images, references, offsets, orientations, interp_mats, interp_index, owners, line_index, volume_in):
    tables = grid_tables()
    score_scale = 1.0 / math.sqrt(FY * 2 * FX)
    moved_all = shifted_refs(references, tables[0], tables[1]).astype(jnp.float32)
    block_count = PARTICLES // IMG_DEV

    def scan_step(volume, block_args):
        block_images, block_offsets, block_orient, block_interp, block_owners, block_lines = block_args
        real_part, imag_part = offset_images(block_images, block_offsets)
        searched = search_images(real_part, imag_part, tables[2], tables[3]).astype(jnp.float32)
        scores = jnp.dot(searched, moved_all.T, precision=lax.Precision.HIGHEST) * score_scale
        score_grid = scores.reshape(IMG_DEV, TY, PROJ, TX)
        evidence, weights = soft_weights(score_grid, block_orient)
        slices = weighted_slices(real_part, imag_part, weights, tables)
        matrices = jnp.take(interp_mats, block_interp, axis=0)
        row_values = project_rows(slices, matrices)
        target = (block_owners[:, :, 0] * LINES_DEV + block_lines).reshape(-1).astype(jnp.int32)
        volume = volume.at[target].add(row_values.reshape(-1, 2 * FX).astype(jnp.float32))
        return (volume, evidence)
    stacked_args = tuple((item.reshape((block_count, IMG_DEV) + item.shape[1:]) for item in (images, offsets, orientations, interp_index, owners, line_index)))
    volume, evidence = lax.scan(scan_step, volume_in, stacked_args)
    return (volume, evidence.reshape(PARTICLES))
```

```python
import functools
import math

import jax
import jax.numpy as jnp
import numpy as np
from jax import lax
from jax.experimental import pallas as pl
from jax.experimental.pallas import tpu as pltpu
from jax.sharding import Mesh
from jax.sharding import PartitionSpec as P

FY = 256
FX = 128
TX = 4
TY = 4
LIST = 2
OFF = 8
INNER = 2
F32 = jnp.float32
BF16 = jnp.bfloat16
I32 = jnp.int32
STEP = 2.0 * math.pi / FY
SHIFTS = OFF + max(TX, TY) // 2
NSHIFT = 24


def vmem_params(mib):
    return pltpu.CompilerParams(vmem_limit_bytes=mib << 20)


def whole(shape):
    return pl.BlockSpec(shape, lambda *_: (0,) * len(shape))


def cost(flops, nbytes):
    return pl.CostEstimate(flops=int(flops), bytes_accessed=int(nbytes), transcendentals=0)


def iota(shape, axis):
    return lax.broadcasted_iota(I32, shape, axis)


def split(value):
    high = value.astype(BF16)
    return high, (value - high.astype(F32)).astype(BF16)


def slot_kernel(dests, cap, me_ref, dest_ref, line_ref, slot_ref, meta_ref, hot_ref):
    blocks = dest_ref.shape[0]
    owner_rows = iota((dests, FY), 0)
    for b in range(blocks):
        hot = owner_rows == dest_ref[b : b + 1, :]
        hot_ref[b * dests : (b + 1) * dests, :] = hot.astype(F32).astype(BF16)
    before = (iota((FY, FY), 0) < iota((FY, FY), 1)).astype(F32).astype(BF16)
    prefix = jnp.dot(hot_ref[...], before, preferred_element_type=F32)
    running = jnp.zeros((dests, 1), F32)
    lane = iota((1, FY), 1).astype(F32)
    ranks = iota((cap, FY), 0)
    total = jnp.zeros((4 * dests, cap), F32)
    for b in range(blocks):
        hot = hot_ref[b * dests : (b + 1) * dests, :].astype(F32)
        part = prefix[b * dests : (b + 1) * dests, :]
        rank = jnp.sum(hot * (part + running), axis=0, keepdims=True)
        running = running + part[:, FY - 1 :] + hot[:, FY - 1 :]
        rank_int = rank.astype(I32)
        slot_ref[b : b + 1, :] = dest_ref[b : b + 1, :] * cap + rank_int
        line = line_ref[b : b + 1, :]
        digits = [
            hot * lane,
            hot * float(b),
            hot * (line & 255).astype(F32),
            hot * ((line >> 8) + 1).astype(F32),
        ]
        left = jnp.concatenate(digits, axis=0).astype(BF16)
        right = (ranks == rank_int).astype(F32).astype(BF16)
        total = total + lax.dot_general(
            left, right, (((1,), (1,)), ((), ())), preferred_element_type=F32
        )
    digit = [total[k * dests : (k + 1) * dests, :].astype(I32) for k in range(4)]
    code = (
        digit[0]
        + digit[1] * FY
        + me_ref[0] * (FY * blocks)
        + (digit[2] + (digit[3] - 1) * 256) * 65536
    )
    meta_ref[...] = jnp.where(digit[3] > 0, code, -1)


def row_slots(me, dest, line, dests, cap):
    blocks = dest.shape[0]
    return pl.pallas_call(
        functools.partial(slot_kernel, dests, cap),
        out_shape=(
            jax.ShapeDtypeStruct((blocks, FY), I32),
            jax.ShapeDtypeStruct((dests, cap), I32),
        ),
        in_specs=[
            pl.BlockSpec(memory_space=pltpu.SMEM),
            pl.BlockSpec(memory_space=pltpu.VMEM),
            pl.BlockSpec(memory_space=pltpu.VMEM),
        ],
        scratch_shapes=[pltpu.VMEM((blocks * dests, FY), BF16)],
        compiler_params=vmem_params(48),
        cost_estimate=cost(2e9, 1e6),
        name="slots",
    )(me, dest, line)


def place_kernel(chunks, slot_ref, image_ref, *refs):
    outs, source, buffer = refs[:chunks], refs[chunks], refs[chunks + 1]
    number, width = image_ref.shape
    slots = buffer.shape[0]
    step = 4096

    def widen(k, carry):
        at = pl.ds(pl.multiple_of(k * step, step), step)
        source[:, at] = image_ref[:, at].astype(F32)
        return carry

    lax.fori_loop(0, width // step, widen, 0)
    fill = slots // 56
    zeros = jnp.zeros((fill, 2 * FX), F32)

    def clear(k, carry):
        buffer[pl.ds(pl.multiple_of(k * fill, fill), fill), :] = zeros
        return carry

    lax.fori_loop(0, 56, clear, 0)

    def place(r, carry):
        at = pl.ds(pl.multiple_of(r * 2 * FX, 2 * FX), 2 * FX)
        for n in range(number):
            row = source[n : n + 1, at]
            for which in range(LIST):
                buffer[pl.ds(slot_ref[n * LIST + which, r], 1), :] = row
        return carry

    lax.fori_loop(0, FY, place, 0)
    rows = slots // chunks
    part = rows // 7
    for k in range(chunks):

        def narrow(i, carry, k=k):
            at = pl.multiple_of(i * part, part)
            outs[k][pl.ds(at, part), :] = buffer[pl.ds(k * rows + at, part), :].astype(BF16)
            return carry

        lax.fori_loop(0, 7, narrow, 0)


def placed_rows(slots, images, chunks, rows):
    number, width = images.shape
    return pl.pallas_call(
        functools.partial(place_kernel, chunks),
        out_shape=[jax.ShapeDtypeStruct((rows, 2 * FX), BF16)] * chunks,
        in_specs=[
            pl.BlockSpec(memory_space=pltpu.SMEM),
            pl.BlockSpec(memory_space=pltpu.VMEM),
        ],
        out_specs=[pl.BlockSpec(memory_space=pltpu.VMEM)] * chunks,
        scratch_shapes=[
            pltpu.VMEM((number, width), F32),
            pltpu.VMEM((chunks * rows, 2 * FX), F32),
        ],
        compiler_params=vmem_params(48),
        cost_estimate=cost(1e6, 30e6),
        name="place",
    )(slots, images)


def rotate(real, imag, cosine, sine):
    return real * cosine - imag * sine, real * sine + imag * cosine


def score_kernel(
    half_ref, turn_ref, image_ref, near_ref, far_ref, offset_ref, orient_ref, interp_ref,
    table_ref, evidence_ref,
):
    number = image_ref.shape[0]
    refs = near_ref.shape[0]
    rows_half = FY // 2
    group = 8
    off_x = offset_ref[:, 0:1]
    off_y = offset_ref[:, 1:2]
    lane = iota((number, FX), 1)

    def wave(units):
        angle = STEP * (units & (FY - 1)).astype(F32)
        return jnp.cos(angle), jnp.sin(angle)

    col_cos, col_sin = wave(-lane * off_x)
    one_cos, one_sin = wave(jnp.broadcast_to(-off_y, (number, FX)))
    ref_lane = iota((1, FX), 1)
    x1_cos, x1_sin = wave(jnp.broadcast_to(ref_lane, (refs, FX)))
    x2_cos, x2_sin = wave(jnp.broadcast_to(2 * ref_lane, (refs, FX)))

    def shifts(real, imag, c1, s1, c2, s2):
        rc, rs, ic, is_ = real * c1, real * s1, imag * c1, imag * s1
        pairs = [
            (real * c2 + imag * s2, imag * c2 - real * s2),
            (rc + is_, ic - rs),
            (real, imag),
            (rc - is_, ic + rs),
        ]
        return pairs

    def stacked(pairs):
        return jnp.concatenate(
            [jnp.concatenate([p.astype(BF16), q.astype(BF16)], axis=1) for p, q in pairs],
            axis=0,
        )

    def run(ref, first, total):
        start_cos, start_sin = wave(-(lane * off_x + first * off_y))

        def block(k, carry):
            total, cosine, sine = carry
            lefts, rights = [], []
            for i in range(group):
                r = first + k * group + i
                at = pl.multiple_of(r * 2 * FX, 2 * FX)
                at_ref = pl.multiple_of((k * group + i) * 2 * FX, 2 * FX)
                real = image_ref[:, pl.ds(at, FX)].astype(F32)
                imag = image_ref[:, pl.ds(at + FX, FX)].astype(F32)
                real, imag = rotate(real, imag, cosine, sine)
                cosine, sine = rotate(cosine, sine, one_cos, one_sin)
                lefts.append(
                    stacked(
                        shifts(
                            real, imag, turn_ref[0, r], turn_ref[1, r], turn_ref[2, r], turn_ref[3, r]
                        )
                    )
                )
                real = ref[:, pl.ds(at_ref, FX)].astype(F32)
                imag = ref[:, pl.ds(at_ref + FX, FX)].astype(F32)
                rights.append(stacked(shifts(real, imag, x1_cos, -x1_sin, x2_cos, -x2_sin)))
            total = total + lax.dot_general(
                jnp.concatenate(lefts, axis=1),
                jnp.concatenate(rights, axis=1),
                (((1,), (1,)), ((), ())),
                preferred_element_type=F32,
            )
            return total, cosine, sine

        total, _, _ = lax.fori_loop(0, rows_half // group, block, (total, start_cos, start_sin))
        return total

    half = half_ref[0]
    total = jnp.zeros((TY * number, TX * refs), F32)
    total = run(near_ref, half * rows_half, total)
    total = run(far_ref, (1 - half) * rows_half, total)
    total = total * (1.0 / math.sqrt(FY * 2 * FX))
    parts = [total[b * number : (b + 1) * number, :] for b in range(TY)]
    top = functools.reduce(jnp.maximum, parts)
    top = jnp.max(top, axis=1, keepdims=True)
    mass = sum(jnp.sum(jnp.exp(part - top), axis=1, keepdims=True) for part in parts)
    evidence = top + jnp.log(mass)
    evidence_ref[...] = jnp.broadcast_to(evidence, (number, FX))
    wide = iota((number, TX * refs), 1)
    slot = iota((number, FX), 1)
    table = jnp.where(slot == 32, off_x.astype(F32), 0.0)
    table = jnp.where(slot == 33, off_y.astype(F32), table)
    for l in range(LIST):
        table = jnp.where(slot == 34 + l, interp_ref[:, l : l + 1].astype(F32), table)
        for b in range(TY):
            weights = jnp.exp(parts[b] - evidence)
            for a in range(TX):
                chosen = wide == a * refs + orient_ref[:, l : l + 1]
                value = jnp.sum(jnp.where(chosen, weights, 0.0), axis=1, keepdims=True)
                table = jnp.where(slot == l * 16 + b * TX + a, value, table)
    table_ref[...] = table


def weights_table(half, images, near, far, offsets, orientations, interp_index):
    number = images.shape[0]
    turn = np.arange(FY) * STEP
    turns = np.stack([np.cos(turn), np.sin(turn), np.cos(2 * turn), np.sin(2 * turn)])
    smem = pl.BlockSpec(memory_space=pltpu.SMEM)
    vmem = pl.BlockSpec(memory_space=pltpu.VMEM)
    return pl.pallas_call(
        score_kernel,
        out_shape=[jax.ShapeDtypeStruct((number, FX), F32)] * 2,
        in_specs=[smem, smem] + [vmem] * 6,
        compiler_params=vmem_params(40),
        cost_estimate=cost(3e9, 5e6),
        name="scores",
    )(
        half, jnp.asarray(turns, F32), images, near, far, offsets, orientations, interp_index
    )


def wave_table():
    shift = np.arange(NSHIFT)[:, None] - SHIFTS
    angle = STEP * ((shift * np.arange(FX)[None, :]) % FY)
    table = np.concatenate(
        [
            np.concatenate([np.cos(angle), np.sin(angle)], axis=1),
            np.concatenate([-np.sin(angle), np.cos(angle)], axis=1),
        ],
        axis=0,
    ).astype(np.float32)
    high = table.astype(jnp.bfloat16)
    low = (table - high.astype(np.float32)).astype(jnp.bfloat16)
    return np.concatenate([high, high, low], axis=0)


def gather_kernel(code_ref, row_ref, table_ref, wave_ref, mats_ref, out_ref, mixed_ref):
    rows = row_ref.shape[0]
    lines = out_ref.shape[0]
    members = table_ref.shape[0]
    count = mats_ref.shape[0]
    size = rows // 7
    per = FY * LIST
    table = table_ref[:, :64]
    table_high, table_low = split(table)
    picks = jnp.concatenate([table_high, table_low], axis=1)

    def block(k, carry):
        at = pl.multiple_of(k * size, size)
        code = code_ref[:, pl.ds(at, size)]
        r = code & (FY - 1)
        which = (code >> 8) & 1
        member = (code >> 9) & (members - 1)
        hot = (iota((members, size), 0) == member).astype(F32).astype(BF16)
        got = lax.dot_general(picks, hot, (((0,), (0,)), ((), ())), preferred_element_type=F32)
        got = got[:64] + got[64:]
        first = which == 0
        weight = jnp.where(first, got[0:16], got[16:32])
        off_x = got[32:33].astype(I32)
        off_y = got[33:34].astype(I32)
        interp = jnp.where(first, got[34:35], got[35:36])
        sub = iota((8, size), 0)
        units = r * ((sub & 3) - TY // 2 - off_y) - jnp.where(sub >= 4, FY // 4, 0)
        wave = jnp.cos(STEP * (units & (FY - 1)).astype(F32))
        gate_real = sum(weight[b * TX : (b + 1) * TX] * wave[b : b + 1] for b in range(TY))
        gate_imag = sum(weight[b * TX : (b + 1) * TX] * wave[4 + b : 5 + b] for b in range(TY))
        spot = iota((NSHIFT, size), 0) + off_x
        coef_real = jnp.zeros((NSHIFT, size), F32)
        coef_imag = jnp.zeros((NSHIFT, size), F32)
        for a in range(TX):
            here = spot == a - TX // 2 + SHIFTS
            coef_real = jnp.where(here, gate_real[a : a + 1], coef_real)
            coef_imag = jnp.where(here, gate_imag[a : a + 1], coef_imag)
        high, low = split(jnp.concatenate([coef_real, coef_imag], axis=0))
        coef = jnp.concatenate([high, low, high], axis=0)
        phase = lax.dot_general(
            coef, wave_ref[...], (((0,), (0,)), ((), ())), preferred_element_type=F32
        )
        values = row_ref[pl.ds(at, size), :].astype(F32)
        real, imag = rotate(values[:, :FX], values[:, FX:], phase[:, :FX], phase[:, FX:])
        slices = jnp.concatenate([real, imag], axis=0).astype(BF16)
        column = jnp.transpose(jnp.broadcast_to(interp, (8, size)))[:, 0:1]
        column = jnp.broadcast_to(column, (size, FX))
        column = jnp.concatenate([column, column], axis=0)
        pieces = [
            jnp.where(column == float(q), slices, jnp.zeros_like(slices)) for q in range(count)
        ]
        mixed = jnp.dot(
            jnp.concatenate(pieces, axis=1),
            mats_ref[...].reshape(count * FX, FX),
            preferred_element_type=F32,
        ).astype(BF16)
        mixed_ref[pl.ds(at, size), :FX] = mixed[:size]
        mixed_ref[pl.ds(at, size), FX:] = mixed[size:]
        return carry

    lax.fori_loop(0, 7, block, 0)
    tile = 256
    line = code_ref[...] >> 16

    def gather(t, carry):
        at = pl.multiple_of(t * tile, tile)
        hot = (iota((tile, rows), 0) + at == line).astype(F32).astype(BF16)
        out_ref[pl.ds(at, tile), :] = jnp.dot(hot, mixed_ref[...], preferred_element_type=F32)
        return carry

    lax.fori_loop(0, lines // tile, gather, 0)


def partial_lines(code, rows, table, mats, lines):
    number = rows.shape[0]
    vmem = pl.BlockSpec(memory_space=pltpu.VMEM)
    return pl.pallas_call(
        gather_kernel,
        out_shape=jax.ShapeDtypeStruct((lines, 2 * FX), F32),
        in_specs=[vmem] * 5,
        scratch_shapes=[pltpu.VMEM((number, 2 * FX), BF16)],
        compiler_params=vmem_params(40),
        cost_estimate=cost(2 * number * 2 * FX * lines + 4e9, 6e6),
        name="lines",
    )(code, rows, table, jnp.asarray(wave_table()), mats)


def block_order(planes):
    return np.array(
        [sorted(range(planes), key=lambda d: (-abs(d - z), -d)) for z in range(planes)], np.int32
    )


def body(
    planes, inner, slab,
    images, references, offsets, orientations, interp_mats, interp_index, owners, line_index, volume_in,
):
    number = images.shape[0]
    lines = volume_in.shape[0]
    group = inner * slab
    devices = planes * group
    rows_all = number * LIST * FY
    cap = max(2, 7 * rows_all // (4 * devices))
    rows = group * cap
    z = lax.axis_index("z")
    member = lax.axis_index("x") * slab + lax.axis_index("slab")
    half = lax.axis_index("slab") % 2

    local = references.shape[0]
    width = references.shape[1]
    mine = lax.dynamic_slice_in_dim(references, half * (width // 2), width // 2, axis=1)
    near = lax.all_to_all(
        jnp.broadcast_to(mine[None], (planes * inner,) + mine.shape), ("z", "x"), 0, 0, tiled=True
    ).reshape(planes * inner * local, width // 2)
    far = lax.ppermute(near, "slab", [(i, i ^ 1) for i in range(slab)])

    order = block_order(planes)
    place_of = np.argsort(order, axis=1).astype(np.int32)
    owner = owners.reshape(number * LIST, FY)
    line = line_index.reshape(number * LIST, FY)
    to_place = jnp.asarray(place_of)[z]
    plane_of = owner // group
    chunk_of = sum(jnp.where(plane_of == k, to_place[k], 0) for k in range(planes))
    dest = chunk_of * group + owner % group
    slots, meta = row_slots(member.reshape(1).astype(I32), dest, line, devices, cap)
    sent = placed_rows(slots, images, planes, rows)
    got_meta = lax.all_to_all(
        meta.reshape(planes, group, cap), ("x", "slab"), 1, 1, tiled=True
    ).reshape(planes, 1, rows)
    got = [
        lax.all_to_all(block.reshape(group, cap, 2 * FX), ("x", "slab"), 0, 0, tiled=True).reshape(
            rows, 2 * FX
        )
        for block in sent
    ]

    table, evidence = weights_table(
        half.reshape(1).astype(I32), images, near, far, offsets, orientations, interp_index
    )
    tables = lax.all_to_all(
        jnp.broadcast_to(table[None], (group,) + table.shape), ("x", "slab"), 0, 0, tiled=True
    ).reshape(group * number, FX)
    parts = [
        partial_lines(got_meta[k], got[k], tables, interp_mats, lines) for k in range(planes)
    ]

    def chosen(index):
        wanted = sorted(set(index.tolist()))
        at = jnp.asarray(index)[z]
        value = parts[wanted[-1]]
        for k in wanted[:-1]:
            value = jnp.where(at == k, parts[k], value)
        return value

    up = down = None
    for s in range(1, planes):
        up_at = np.array([place_of[p, planes - s + p] if p < s else place_of[0, planes - s] for p in range(planes)])
        down_at = np.array(
            [
                place_of[p, p - planes + s] if p >= planes - s else place_of[planes - 1, s - 1]
                for p in range(planes)
            ]
        )
        up_send, down_send = chosen(up_at), chosen(down_at)
        if s > 1:
            up_send = up_send + up.astype(F32)
            down_send = down_send + down.astype(F32)
        up = lax.ppermute(up_send.astype(BF16), "z", [(p, p + 1) for p in range(s)])
        down = lax.ppermute(
            down_send.astype(BF16), "z", [(p, p - 1) for p in range(planes - s, planes)]
        )
    volume = volume_in + parts[planes - 1] + up.astype(F32) + down.astype(F32)
    return volume, evidence[:, 0]


def solution(mesh):
    dom, slab = mesh.shape["dom"], mesh.shape["slab"]
    planes = dom // INNER
    fine = Mesh(mesh.devices.reshape(planes, INNER, slab), ("z", "x", "slab"))
    every = ("z", "x", "slab")
    in_specs = (
        P(every, None),
        P(("z", "x"), None),
        P(every, None),
        P(every, None),
        P(),
        P(every, None),
        P(every, None, None),
        P(every, None),
        P(every, None),
    )
    out_specs = (P(every, None), P(every))
    return jax.shard_map(
        functools.partial(body, planes, INNER, slab),
        mesh=fine,
        in_specs=in_specs,
        out_specs=out_specs,
        check_vma=False,
    )
```

```python
import functools
import math

import jax
import jax.numpy as jnp
import numpy as np
from jax import lax
from jax.experimental import pallas as pl
from jax.experimental.pallas import tpu as pltpu
from jax.sharding import Mesh
from jax.sharding import PartitionSpec as P

FY = 256
FX = 128
TX = 4
TY = 4
LIST = 2
OFF = 8
INNER = 2
F32 = jnp.float32
BF16 = jnp.bfloat16
I32 = jnp.int32
STEP = 2.0 * math.pi / FY
SHIFTS = OFF + max(TX, TY) // 2
NSHIFT = 24


def vmem_params(mib):
    return pltpu.CompilerParams(vmem_limit_bytes=mib << 20)


def whole(shape):
    return pl.BlockSpec(shape, lambda *_: (0,) * len(shape))


def cost(flops, nbytes):
    return pl.CostEstimate(flops=int(flops), bytes_accessed=int(nbytes), transcendentals=0)


def iota(shape, axis):
    return lax.broadcasted_iota(I32, shape, axis)


def split(value):
    high = value.astype(BF16)
    return high, (value - high.astype(F32)).astype(BF16)


def slot_kernel(
    dests, group, pad, place_ref, owner_ref, line_ref, image_ref,
    index_ref, digit_ref, real_ref, imag_ref, hot_ref,
):
    number = owner_ref.shape[0]
    blocks = number * LIST
    planes = dests // group
    z = lax.axis_index("z")

    def widen(k, carry):
        for i in range(8):
            r = k * 8 + i
            at = pl.multiple_of(r * 2 * FX, 2 * FX)
            to = pl.ds(pl.multiple_of(r * number, number), number)
            real_ref[to, :] = image_ref[:, pl.ds(at, FX)].astype(F32)
            imag_ref[to, :] = image_ref[:, pl.ds(at + FX, FX)].astype(F32)
        return carry

    lax.fori_loop(0, FY // 8, widen, 0)
    owner = owner_ref[...]
    plane = owner // group
    chunk = jnp.zeros_like(owner)
    for k in range(planes):
        chunk = jnp.where(plane == k, place_ref[z, k], chunk)
    dest = chunk * group + (owner & (group - 1))
    owner_rows = iota((dests, FY), 0)
    for b in range(blocks):
        n, l = b // LIST, b % LIST
        hot = owner_rows == dest[n : n + 1, l * FY : (l + 1) * FY]
        hot_ref[b * dests : (b + 1) * dests, :] = hot.astype(F32).astype(BF16)
    before = (iota((FY, FY), 0) < iota((FY, FY), 1)).astype(F32).astype(BF16)
    prefix = jnp.dot(hot_ref[...], before, preferred_element_type=F32)
    running = jnp.zeros((dests, 1), F32)
    lane = iota((1, FY), 1).astype(F32)
    ranks = iota((pad, FY), 0)
    total = jnp.zeros((4 * dests, pad), F32)
    for b in range(blocks):
        n, l = b // LIST, b % LIST
        hot = hot_ref[b * dests : (b + 1) * dests, :].astype(F32)
        part = prefix[b * dests : (b + 1) * dests, :]
        rank = jnp.sum(hot * (part + running), axis=0, keepdims=True).astype(I32)
        running = running + part[:, FY - 1 :] + hot[:, FY - 1 :]
        line = line_ref[n : n + 1, l * FY : (l + 1) * FY]
        digits = [
            hot * lane,
            hot * float(b),
            hot * (line & 255).astype(F32),
            hot * ((line >> 8) + 1).astype(F32),
        ]
        left = jnp.concatenate(digits, axis=0).astype(BF16)
        right = (ranks == rank).astype(F32).astype(BF16)
        total = total + lax.dot_general(
            left, right, (((1,), (1,)), ((), ())), preferred_element_type=F32
        )
    digit_ref[...] = total
    row = total[:dests].astype(I32) * number + (total[dests : 2 * dests].astype(I32) >> 1)
    index_ref[...] = jnp.where(iota((dests, pad), 1) == pad - 1, running.astype(I32), row)


def row_slots(places, owners, lines, images, dests, group, pad):
    number, width = images.shape
    return pl.pallas_call(
        functools.partial(slot_kernel, dests, group, pad),
        out_shape=(
            jax.ShapeDtypeStruct((dests, pad), I32),
            jax.ShapeDtypeStruct((4 * dests, pad), F32),
            pltpu.VMEM((number * FY, FX), F32),
            pltpu.VMEM((number * FY, FX), F32),
        ),
        in_specs=[pl.BlockSpec(memory_space=pltpu.SMEM)]
        + [pl.BlockSpec(memory_space=pltpu.VMEM)] * 3,
        scratch_shapes=[pltpu.VMEM((number * LIST * dests, FY), BF16)],
        compiler_params=vmem_params(24),
        cost_estimate=cost(3e9, 12e6),
        name="slots",
    )(places, owners, lines, images)


def place_kernel(
    chunk, cap, index_ref, digit_ref, real_ref, imag_ref, out_ref, left_ref, right_ref, held, sems
):
    group, pad = index_ref.shape
    dests = digit_ref.shape[0] // 4
    words = pad // (2 * FX)
    span = cap + 16
    zeros = jnp.zeros((group * span, FX), F32)

    left_ref[...] = zeros
    right_ref[...] = zeros
    copies = []
    for d in range(group):
        start = d * span

        def eight(i, inner, d=d, start=start):
            for j in range(8):
                w = i * 8 + j
                at = index_ref[d, w]
                left_ref[pl.ds(start + w, 1), :] = real_ref[pl.ds(at, 1), :]
                right_ref[pl.ds(start + w, 1), :] = imag_ref[pl.ds(at, 1), :]
            return inner

        lax.fori_loop(0, (index_ref[d, pad - 1] + 7) // 8, eight, 0)
        for which in range(4):
            row = which * dests + chunk * group + d
            for word in range(words):
                to = start + cap + which * words + word
                lane = word * 2 * FX
                left_ref[to : to + 1, :] = digit_ref[row : row + 1, lane : lane + FX]
                right_ref[to : to + 1, :] = digit_ref[row : row + 1, lane + FX : lane + 2 * FX]
        at = slice(start, start + span)
        held[at, :FX] = left_ref[at, :].astype(BF16)
        held[at, FX:] = right_ref[at, :].astype(BF16)
        copies.append(pltpu.make_async_copy(held.at[at], out_ref.at[at], sems.at[d]))
        copies[-1].start()
    for copy in copies:
        copy.wait()


def placed_rows(chunk, group, cap, index, digits, real, imag):
    pad = index.shape[1]
    span = cap + 16
    vmem = pl.BlockSpec(memory_space=pltpu.VMEM)
    return pl.pallas_call(
        functools.partial(place_kernel, chunk, cap),
        grid=(1,),
        out_shape=pltpu.HBM((group * span, 2 * FX), BF16),
        in_specs=[
            pl.BlockSpec((group, pad), lambda i: (chunk, 0), memory_space=pltpu.SMEM),
            vmem,
            vmem,
            vmem,
        ],
        out_specs=pl.BlockSpec(memory_space=pltpu.HBM),
        scratch_shapes=[pltpu.VMEM((group * span, FX), F32)] * 2
        + [pltpu.VMEM((group * span, 2 * FX), BF16), pltpu.SemaphoreType.DMA((group,))],
        compiler_params=vmem_params(16),
        cost_estimate=cost(1e6, 8e6),
        name="place",
    )(index, digits, real, imag)


def rotate(real, imag, cosine, sine):
    return real * cosine - imag * sine, real * sine + imag * cosine


def score_kernel(
    planes, inner, half_ref, turn_ref, image_ref, near_ref, far_ref, offset_ref, orient_ref, interp_ref,
    table_ref, evidence_ref,
):
    number = image_ref.shape[0]
    refs = near_ref.shape[0]
    rows_half = FY // 2
    group = 8
    off_x = offset_ref[:, 0:1]
    off_y = offset_ref[:, 1:2]
    lane = iota((number, FX), 1)

    def wave(units):
        angle = STEP * (units & (FY - 1)).astype(F32)
        return jnp.cos(angle), jnp.sin(angle)

    col_cos, col_sin = wave(-lane * off_x)
    one_cos, one_sin = wave(jnp.broadcast_to(-off_y, (number, FX)))
    ref_lane = iota((1, FX), 1)
    x1_cos, x1_sin = wave(jnp.broadcast_to(ref_lane, (refs, FX)))
    x2_cos, x2_sin = wave(jnp.broadcast_to(2 * ref_lane, (refs, FX)))

    def shifts(real, imag, c1, s1, c2, s2):
        rc, rs, ic, is_ = real * c1, real * s1, imag * c1, imag * s1
        pairs = [
            (real * c2 + imag * s2, imag * c2 - real * s2),
            (rc + is_, ic - rs),
            (real, imag),
            (rc - is_, ic + rs),
        ]
        return pairs

    def stacked(pairs):
        return jnp.concatenate(
            [jnp.concatenate([p.astype(BF16), q.astype(BF16)], axis=1) for p, q in pairs],
            axis=0,
        )

    def run(ref, first, total):
        start_cos, start_sin = wave(-(lane * off_x + first * off_y))

        def block(k, carry):
            total, cosine, sine = carry
            lefts, rights = [], []
            for i in range(group):
                r = first + k * group + i
                at = pl.multiple_of(r * 2 * FX, 2 * FX)
                at_ref = pl.multiple_of((k * group + i) * 2 * FX, 2 * FX)
                real = image_ref[:, pl.ds(at, FX)].astype(F32)
                imag = image_ref[:, pl.ds(at + FX, FX)].astype(F32)
                real, imag = rotate(real, imag, cosine, sine)
                cosine, sine = rotate(cosine, sine, one_cos, one_sin)
                lefts.append(
                    stacked(
                        shifts(
                            real, imag, turn_ref[0, r], turn_ref[1, r], turn_ref[2, r], turn_ref[3, r]
                        )
                    )
                )
                real = ref[:, pl.ds(at_ref, FX)].astype(F32)
                imag = ref[:, pl.ds(at_ref + FX, FX)].astype(F32)
                rights.append(stacked(shifts(real, imag, x1_cos, -x1_sin, x2_cos, -x2_sin)))
            total = total + lax.dot_general(
                jnp.concatenate(lefts, axis=1),
                jnp.concatenate(rights, axis=1),
                (((1,), (1,)), ((), ())),
                preferred_element_type=F32,
            )
            return total, cosine, sine

        total, _, _ = lax.fori_loop(0, rows_half // group, block, (total, start_cos, start_sin))
        return total

    half = half_ref[0]
    total = jnp.zeros((TY * number, TX * refs), F32)
    total = run(near_ref, half * rows_half, total)
    total = run(far_ref, (1 - half) * rows_half, total)
    total = total * (1.0 / math.sqrt(FY * 2 * FX))
    parts = [total[b * number : (b + 1) * number, :] for b in range(TY)]
    top = functools.reduce(jnp.maximum, parts)
    top = jnp.max(top, axis=1, keepdims=True)
    mass = sum(jnp.sum(jnp.exp(part - top), axis=1, keepdims=True) for part in parts)
    evidence = top + jnp.log(mass)
    evidence_ref[...] = jnp.broadcast_to(evidence, (number, FX))
    spot = iota((number, TX * refs), 1)
    shift_of = spot // refs
    spot = spot & (refs - 1)
    local = refs // (planes * inner)
    plane = lax.axis_index("z") - spot // (inner * local)
    plane = jnp.where(plane < 0, plane + planes, plane)
    column = lax.axis_index("x") ^ ((spot // local) & (inner - 1))
    name = (plane * inner + column) * local + (spot & (local - 1))
    slot = iota((number, FX), 1)
    table = jnp.where(slot == 32, off_x.astype(F32), 0.0)
    table = jnp.where(slot == 33, off_y.astype(F32), table)
    for l in range(LIST):
        table = jnp.where(slot == 34 + l, interp_ref[:, l : l + 1].astype(F32), table)
        for b in range(TY):
            weights = jnp.exp(parts[b] - evidence)
            for a in range(TX):
                chosen = (name == orient_ref[:, l : l + 1]) & (shift_of == a)
                value = jnp.sum(jnp.where(chosen, weights, 0.0), axis=1, keepdims=True)
                table = jnp.where(slot == l * 16 + b * TX + a, value, table)
    table_ref[...] = table


def weights_table(planes, inner, half, images, near, far, offsets, orientations, interp_index):
    number = images.shape[0]
    turn = np.arange(FY) * STEP
    turns = np.stack([np.cos(turn), np.sin(turn), np.cos(2 * turn), np.sin(2 * turn)])
    smem = pl.BlockSpec(memory_space=pltpu.SMEM)
    vmem = pl.BlockSpec(memory_space=pltpu.VMEM)
    return pl.pallas_call(
        functools.partial(score_kernel, planes, inner),
        out_shape=[jax.ShapeDtypeStruct((number, FX), F32)] * 2,
        in_specs=[smem, smem] + [vmem] * 6,
        compiler_params=vmem_params(16),
        cost_estimate=cost(3e9, 5e6),
        name="scores",
    )(
        half, jnp.asarray(turns, F32), images, near, far, offsets, orientations, interp_index
    )


def wave_table():
    shift = np.arange(NSHIFT)[:, None] - SHIFTS
    angle = STEP * ((shift * np.arange(FX)[None, :]) % FY)
    table = np.concatenate(
        [
            np.concatenate([np.cos(angle), np.sin(angle)], axis=1),
            np.concatenate([-np.sin(angle), np.cos(angle)], axis=1),
        ],
        axis=0,
    ).astype(np.float32)
    high = table.astype(jnp.bfloat16)
    low = (table - high.astype(np.float32)).astype(jnp.bfloat16)
    return np.concatenate([high, high, low], axis=0)


def gather_kernel(cap, pad, first, row_ref, table_ref, wave_ref, mats_ref, *refs):
    base_ref = refs[0] if first is None else None
    out_ref, mixed_ref, line_ref = refs[1 if first is None else 0], refs[-2], refs[-1]
    lines = out_ref.shape[0]
    members = table_ref.shape[0]
    count = mats_ref.shape[0]
    span = cap + 16
    group = row_ref.shape[0] // span
    words = pad // (2 * FX)
    low_count = count // 2
    table_high, table_low = split(table_ref[:, :64])
    picks = jnp.concatenate([table_high, table_low], axis=1)
    number = members // group
    mats = jnp.concatenate(
        [mats_ref[:low_count].reshape(low_count * FX, FX), mats_ref[low_count:].reshape(low_count * FX, FX)],
        axis=1,
    )
    def block(s, carry):
        at = pl.multiple_of(s * span, 16)
        extra = row_ref[pl.ds(at + cap, 16), :].astype(F32)
        digit = [
            jnp.concatenate(
                [extra[which * words + word : which * words + word + 1] for word in range(words)],
                axis=1,
            )[:, :cap].astype(I32)
            for which in range(4)
        ]
        r = digit[0]
        member = s * number + (digit[1] >> 1)
        front = (digit[1] & 1) == 0
        line_ref[s] = digit[2] + (digit[3] - 1) * 256
        hot = (iota((members, cap), 0) == member).astype(F32).astype(BF16)
        got = lax.dot_general(picks, hot, (((0,), (0,)), ((), ())), preferred_element_type=F32)
        got = got[:64] + got[64:]
        weight = jnp.where(front, got[0:16], got[16:32])
        off_x = got[32:33].astype(I32)
        off_y = got[33:34].astype(I32)
        interp = jnp.where(front, got[34:35], got[35:36])
        sub = iota((8, cap), 0)
        units = r * ((sub & 3) - TY // 2 - off_y) - jnp.where(sub >= 4, FY // 4, 0)
        wave = jnp.cos(STEP * (units & (FY - 1)).astype(F32))
        gate_real = sum(weight[b * TX : (b + 1) * TX] * wave[b : b + 1] for b in range(TY))
        gate_imag = sum(weight[b * TX : (b + 1) * TX] * wave[4 + b : 5 + b] for b in range(TY))
        spot = iota((NSHIFT, cap), 0) + off_x
        coef_real = jnp.zeros((NSHIFT, cap), F32)
        coef_imag = jnp.zeros((NSHIFT, cap), F32)
        for a in range(TX):
            here = spot == a - TX // 2 + SHIFTS
            coef_real = jnp.where(here, gate_real[a : a + 1], coef_real)
            coef_imag = jnp.where(here, gate_imag[a : a + 1], coef_imag)
        high, low = split(jnp.concatenate([coef_real, coef_imag], axis=0))
        coef = jnp.concatenate([high, low, high], axis=0)
        phase = lax.dot_general(
            coef, wave_ref[...], (((0,), (0,)), ((), ())), preferred_element_type=F32
        )
        values = row_ref[pl.ds(at, cap), :].astype(F32)
        real, imag = rotate(values[:, :FX], values[:, FX:], phase[:, :FX], phase[:, FX:])
        slices = jnp.concatenate([real, imag], axis=0).astype(BF16)
        column = jnp.transpose(jnp.broadcast_to(interp, (8, cap)))[:, 0:1]
        column = jnp.broadcast_to(column, (cap, FX)).astype(I32)
        column = jnp.concatenate([column, column], axis=0)
        which = jnp.where(column >= low_count, column - low_count, column)
        zero = jnp.zeros_like(slices)
        pieces = [jnp.where(which == q, slices, zero) for q in range(low_count)]
        mixed = jnp.dot(jnp.concatenate(pieces, axis=1), mats, preferred_element_type=F32)
        mixed = jnp.where(column >= low_count, mixed[:, FX:], mixed[:, :FX]).astype(BF16)
        to = pl.ds(pl.multiple_of(s * cap, 16), cap)
        mixed_ref[to, :FX] = mixed[:cap]
        mixed_ref[to, FX:] = mixed[cap:]
        return carry

    lax.fori_loop(0, group, block, 0, unroll=2)
    line = jnp.concatenate([line_ref[s] for s in range(group)], axis=1)
    tile = min(512, lines // 2)
    rows = iota((tile, group * cap), 0)
    for at in range(0, lines, tile):
        hot = jnp.where(rows == line - at, 1.0, 0.0).astype(BF16)
        value = jnp.dot(hot, mixed_ref[...], preferred_element_type=F32)
        if base_ref is not None:
            value = value + base_ref[at : at + tile, :]
        out_ref[at : at + tile, :] = value
        if first:
            piece = refs[1 + at // (lines // 2)]
            spot = at % (lines // 2)
            piece[spot : spot + tile, :] = value.astype(BF16)


def partial_lines(cap, pad, rows, table, mats, lines, first, base=None):
    group = rows.shape[0] // (cap + 16)
    shape = jax.ShapeDtypeStruct((lines, 2 * FX), F32)
    short = jax.ShapeDtypeStruct((lines // 2, 2 * FX), BF16)
    vmem = pl.BlockSpec(memory_space=pltpu.VMEM)
    extra = () if base is None else (base,)
    return pl.pallas_call(
        functools.partial(gather_kernel, cap, pad, None if extra else first),
        out_shape=(shape, short, short) if first else shape,
        in_specs=[vmem] * (4 + len(extra)),
        scratch_shapes=[
            pltpu.VMEM((group * cap, 2 * FX), BF16),
            pltpu.VMEM((group, 1, cap), I32),
        ],
        compiler_params=vmem_params(24),
        cost_estimate=cost(1e6, 1e5),
        name="lines",
    )(rows, table, jnp.asarray(wave_table()), mats, *extra)


def relay_kernel(planes, step, place_of, pieces, *refs):
    refs = list(refs)
    up_out, down_out = refs[-2:]
    downs, ups = refs[-2 - pieces : -2], refs[-2 - 2 * pieces : -2 - pieces]
    parts = refs[: -2 - 2 * pieces]
    z = lax.axis_index("z")
    lines = up_out.shape[0]
    length = lines // pieces
    tile = min(512, length)

    def send(part, came, out):
        for at in range(0, lines, tile):
            value = part[at : at + tile, :]
            if came is not None:
                spot = at % length
                value = value + came[at // length][spot : spot + tile, :].astype(F32)
            out[at : at + tile, :] = value.astype(BF16)

    for p in range(planes):
        goes_up, goes_down = p < step, p >= planes - step
        if goes_up or goes_down:

            @pl.when(z == p)
            def _(p=p, goes_up=goes_up, goes_down=goes_down):
                if goes_up:
                    part = parts[place_of[p, planes - step + p]]
                    send(part, ups if p > 0 else None, up_out)
                if goes_down:
                    part = parts[place_of[p, p - planes + step]]
                    send(part, downs if p < planes - 1 else None, down_out)


def relay(planes, step, place_of, parts, up, down):
    vmem = pl.BlockSpec(memory_space=pltpu.VMEM)
    return pl.pallas_call(
        functools.partial(relay_kernel, planes, step, place_of, len(up)),
        out_shape=[jax.ShapeDtypeStruct(parts[0].shape, BF16)] * 2,
        in_specs=[vmem] * (len(parts) + 2 * len(up)),
        compiler_params=vmem_params(14),
        cost_estimate=cost(1e6, 1e5),
        name="relay",
    )(*parts, *up, *down)


def together(*values):
    return lax.optimization_barrier(values)


def block_order(planes):
    return np.array(
        [sorted(range(planes), key=lambda d: (-abs(d - z), -d)) for z in range(planes)], np.int32
    )


def body(
    planes, inner, slab,
    images, references, offsets, orientations, interp_mats, interp_index, owners, line_index, volume_in,
):
    number = images.shape[0]
    lines = volume_in.shape[0]
    group = inner * slab
    devices = planes * group
    rows_all = number * LIST * FY
    cap = max(2, 7 * rows_all // (4 * devices))
    span = cap + 16
    pad = -(-(cap + 1) // (2 * FX)) * 2 * FX
    half = lax.axis_index("slab") % 2

    local = references.shape[0]
    width = references.shape[1]
    mine = lax.dynamic_slice_in_dim(references, half * (width // 2), width // 2, axis=1)
    block = [mine]
    for e in range(1, inner):
        block.append(lax.ppermute(mine, "x", [(i, i ^ e) for i in range(inner)]))

    place_of = np.argsort(block_order(planes), axis=1).astype(np.int32)
    index, digits, real, imag = row_slots(
        jnp.asarray(place_of),
        owners.reshape(number, LIST * FY),
        line_index,
        images,
        devices,
        group,
        pad,
    )
    block, index = together(block, index)
    block = jnp.concatenate(block, axis=0)
    near = [block]
    for shift in range(1, planes):
        near.append(lax.ppermute(block, "z", [(p, (p + shift) % planes) for p in range(planes)]))
    def place(k, index):
        return placed_rows(k, group, cap, index, digits, real, imag)

    early = min(3, planes)
    placed = [place(k, index) for k in range(early)]

    def to_members(value):
        return lax.all_to_all(
            value.reshape(group, span, 2 * FX), ("x", "slab"), 0, 0, tiled=True
        ).reshape(group * span, 2 * FX)

    got = to_members(placed[0])
    near, placed[1:3] = together(near, placed[1:3])
    near = jnp.concatenate(near, axis=0)
    far = lax.ppermute(near, "slab", [(i, i ^ 1) for i in range(slab)])
    near, far, got = together(near, far, got)
    table, evidence = weights_table(
        planes, inner, half.reshape(1).astype(I32), images, near, far, offsets, orientations,
        interp_index,
    )
    tables = lax.all_to_all(
        jnp.broadcast_to(table[None], (group,) + table.shape), ("x", "slab"), 0, 0, tiled=True
    ).reshape(group * number, FX)
    tables, placed[1] = together(tables, placed[1])
    got = [got, to_members(placed[1])]

    def lines_of(k, base=None):
        return partial_lines(cap, pad, got[k], tables, interp_mats, lines, k == 0, base)

    def fetch(k, value):
        if k < planes:
            value, placed[k] = together(value, placed[k])
            got.append(to_members(placed[k]))
        return value

    part, *short = lines_of(0)
    part, index = together(part, index)
    placed += [place(k, index) for k in range(early, planes)]
    parts = [part]
    ends = sorted({(0, 1), (planes - 1, planes - 2)})
    up = [lax.ppermute(piece, "z", ends) for piece in short]
    up[0] = fetch(2, up[0])
    down = up
    for s in range(2, planes):
        parts.append(fetch(s + 1, lines_of(s - 1)))
        up_send, down_send = relay(planes, s, place_of, parts, up, down)
        up = [lax.ppermute(up_send, "z", [(p, p + 1) for p in range(s)])]
        down = [lax.ppermute(down_send, "z", [(p, p - 1) for p in range(planes - s, planes)])]
    last = lines_of(planes - 1, volume_in)
    volume = last + jnp.concatenate(up, axis=0).astype(F32) + jnp.concatenate(down, axis=0).astype(F32)
    return volume, evidence[:, 0]


def solution(mesh):
    dom, slab = mesh.shape["dom"], mesh.shape["slab"]
    planes = dom // INNER
    fine = Mesh(mesh.devices.reshape(planes, INNER, slab), ("z", "x", "slab"))
    every = ("z", "x", "slab")
    in_specs = (
        P(every, None),
        P(("z", "x"), None),
        P(every, None),
        P(every, None),
        P(),
        P(every, None),
        P(every, None, None),
        P(every, None),
        P(every, None),
    )
    out_specs = (P(every, None), P(every))
    return jax.shard_map(
        functools.partial(body, planes, INNER, slab),
        mesh=fine,
        in_specs=in_specs,
        out_specs=out_specs,
        check_vma=False,
    )
```

```python
import functools
import math

import jax
import jax.numpy as jnp
import numpy as np
from jax import lax
from jax.experimental import pallas as pl
from jax.experimental.pallas import tpu as pltpu
from jax.sharding import Mesh
from jax.sharding import PartitionSpec as P

FY = 256
FX = 128
TX = 4
TY = 4
LIST = 2
OFF = 8
INNER = 2
F32 = jnp.float32
BF16 = jnp.bfloat16
I32 = jnp.int32
STEP = 2.0 * math.pi / FY
SHIFTS = OFF + max(TX, TY) // 2
NSHIFT = 24


def vmem_params(mib):
    return pltpu.CompilerParams(vmem_limit_bytes=mib << 20)


def whole(shape):
    return pl.BlockSpec(shape, lambda *_: (0,) * len(shape))


def cost(flops, nbytes):
    return pl.CostEstimate(flops=int(flops), bytes_accessed=int(nbytes), transcendentals=0)


def iota(shape, axis):
    return lax.broadcasted_iota(I32, shape, axis)


def in_hbm(value):
    return pltpu.with_memory_space_constraint(value, pltpu.HBM)


def split(value):
    high = value.astype(BF16)
    return high, (value - high.astype(F32)).astype(BF16)


def slot_kernel(
    dests, group, pad, place_of, owner_ref, line_from, image_from,
    index_ref, digit_ref, real_ref, imag_ref, hot_ref, line_ref, image_ref, sems,
):
    number = owner_ref.shape[0]
    blocks = number * LIST
    planes = dests // group
    z = lax.axis_index("z")
    lines_in = pltpu.make_async_copy(line_from, line_ref, sems.at[0])
    lines_in.start()
    images_in = pltpu.make_async_copy(image_from, image_ref, sems.at[1])
    images_in.start()

    def widen(k, carry):
        for i in range(8):
            r = k * 8 + i
            at = pl.multiple_of(r * 2 * FX, 2 * FX)
            to = pl.ds(pl.multiple_of(r * number, number), number)
            real_ref[to, :] = image_ref[:, pl.ds(at, FX)].astype(F32)
            imag_ref[to, :] = image_ref[:, pl.ds(at + FX, FX)].astype(F32)
        return carry

    owner = owner_ref[...]
    plane = owner // group
    chunk = jnp.zeros_like(owner)
    for k in range(planes):
        at = functools.reduce(
            lambda value, p: jnp.where(z == p, int(place_of[p, k]), value), range(planes), 0
        )
        chunk = jnp.where(plane == k, at, chunk)
    dest = chunk * group + (owner & (group - 1))
    owner_rows = iota((dests, FY), 0)
    for b in range(blocks):
        n, l = b // LIST, b % LIST
        hot = owner_rows == dest[n : n + 1, l * FY : (l + 1) * FY]
        hot_ref[b * dests : (b + 1) * dests, :] = hot.astype(F32).astype(BF16)
    before = (iota((FY, FY), 0) < iota((FY, FY), 1)).astype(F32).astype(BF16)
    prefix = jnp.dot(hot_ref[...], before, preferred_element_type=F32)
    lines_in.wait()
    running = jnp.zeros((dests, 1), F32)
    lane = iota((1, FY), 1).astype(F32)
    ranks = iota((pad, FY), 0)
    total = jnp.zeros((4 * dests, pad), F32)
    for b in range(blocks):
        n, l = b // LIST, b % LIST
        hot = hot_ref[b * dests : (b + 1) * dests, :].astype(F32)
        part = prefix[b * dests : (b + 1) * dests, :]
        rank = jnp.sum(hot * (part + running), axis=0, keepdims=True).astype(I32)
        running = running + part[:, FY - 1 :] + hot[:, FY - 1 :]
        line = line_ref[n : n + 1, l * FY : (l + 1) * FY]
        digits = [
            hot * lane,
            hot * float(b),
            hot * (line & 255).astype(F32),
            hot * ((line >> 8) + 1).astype(F32),
        ]
        left = jnp.concatenate(digits, axis=0).astype(BF16)
        right = (ranks == rank).astype(F32).astype(BF16)
        total = total + lax.dot_general(
            left, right, (((1,), (1,)), ((), ())), preferred_element_type=F32
        )
    digit_ref[...] = total
    row = total[:dests].astype(I32) * number + (total[dests : 2 * dests].astype(I32) >> 1)
    index_ref[...] = jnp.where(iota((dests, pad), 1) == pad - 1, running.astype(I32), row)
    images_in.wait()
    lax.fori_loop(0, FY // 8, widen, 0)


def row_slots(place_of, owners, lines, images, dests, group, pad):
    number, width = images.shape
    return pl.pallas_call(
        functools.partial(slot_kernel, dests, group, pad, place_of),
        out_shape=(
            jax.ShapeDtypeStruct((dests, pad), I32),
            jax.ShapeDtypeStruct((4 * dests, pad), F32),
            pltpu.VMEM((number * FY, FX), F32),
            pltpu.VMEM((number * FY, FX), F32),
        ),
        in_specs=[pl.BlockSpec(memory_space=pltpu.VMEM)]
        + [pl.BlockSpec(memory_space=pltpu.HBM)] * 2,
        scratch_shapes=[
            pltpu.VMEM((number * LIST * dests, FY), BF16),
            pltpu.VMEM(lines.shape, I32),
            pltpu.VMEM(images.shape, BF16),
            pltpu.SemaphoreType.DMA((2,)),
        ],
        compiler_params=vmem_params(20),
        cost_estimate=cost(3e9, 12e6),
        name="slots",
    )(owners, in_hbm(lines), in_hbm(images))


def place_kernel(
    chunk, cap, index_ref, digit_ref, real_ref, imag_ref, out_ref, token_ref, left_ref, right_ref,
    held, sems,
):
    group, pad = index_ref.shape
    dests = digit_ref.shape[0] // 4
    words = pad // (2 * FX)
    span = cap + 16
    zeros = jnp.zeros((group * span, FX), F32)

    left_ref[...] = zeros
    right_ref[...] = zeros
    token_ref[...] = jnp.zeros_like(token_ref)
    copies = []
    for d in range(group):
        start = d * span

        def eight(i, inner, d=d, start=start):
            for j in range(8):
                w = i * 8 + j
                at = index_ref[d, w]
                left_ref[pl.ds(start + w, 1), :] = real_ref[pl.ds(at, 1), :]
                right_ref[pl.ds(start + w, 1), :] = imag_ref[pl.ds(at, 1), :]
            return inner

        lax.fori_loop(0, (index_ref[d, pad - 1] + 7) // 8, eight, 0)
        for which in range(4):
            row = which * dests + chunk * group + d
            for word in range(words):
                to = start + cap + which * words + word
                lane = word * 2 * FX
                left_ref[to : to + 1, :] = digit_ref[row : row + 1, lane : lane + FX]
                right_ref[to : to + 1, :] = digit_ref[row : row + 1, lane + FX : lane + 2 * FX]
        at = slice(start, start + span)
        held[at, :FX] = left_ref[at, :].astype(BF16)
        held[at, FX:] = right_ref[at, :].astype(BF16)
        copies.append(pltpu.make_async_copy(held.at[at], out_ref.at[at], sems.at[d]))
        copies[-1].start()
    for copy in copies:
        copy.wait()


def placed_rows(chunk, group, cap, index, digits, real, imag):
    pad = index.shape[1]
    span = cap + 16
    vmem = pl.BlockSpec(memory_space=pltpu.VMEM)
    return pl.pallas_call(
        functools.partial(place_kernel, chunk, cap),
        grid=(1,),
        out_shape=(pltpu.HBM((group * span, 2 * FX), BF16), jax.ShapeDtypeStruct((8, FX), F32)),
        in_specs=[
            pl.BlockSpec((group, pad), lambda i: (chunk, 0), memory_space=pltpu.SMEM),
            vmem,
            vmem,
            vmem,
        ],
        out_specs=(pl.BlockSpec(memory_space=pltpu.HBM), vmem),
        scratch_shapes=[pltpu.VMEM((group * span, FX), F32)] * 2
        + [pltpu.VMEM((group * span, 2 * FX), BF16), pltpu.SemaphoreType.DMA((group,))],
        compiler_params=vmem_params(12),
        cost_estimate=cost(1e5, 1e5),
        name="place",
    )(index, digits, real, imag)


def rotate(real, imag, cosine, sine):
    return real * cosine - imag * sine, real * sine + imag * cosine


def score_kernel(
    planes, inner, half_ref, turn_ref, image_from, near_ref, far_ref, offset_ref, orient_ref,
    interp_ref, token_ref, table_ref, evidence_ref, image_ref, sems,
):
    number = image_ref.shape[0]
    refs = near_ref.shape[0]
    rows_half = FY // 2
    group = 8
    half = half_ref[0]
    copies = []
    for k in range(4):
        side = half if k < 2 else 1 - half
        quarter = FY * FX // 2
        at = pl.ds(pl.multiple_of((side * 2 + k % 2) * quarter, quarter), quarter)
        copies.append(
            pltpu.make_async_copy(image_from.at[:, at], image_ref.at[:, at], sems.at[k])
        )
        copies[-1].start()
    off_x = offset_ref[:, 0:1]
    off_y = offset_ref[:, 1:2]
    lane = iota((number, FX), 1)

    def wave(units):
        angle = STEP * (units & (FY - 1)).astype(F32)
        return jnp.cos(angle), jnp.sin(angle)

    col_cos, col_sin = wave(-lane * off_x)
    one_cos, one_sin = wave(jnp.broadcast_to(-off_y, (number, FX)))
    ref_lane = iota((1, FX), 1)
    x1_cos, x1_sin = wave(jnp.broadcast_to(ref_lane, (refs, FX)))
    x2_cos, x2_sin = wave(jnp.broadcast_to(2 * ref_lane, (refs, FX)))

    def shifts(real, imag, c1, s1, c2, s2):
        rc, rs, ic, is_ = real * c1, real * s1, imag * c1, imag * s1
        pairs = [
            (real * c2 + imag * s2, imag * c2 - real * s2),
            (rc + is_, ic - rs),
            (real, imag),
            (rc - is_, ic + rs),
        ]
        return pairs

    def stacked(pairs):
        return jnp.concatenate(
            [jnp.concatenate([p.astype(BF16), q.astype(BF16)], axis=1) for p, q in pairs],
            axis=0,
        )

    def run(ref, first, total, waits):
        start_cos, start_sin = wave(-(lane * off_x + first * off_y))

        def block(k, carry):
            total, cosine, sine = carry
            lefts, rights = [], []
            for i in range(group):
                r = first + k * group + i
                at = pl.multiple_of(r * 2 * FX, 2 * FX)
                at_ref = pl.multiple_of((k * group + i) * 2 * FX, 2 * FX)
                real = image_ref[:, pl.ds(at, FX)].astype(F32)
                imag = image_ref[:, pl.ds(at + FX, FX)].astype(F32)
                real, imag = rotate(real, imag, cosine, sine)
                cosine, sine = rotate(cosine, sine, one_cos, one_sin)
                lefts.append(
                    stacked(
                        shifts(
                            real, imag, turn_ref[0, r], turn_ref[1, r], turn_ref[2, r], turn_ref[3, r]
                        )
                    )
                )
                real = ref[:, pl.ds(at_ref, FX)].astype(F32)
                imag = ref[:, pl.ds(at_ref + FX, FX)].astype(F32)
                rights.append(stacked(shifts(real, imag, x1_cos, -x1_sin, x2_cos, -x2_sin)))
            total = total + lax.dot_general(
                jnp.concatenate(lefts, axis=1),
                jnp.concatenate(rights, axis=1),
                (((1,), (1,)), ((), ())),
                preferred_element_type=F32,
            )
            return total, cosine, sine

        carry = (total, start_cos, start_sin)
        turns = rows_half // group // len(waits)
        for k, wait in enumerate(waits):
            wait.wait()
            carry = lax.fori_loop(k * turns, (k + 1) * turns, block, carry)
        return carry[0]

    total = jnp.zeros((TY * number, TX * refs), F32)
    total = run(near_ref, half * rows_half, total, copies[:2])
    total = run(far_ref, (1 - half) * rows_half, total, copies[2:])
    total = total * (1.0 / math.sqrt(FY * 2 * FX))
    parts = [total[b * number : (b + 1) * number, :] for b in range(TY)]
    top = functools.reduce(jnp.maximum, parts)
    top = jnp.max(top, axis=1, keepdims=True)
    mass = sum(jnp.sum(jnp.exp(part - top), axis=1, keepdims=True) for part in parts)
    evidence = top + jnp.log(mass)
    evidence_ref[...] = jnp.broadcast_to(evidence, (number, FX))
    spot = iota((number, TX * refs), 1)
    shift_of = spot // refs
    spot = spot & (refs - 1)
    local = refs // (planes * inner)
    plane = lax.axis_index("z") - spot // (inner * local)
    plane = jnp.where(plane < 0, plane + planes, plane)
    column = lax.axis_index("x") ^ ((spot // local) & (inner - 1))
    name = (plane * inner + column) * local + (spot & (local - 1))
    slot = iota((number, FX), 1)
    table = jnp.where(slot == 32, off_x.astype(F32), 0.0)
    table = jnp.where(slot == 33, off_y.astype(F32), table)
    for l in range(LIST):
        table = jnp.where(slot == 34 + l, interp_ref[:, l : l + 1].astype(F32), table)
        for b in range(TY):
            weights = jnp.exp(parts[b] - evidence)
            for a in range(TX):
                chosen = (name == orient_ref[:, l : l + 1]) & (shift_of == a)
                value = jnp.sum(jnp.where(chosen, weights, 0.0), axis=1, keepdims=True)
                table = jnp.where(slot == l * 16 + b * TX + a, value, table)
    table_ref[...] = table


def weights_table(
    planes, inner, half, images, near, far, offsets, orientations, interp_index, token
):
    number = images.shape[0]
    turn = np.arange(FY) * STEP
    turns = np.stack([np.cos(turn), np.sin(turn), np.cos(2 * turn), np.sin(2 * turn)])
    smem = pl.BlockSpec(memory_space=pltpu.SMEM)
    vmem = pl.BlockSpec(memory_space=pltpu.VMEM)
    return pl.pallas_call(
        functools.partial(score_kernel, planes, inner),
        out_shape=[jax.ShapeDtypeStruct((number, FX), F32)] * 2,
        in_specs=[smem, smem, pl.BlockSpec(memory_space=pltpu.HBM)] + [vmem] * 6,
        scratch_shapes=[pltpu.VMEM(images.shape, BF16), pltpu.SemaphoreType.DMA((4,))],
        compiler_params=vmem_params(14),
        cost_estimate=cost(5e9, 5e6),
        name="scores",
    )(
        half, jnp.asarray(turns, F32), in_hbm(images), near, far, offsets, orientations,
        interp_index, token,
    )


def wave_table():
    shift = np.arange(NSHIFT)[:, None] - SHIFTS
    angle = STEP * ((shift * np.arange(FX)[None, :]) % FY)
    table = np.concatenate(
        [
            np.concatenate([np.cos(angle), np.sin(angle)], axis=1),
            np.concatenate([-np.sin(angle), np.cos(angle)], axis=1),
        ],
        axis=0,
    ).astype(np.float32)
    high = table.astype(jnp.bfloat16)
    low = (table - high.astype(np.float32)).astype(jnp.bfloat16)
    return np.concatenate([high, high, low], axis=0)


def gather_kernel(cap, pad, first, row_ref, table_ref, wave_ref, mats_ref, *refs):
    base_ref = refs[0] if first is None else None
    out_ref, mixed_ref, line_ref = refs[1 if first is None else 0], refs[-2], refs[-1]
    lines = out_ref.shape[0]
    members = table_ref.shape[0]
    count = mats_ref.shape[0]
    span = cap + 16
    group = row_ref.shape[0] // span
    words = pad // (2 * FX)
    low_count = count // 2
    table_high, table_low = split(table_ref[:, :64])
    picks = jnp.concatenate([table_high, table_low], axis=1)
    number = members // group
    mats = jnp.concatenate(
        [mats_ref[:low_count].reshape(low_count * FX, FX), mats_ref[low_count:].reshape(low_count * FX, FX)],
        axis=1,
    )
    def block(s, carry):
        at = pl.multiple_of(s * span, 16)
        extra = row_ref[pl.ds(at + cap, 16), :].astype(F32)
        digit = [
            jnp.concatenate(
                [extra[which * words + word : which * words + word + 1] for word in range(words)],
                axis=1,
            )[:, :cap].astype(I32)
            for which in range(4)
        ]
        r = digit[0]
        member = s * number + (digit[1] >> 1)
        front = (digit[1] & 1) == 0
        line_ref[s] = digit[2] + (digit[3] - 1) * 256
        hot = (iota((members, cap), 0) == member).astype(F32).astype(BF16)
        got = lax.dot_general(picks, hot, (((0,), (0,)), ((), ())), preferred_element_type=F32)
        got = got[:64] + got[64:]
        weight = jnp.where(front, got[0:16], got[16:32])
        off_x = got[32:33].astype(I32)
        off_y = got[33:34].astype(I32)
        interp = jnp.where(front, got[34:35], got[35:36])
        sub = iota((8, cap), 0)
        units = r * ((sub & 3) - TY // 2 - off_y) - jnp.where(sub >= 4, FY // 4, 0)
        wave = jnp.cos(STEP * (units & (FY - 1)).astype(F32))
        gate_real = sum(weight[b * TX : (b + 1) * TX] * wave[b : b + 1] for b in range(TY))
        gate_imag = sum(weight[b * TX : (b + 1) * TX] * wave[4 + b : 5 + b] for b in range(TY))
        spot = iota((NSHIFT, cap), 0) + off_x
        coef_real = jnp.zeros((NSHIFT, cap), F32)
        coef_imag = jnp.zeros((NSHIFT, cap), F32)
        for a in range(TX):
            here = spot == a - TX // 2 + SHIFTS
            coef_real = jnp.where(here, gate_real[a : a + 1], coef_real)
            coef_imag = jnp.where(here, gate_imag[a : a + 1], coef_imag)
        high, low = split(jnp.concatenate([coef_real, coef_imag], axis=0))
        coef = jnp.concatenate([high, low, high], axis=0)
        phase = lax.dot_general(
            coef, wave_ref[...], (((0,), (0,)), ((), ())), preferred_element_type=F32
        )
        values = row_ref[pl.ds(at, cap), :].astype(F32)
        real, imag = rotate(values[:, :FX], values[:, FX:], phase[:, :FX], phase[:, FX:])
        slices = jnp.concatenate([real, imag], axis=0).astype(BF16)
        column = jnp.transpose(jnp.broadcast_to(interp, (8, cap)))[:, 0:1]
        column = jnp.broadcast_to(column, (cap, FX)).astype(I32)
        column = jnp.concatenate([column, column], axis=0)
        which = jnp.where(column >= low_count, column - low_count, column)
        zero = jnp.zeros_like(slices)
        pieces = [jnp.where(which == q, slices, zero) for q in range(low_count)]
        mixed = jnp.dot(jnp.concatenate(pieces, axis=1), mats, preferred_element_type=F32)
        mixed = jnp.where(column >= low_count, mixed[:, FX:], mixed[:, :FX]).astype(BF16)
        to = pl.ds(pl.multiple_of(s * cap, 16), cap)
        mixed_ref[to, :FX] = mixed[:cap]
        mixed_ref[to, FX:] = mixed[cap:]
        return carry

    lax.fori_loop(0, group, block, 0, unroll=2)
    line = jnp.concatenate([line_ref[s] for s in range(group)], axis=1)
    tile = min(512, lines // 2)
    rows = iota((tile, group * cap), 0)
    for at in range(0, lines, tile):
        hot = jnp.where(rows == line - at, 1.0, 0.0).astype(BF16)
        value = jnp.dot(hot, mixed_ref[...], preferred_element_type=F32)
        if base_ref is not None:
            value = value + base_ref[at : at + tile, :]
        out_ref[at : at + tile, :] = value
        if first:
            refs[1][at : at + tile, :] = value.astype(BF16)


def partial_lines(cap, pad, rows, table, mats, lines, first, base=None):
    group = rows.shape[0] // (cap + 16)
    shape = jax.ShapeDtypeStruct((lines, 2 * FX), F32)
    short = jax.ShapeDtypeStruct((lines, 2 * FX), BF16)
    vmem = pl.BlockSpec(memory_space=pltpu.VMEM)
    extra = () if base is None else (base,)
    return pl.pallas_call(
        functools.partial(gather_kernel, cap, pad, None if extra else first),
        out_shape=(shape, short) if first else shape,
        in_specs=[vmem] * (4 + len(extra)),
        scratch_shapes=[
            pltpu.VMEM((group * cap, 2 * FX), BF16),
            pltpu.VMEM((group, 1, cap), I32),
        ],
        compiler_params=vmem_params(20),
        cost_estimate=cost(1e6, 1e5),
        name="lines",
    )(rows, table, jnp.asarray(wave_table()), mats, *extra)


def relay_kernel(planes, step, place_of, pieces, *refs):
    refs = list(refs)
    up_out, down_out = refs[-2:]
    downs, ups = refs[-2 - pieces : -2], refs[-2 - 2 * pieces : -2 - pieces]
    parts = refs[: -2 - 2 * pieces]
    z = lax.axis_index("z")
    lines = up_out.shape[0]
    length = lines // pieces
    tile = min(512, length)

    def send(part, came, out):
        for at in range(0, lines, tile):
            value = part[at : at + tile, :]
            if came is not None:
                spot = at % length
                value = value + came[at // length][spot : spot + tile, :].astype(F32)
            out[at : at + tile, :] = value.astype(BF16)

    for p in range(planes):
        goes_up, goes_down = p < step, p >= planes - step
        if goes_up or goes_down:

            @pl.when(z == p)
            def _(p=p, goes_up=goes_up, goes_down=goes_down):
                if goes_up:
                    part = parts[place_of[p, planes - step + p]]
                    send(part, ups if p > 0 else None, up_out)
                if goes_down:
                    part = parts[place_of[p, p - planes + step]]
                    send(part, downs if p < planes - 1 else None, down_out)


def relay(planes, step, place_of, parts, up, down):
    vmem = pl.BlockSpec(memory_space=pltpu.VMEM)
    return pl.pallas_call(
        functools.partial(relay_kernel, planes, step, place_of, len(up)),
        out_shape=[jax.ShapeDtypeStruct(parts[0].shape, BF16)] * 2,
        in_specs=[vmem] * (len(parts) + 2 * len(up)),
        compiler_params=vmem_params(14),
        cost_estimate=cost(60e9, 8e6),
        name="relay",
    )(*parts, *up, *down)


def together(*values):
    return lax.optimization_barrier(values)


def block_order(planes):
    return np.array(
        [sorted(range(planes), key=lambda d: (-abs(d - z), -d)) for z in range(planes)], np.int32
    )


def body(
    planes, inner, slab,
    images, references, offsets, orientations, interp_mats, interp_index, owners, line_index, volume_in,
):
    number = images.shape[0]
    lines = volume_in.shape[0]
    group = inner * slab
    devices = planes * group
    rows_all = number * LIST * FY
    cap = max(2, 7 * rows_all // (4 * devices))
    span = cap + 16
    pad = -(-(cap + 1) // (2 * FX)) * 2 * FX
    half = lax.axis_index("slab") % 2

    local = references.shape[0]
    width = references.shape[1]
    mine = lax.dynamic_slice_in_dim(references, half * (width // 2), width // 2, axis=1)
    block = [mine]
    for e in range(1, inner):
        block.append(lax.ppermute(mine, "x", [(i, i ^ e) for i in range(inner)]))

    place_of = np.argsort(block_order(planes), axis=1).astype(np.int32)
    index, digits, real, imag = row_slots(
        place_of,
        owners.reshape(number, LIST * FY),
        line_index,
        images,
        devices,
        group,
        pad,
    )
    block, index = together(block, index)
    block = jnp.concatenate(block, axis=0)
    near = [block]
    for shift in range(1, planes):
        near.append(lax.ppermute(block, "z", [(p, (p + shift) % planes) for p in range(planes)]))
    def place(k, index):
        return placed_rows(k, group, cap, index, digits, real, imag)

    first, token = place(0, index)
    placed = [first]

    def to_members(value):
        return lax.all_to_all(
            value.reshape(group, span, 2 * FX), ("x", "slab"), 0, 0, tiled=True
        ).reshape(group * span, 2 * FX)

    got = to_members(placed[0])
    near, token = together(near, token)
    near = jnp.concatenate(near, axis=0)
    far = lax.ppermute(near, "slab", [(i, i ^ 1) for i in range(slab)])
    table, evidence = weights_table(
        planes, inner, half.reshape(1).astype(I32), images, near, far, offsets, orientations,
        interp_index, token,
    )
    table, got, index = together(table, got, index)
    placed.append(place(1, index)[0])
    tables = lax.all_to_all(
        jnp.broadcast_to(table[None], (group,) + table.shape), ("x", "slab"), 0, 0, tiled=True
    ).reshape(group * number, FX)
    tables, placed[1] = together(tables, placed[1])
    got = [got, to_members(placed[1])]

    def lines_of(k, base=None):
        return partial_lines(cap, pad, got[k], tables, interp_mats, lines, k == 0, base)

    def fetch(k, value):
        if k < planes:
            value, held = together(value, index)
            placed.append(place(k, held)[0])
            got.append(to_members(placed[k]))
        return value

    part, short = lines_of(0)
    parts = [fetch(2, part)]
    up = down = [lax.ppermute(short, "z", sorted({(0, 1), (planes - 1, planes - 2)}))]
    for s in range(2, planes):
        parts.append(fetch(s + 1, lines_of(s - 1)))
        up_send, down_send = relay(planes, s, place_of, parts, up, down)
        up = [lax.ppermute(up_send, "z", [(p, p + 1) for p in range(s)])]
        down = [lax.ppermute(down_send, "z", [(p, p - 1) for p in range(planes - s, planes)])]
    last = lines_of(planes - 1, volume_in)
    volume = last + jnp.concatenate(up, axis=0).astype(F32) + jnp.concatenate(down, axis=0).astype(F32)
    return volume, evidence[:, 0]


def solution(mesh):
    dom, slab = mesh.shape["dom"], mesh.shape["slab"]
    planes = dom // INNER
    fine = Mesh(mesh.devices.reshape(planes, INNER, slab), ("z", "x", "slab"))
    every = ("z", "x", "slab")
    in_specs = (
        P(every, None),
        P(("z", "x"), None),
        P(every, None),
        P(every, None),
        P(),
        P(every, None),
        P(every, None, None),
        P(every, None),
        P(every, None),
    )
    out_specs = (P(every, None), P(every))
    return jax.shard_map(
        functools.partial(body, planes, INNER, slab),
        mesh=fine,
        in_specs=in_specs,
        out_specs=out_specs,
        check_vma=False,
    )
```

```python
import functools
import math

import jax
import jax.numpy as jnp
import numpy as np
from jax import lax
from jax.experimental import pallas as pl
from jax.experimental.pallas import tpu as pltpu
from jax.sharding import Mesh
from jax.sharding import PartitionSpec as P

FY = 256
FX = 128
TX = 4
TY = 4
LIST = 2
OFF = 8
INNER = 2
F32 = jnp.float32
BF16 = jnp.bfloat16
I32 = jnp.int32
STEP = 2.0 * math.pi / FY
SHIFTS = OFF + max(TX, TY) // 2
NSHIFT = 24


def vmem_params(mib):
    return pltpu.CompilerParams(vmem_limit_bytes=mib << 20)


def whole(shape):
    return pl.BlockSpec(shape, lambda *_: (0,) * len(shape))


def cost(flops, nbytes):
    return pl.CostEstimate(flops=int(flops), bytes_accessed=int(nbytes), transcendentals=0)


def iota(shape, axis):
    return lax.broadcasted_iota(I32, shape, axis)


def in_hbm(value):
    return pltpu.with_memory_space_constraint(value, pltpu.HBM)


def split(value):
    high = value.astype(BF16)
    return high, (value - high.astype(F32)).astype(BF16)


def slot_kernel(
    dests, group, pad, place_of, owner_ref, line_from, image_from,
    index_ref, digit_ref, real_ref, imag_ref, hot_ref, line_ref, image_ref, sems,
):
    number = owner_ref.shape[0]
    blocks = number * LIST
    planes = dests // group
    z = lax.axis_index("z")
    lines_in = pltpu.make_async_copy(line_from, line_ref, sems.at[0])
    lines_in.start()
    images_in = pltpu.make_async_copy(image_from, image_ref, sems.at[1])
    images_in.start()

    def widen(k, carry):
        for i in range(8):
            r = k * 8 + i
            at = pl.multiple_of(r * 2 * FX, 2 * FX)
            to = pl.ds(pl.multiple_of(r * number, number), number)
            real_ref[to, :] = image_ref[:, pl.ds(at, FX)].astype(F32)
            imag_ref[to, :] = image_ref[:, pl.ds(at + FX, FX)].astype(F32)
        return carry

    owner = owner_ref[...]
    plane = owner // group
    chunk = jnp.zeros_like(owner)
    for k in range(planes):
        at = functools.reduce(
            lambda value, p: jnp.where(z == p, int(place_of[p, k]), value), range(planes), 0
        )
        chunk = jnp.where(plane == k, at, chunk)
    dest = chunk * group + (owner & (group - 1))
    owner_rows = iota((dests, FY), 0)
    for b in range(blocks):
        n, l = b // LIST, b % LIST
        hot = owner_rows == dest[n : n + 1, l * FY : (l + 1) * FY]
        hot_ref[b * dests : (b + 1) * dests, :] = hot.astype(F32).astype(BF16)
    before = (iota((FY, FY), 0) < iota((FY, FY), 1)).astype(F32).astype(BF16)
    prefix = jnp.dot(hot_ref[...], before, preferred_element_type=F32)
    lines_in.wait()
    running = jnp.zeros((dests, 1), F32)
    lane = iota((1, FY), 1).astype(F32)
    ranks = iota((pad, FY), 0)
    total = jnp.zeros((4 * dests, pad), F32)
    for b in range(blocks):
        n, l = b // LIST, b % LIST
        hot = hot_ref[b * dests : (b + 1) * dests, :].astype(F32)
        part = prefix[b * dests : (b + 1) * dests, :]
        rank = jnp.sum(hot * (part + running), axis=0, keepdims=True).astype(I32)
        running = running + part[:, FY - 1 :] + hot[:, FY - 1 :]
        line = line_ref[n : n + 1, l * FY : (l + 1) * FY]
        digits = [
            hot * lane,
            hot * float(b),
            hot * (line & 255).astype(F32),
            hot * ((line >> 8) + 1).astype(F32),
        ]
        left = jnp.concatenate(digits, axis=0).astype(BF16)
        right = (ranks == rank).astype(F32).astype(BF16)
        total = total + lax.dot_general(
            left, right, (((1,), (1,)), ((), ())), preferred_element_type=F32
        )
    digit_ref[...] = total
    row = total[:dests].astype(I32) * number + (total[dests : 2 * dests].astype(I32) >> 1)
    index_ref[...] = jnp.where(iota((dests, pad), 1) == pad - 1, running.astype(I32), row)
    images_in.wait()
    lax.fori_loop(0, FY // 8, widen, 0)


def row_slots(place_of, owners, lines, images, dests, group, pad):
    number, width = images.shape
    return pl.pallas_call(
        functools.partial(slot_kernel, dests, group, pad, place_of),
        out_shape=(
            jax.ShapeDtypeStruct((dests, pad), I32),
            jax.ShapeDtypeStruct((4 * dests, pad), F32),
            pltpu.VMEM((number * FY, FX), F32),
            pltpu.VMEM((number * FY, FX), F32),
        ),
        in_specs=[pl.BlockSpec(memory_space=pltpu.VMEM)]
        + [pl.BlockSpec(memory_space=pltpu.HBM)] * 2,
        scratch_shapes=[
            pltpu.VMEM((number * LIST * dests, FY), BF16),
            pltpu.VMEM(lines.shape, I32),
            pltpu.VMEM(images.shape, BF16),
            pltpu.SemaphoreType.DMA((2,)),
        ],
        compiler_params=vmem_params(20),
        cost_estimate=cost(3e9, 12e6),
        name="slots",
    )(owners, in_hbm(lines), in_hbm(images))


def place_kernel(
    chunk, cap, index_ref, digit_ref, real_ref, imag_ref, out_ref, token_ref, left_ref, right_ref,
    held, sems,
):
    group, pad = index_ref.shape
    dests = digit_ref.shape[0] // 4
    words = pad // (2 * FX)
    span = cap + 16
    zeros = jnp.zeros((group * span, FX), F32)

    left_ref[...] = zeros
    right_ref[...] = zeros
    token_ref[...] = jnp.zeros_like(token_ref)
    def member(d, carry):
        start = d * span

        def some(i, inner):
            spots = [index_ref[d, i * 32 + j] for j in range(32)]
            lefts = [real_ref[pl.ds(at, 1), :] for at in spots]
            rights = [imag_ref[pl.ds(at, 1), :] for at in spots]
            for j in range(32):
                left_ref[pl.ds(start + i * 32 + j, 1), :] = lefts[j]
                right_ref[pl.ds(start + i * 32 + j, 1), :] = rights[j]
            return inner

        lax.fori_loop(0, (index_ref[d, pad - 1] + 31) // 32, some, 0)
        return carry

    lax.fori_loop(0, group, member, 0)
    copies = []
    for d in range(group):
        start = d * span
        for which in range(4):
            row = which * dests + chunk * group + d
            for word in range(words):
                to = start + cap + which * words + word
                lane = word * 2 * FX
                left_ref[to : to + 1, :] = digit_ref[row : row + 1, lane : lane + FX]
                right_ref[to : to + 1, :] = digit_ref[row : row + 1, lane + FX : lane + 2 * FX]
        at = slice(start, start + span)
        held[at, :FX] = left_ref[at, :].astype(BF16)
        held[at, FX:] = right_ref[at, :].astype(BF16)
        copies.append(pltpu.make_async_copy(held.at[at], out_ref.at[at], sems.at[d]))
        copies[-1].start()
    for copy in copies:
        copy.wait()


def placed_rows(chunk, group, cap, index, digits, real, imag):
    pad = index.shape[1]
    span = cap + 16
    vmem = pl.BlockSpec(memory_space=pltpu.VMEM)
    return pl.pallas_call(
        functools.partial(place_kernel, chunk, cap),
        grid=(1,),
        out_shape=(pltpu.HBM((group * span, 2 * FX), BF16), jax.ShapeDtypeStruct((8, FX), F32)),
        in_specs=[
            pl.BlockSpec((group, pad), lambda i: (chunk, 0), memory_space=pltpu.SMEM),
            vmem,
            vmem,
            vmem,
        ],
        out_specs=(pl.BlockSpec(memory_space=pltpu.HBM), vmem),
        scratch_shapes=[pltpu.VMEM((group * span, FX), F32)] * 2
        + [pltpu.VMEM((group * span, 2 * FX), BF16), pltpu.SemaphoreType.DMA((group,))],
        compiler_params=vmem_params(12),
        cost_estimate=cost(1e5, 1e5),
        name="place",
    )(index, digits, real, imag)


def rotate(real, imag, cosine, sine):
    return real * cosine - imag * sine, real * sine + imag * cosine


def score_kernel(
    planes, inner, half_ref, turn_ref, image_from, near_ref, far_ref, offset_ref, orient_ref,
    interp_ref, token_ref, table_ref, evidence_ref, image_ref, sems,
):
    number = image_ref.shape[0]
    refs = near_ref.shape[0]
    rows_half = FY // 2
    group = 32
    half = half_ref[0]
    copies = []
    for k in range(4):
        side = half if k < 2 else 1 - half
        quarter = FY * FX // 2
        at = pl.ds(pl.multiple_of((side * 2 + k % 2) * quarter, quarter), quarter)
        copies.append(
            pltpu.make_async_copy(image_from.at[:, at], image_ref.at[:, at], sems.at[k])
        )
        copies[-1].start()
    off_x = offset_ref[:, 0:1]
    off_y = offset_ref[:, 1:2]
    lane = iota((number, FX), 1)

    def wave(units):
        angle = STEP * (units & (FY - 1)).astype(F32)
        return jnp.cos(angle), jnp.sin(angle)

    col_cos, col_sin = wave(-lane * off_x)
    one_cos, one_sin = wave(jnp.broadcast_to(-off_y, (number, FX)))
    ref_lane = iota((1, FX), 1)
    x1_cos, x1_sin = wave(jnp.broadcast_to(ref_lane, (refs, FX)))
    x2_cos, x2_sin = wave(jnp.broadcast_to(2 * ref_lane, (refs, FX)))

    def shifts(real, imag, c1, s1, c2, s2):
        rc, rs, ic, is_ = real * c1, real * s1, imag * c1, imag * s1
        pairs = [
            (real * c2 + imag * s2, imag * c2 - real * s2),
            (rc + is_, ic - rs),
            (real, imag),
            (rc - is_, ic + rs),
        ]
        return pairs

    def stacked(pairs):
        return jnp.concatenate(
            [jnp.concatenate([p.astype(BF16), q.astype(BF16)], axis=1) for p, q in pairs],
            axis=0,
        )

    def run(ref, first, total, waits):
        start_cos, start_sin = wave(-(lane * off_x + first * off_y))

        def block(k, carry):
            total, cosine, sine = carry
            lefts, rights = [], []
            for i in range(group):
                r = first + k * group + i
                at = pl.multiple_of(r * 2 * FX, 2 * FX)
                at_ref = pl.multiple_of((k * group + i) * 2 * FX, 2 * FX)
                real = image_ref[:, pl.ds(at, FX)].astype(F32)
                imag = image_ref[:, pl.ds(at + FX, FX)].astype(F32)
                real, imag = rotate(real, imag, cosine, sine)
                cosine, sine = rotate(cosine, sine, one_cos, one_sin)
                lefts.append(
                    stacked(
                        shifts(
                            real, imag, turn_ref[0, r], turn_ref[1, r], turn_ref[2, r], turn_ref[3, r]
                        )
                    )
                )
                real = ref[:, pl.ds(at_ref, FX)].astype(F32)
                imag = ref[:, pl.ds(at_ref + FX, FX)].astype(F32)
                rights.append(stacked(shifts(real, imag, x1_cos, -x1_sin, x2_cos, -x2_sin)))
            total = total + lax.dot_general(
                jnp.concatenate(lefts, axis=1),
                jnp.concatenate(rights, axis=1),
                (((1,), (1,)), ((), ())),
                preferred_element_type=F32,
            )
            return total, cosine, sine

        carry = (total, start_cos, start_sin)
        turns = rows_half // group // len(waits)
        for k, wait in enumerate(waits):
            wait.wait()
            carry = lax.fori_loop(k * turns, (k + 1) * turns, block, carry)
        return carry[0]

    total = jnp.zeros((TY * number, TX * refs), F32)
    total = run(near_ref, half * rows_half, total, copies[:2])
    total = run(far_ref, (1 - half) * rows_half, total, copies[2:])
    total = total * (1.0 / math.sqrt(FY * 2 * FX))
    parts = [total[b * number : (b + 1) * number, :] for b in range(TY)]
    top = functools.reduce(jnp.maximum, parts)
    top = jnp.max(top, axis=1, keepdims=True)
    mass = sum(jnp.sum(jnp.exp(part - top), axis=1, keepdims=True) for part in parts)
    evidence = top + jnp.log(mass)
    evidence_ref[...] = jnp.broadcast_to(evidence, (number, FX))
    spot = iota((number, TX * refs), 1)
    shift_of = spot // refs
    spot = spot & (refs - 1)
    local = refs // (planes * inner)
    plane = lax.axis_index("z") - spot // (inner * local)
    plane = jnp.where(plane < 0, plane + planes, plane)
    column = lax.axis_index("x") ^ ((spot // local) & (inner - 1))
    name = (plane * inner + column) * local + (spot & (local - 1))
    slot = iota((number, FX), 1)
    table = jnp.where(slot == 32, off_x.astype(F32), 0.0)
    table = jnp.where(slot == 33, off_y.astype(F32), table)
    for l in range(LIST):
        table = jnp.where(slot == 34 + l, interp_ref[:, l : l + 1].astype(F32), table)
        for b in range(TY):
            weights = jnp.exp(parts[b] - evidence)
            for a in range(TX):
                chosen = (name == orient_ref[:, l : l + 1]) & (shift_of == a)
                value = jnp.sum(jnp.where(chosen, weights, 0.0), axis=1, keepdims=True)
                table = jnp.where(slot == l * 16 + b * TX + a, value, table)
    table_ref[...] = table


def weights_table(
    planes, inner, half, images, near, far, offsets, orientations, interp_index, token
):
    number = images.shape[0]
    turn = np.arange(FY) * STEP
    turns = np.stack([np.cos(turn), np.sin(turn), np.cos(2 * turn), np.sin(2 * turn)])
    smem = pl.BlockSpec(memory_space=pltpu.SMEM)
    vmem = pl.BlockSpec(memory_space=pltpu.VMEM)
    return pl.pallas_call(
        functools.partial(score_kernel, planes, inner),
        out_shape=[jax.ShapeDtypeStruct((number, FX), F32)] * 2,
        in_specs=[smem, smem, pl.BlockSpec(memory_space=pltpu.HBM)] + [vmem] * 6,
        scratch_shapes=[pltpu.VMEM(images.shape, BF16), pltpu.SemaphoreType.DMA((4,))],
        compiler_params=vmem_params(14),
        cost_estimate=cost(1e9, 5e6),
        name="scores",
    )(
        half, jnp.asarray(turns, F32), in_hbm(images), near, far, offsets, orientations,
        interp_index, token,
    )


def wave_table():
    shift = np.arange(NSHIFT)[:, None] - SHIFTS
    angle = STEP * ((shift * np.arange(FX)[None, :]) % FY)
    table = np.concatenate(
        [
            np.concatenate([np.cos(angle), np.sin(angle)], axis=1),
            np.concatenate([-np.sin(angle), np.cos(angle)], axis=1),
        ],
        axis=0,
    ).astype(np.float32)
    high = table.astype(jnp.bfloat16)
    low = (table - high.astype(np.float32)).astype(jnp.bfloat16)
    return np.concatenate([high, high, low], axis=0)


def gather_kernel(cap, pad, first, row_from, table_ref, wave_ref, mats_ref, *refs):
    base_ref = refs[0] if first is None else None
    out_ref = refs[1 if first is None else 0]
    mixed_ref, line_ref, row_ref, sems = refs[-4:]
    lines = out_ref.shape[0]
    members = table_ref.shape[0]
    count = mats_ref.shape[0]
    span = cap + 16
    group = row_ref.shape[0] // span
    words = pad // (2 * FX)

    def fetch(s):
        at = pl.ds(pl.multiple_of(s * span, 16), span)
        return pltpu.make_async_copy(row_from.at[at], row_ref.at[at], sems.at[s])

    for s in range(group):
        fetch(s).start()
    low_count = count // 2
    table_high, table_low = split(table_ref[:, :64])
    picks = jnp.concatenate([table_high, table_low], axis=1)
    number = members // group
    mats = jnp.concatenate(
        [mats_ref[:low_count].reshape(low_count * FX, FX), mats_ref[low_count:].reshape(low_count * FX, FX)],
        axis=1,
    )
    def block(s, carry):
        fetch(s).wait()
        at = pl.multiple_of(s * span, 16)
        extra = row_ref[pl.ds(at + cap, 16), :].astype(F32)
        digit = [
            jnp.concatenate(
                [extra[which * words + word : which * words + word + 1] for word in range(words)],
                axis=1,
            )[:, :cap].astype(I32)
            for which in range(4)
        ]
        r = digit[0]
        member = s * number + (digit[1] >> 1)
        front = (digit[1] & 1) == 0
        line_ref[s] = digit[2] + (digit[3] - 1) * 256
        hot = (iota((members, cap), 0) == member).astype(F32).astype(BF16)
        got = lax.dot_general(picks, hot, (((0,), (0,)), ((), ())), preferred_element_type=F32)
        got = got[:64] + got[64:]
        weight = jnp.where(front, got[0:16], got[16:32])
        off_x = got[32:33].astype(I32)
        off_y = got[33:34].astype(I32)
        interp = jnp.where(front, got[34:35], got[35:36])
        sub = iota((8, cap), 0)
        units = r * ((sub & 3) - TY // 2 - off_y) - jnp.where(sub >= 4, FY // 4, 0)
        wave = jnp.cos(STEP * (units & (FY - 1)).astype(F32))
        gate_real = sum(weight[b * TX : (b + 1) * TX] * wave[b : b + 1] for b in range(TY))
        gate_imag = sum(weight[b * TX : (b + 1) * TX] * wave[4 + b : 5 + b] for b in range(TY))
        spot = iota((NSHIFT, cap), 0) + off_x
        coef_real = jnp.zeros((NSHIFT, cap), F32)
        coef_imag = jnp.zeros((NSHIFT, cap), F32)
        for a in range(TX):
            here = spot == a - TX // 2 + SHIFTS
            coef_real = jnp.where(here, gate_real[a : a + 1], coef_real)
            coef_imag = jnp.where(here, gate_imag[a : a + 1], coef_imag)
        high, low = split(jnp.concatenate([coef_real, coef_imag], axis=0))
        coef = jnp.concatenate([high, low, high], axis=0)
        phase = lax.dot_general(
            coef, wave_ref[...], (((0,), (0,)), ((), ())), preferred_element_type=F32
        )
        values = row_ref[pl.ds(at, cap), :].astype(F32)
        real, imag = rotate(values[:, :FX], values[:, FX:], phase[:, :FX], phase[:, FX:])
        slices = jnp.concatenate([real, imag], axis=0).astype(BF16)
        column = jnp.transpose(jnp.broadcast_to(interp, (8, cap)))[:, 0:1]
        column = jnp.broadcast_to(column, (cap, FX)).astype(I32)
        column = jnp.concatenate([column, column], axis=0)
        which = jnp.where(column >= low_count, column - low_count, column)
        zero = jnp.zeros_like(slices)
        pieces = [jnp.where(which == q, slices, zero) for q in range(low_count)]
        mixed = jnp.dot(jnp.concatenate(pieces, axis=1), mats, preferred_element_type=F32)
        mixed = jnp.where(column >= low_count, mixed[:, FX:], mixed[:, :FX]).astype(BF16)
        to = pl.ds(pl.multiple_of(s * cap, 16), cap)
        mixed_ref[to, :FX] = mixed[:cap]
        mixed_ref[to, FX:] = mixed[cap:]
        return carry

    lax.fori_loop(0, group, block, 0, unroll=group if first else 2)
    line = jnp.concatenate([line_ref[s] for s in range(group)], axis=1)
    tile = min(512, lines // 2)
    rows = iota((tile, group * cap), 0)
    for at in range(0, lines, tile):
        hot = jnp.where(rows == line - at, 1.0, 0.0).astype(BF16)
        value = jnp.dot(hot, mixed_ref[...], preferred_element_type=F32)
        if base_ref is not None:
            value = value + base_ref[at : at + tile, :]
        out_ref[at : at + tile, :] = value
        if first:
            refs[1][at : at + tile, :] = value.astype(BF16)


def partial_lines(cap, pad, rows, table, mats, lines, first, base=None):
    group = rows.shape[0] // (cap + 16)
    shape = jax.ShapeDtypeStruct((lines, 2 * FX), F32)
    short = jax.ShapeDtypeStruct((lines, 2 * FX), BF16)
    vmem = pl.BlockSpec(memory_space=pltpu.VMEM)
    extra = () if base is None else (base,)
    return pl.pallas_call(
        functools.partial(gather_kernel, cap, pad, None if extra else first),
        out_shape=(shape, short) if first else shape,
        in_specs=[pl.BlockSpec(memory_space=pltpu.HBM)] + [vmem] * (3 + len(extra)),
        scratch_shapes=[
            pltpu.VMEM((group * cap, 2 * FX), BF16),
            pltpu.VMEM((group, 1, cap), I32),
            pltpu.VMEM(rows.shape, BF16),
            pltpu.SemaphoreType.DMA((group,)),
        ],
        compiler_params=vmem_params(20),
        cost_estimate=cost(1e6, 1e5),
        name="lines",
    )(in_hbm(rows), table, jnp.asarray(wave_table()), mats, *extra)


def relay_kernel(planes, step, place_of, *refs):
    up_from, down_from, _, _, up_to, down_to, came_ref, sent_ref, sems = refs[-9:]
    parts = refs[:-9]
    z = lax.axis_index("z")
    lines = up_to.shape[0]
    tile = min(512, lines)
    tiles = lines // tile

    def pull(came, way, k):
        at = pl.ds(k * tile, tile)
        return pltpu.make_async_copy(came.at[at], came_ref.at[way, at], sems.at[0, way, k])

    def push(out, way, k):
        at = pl.ds(k * tile, tile)
        return pltpu.make_async_copy(sent_ref.at[way, at], out.at[at], sems.at[1, way, k])

    for p in range(planes):
        jobs = []
        if p < step:
            jobs.append((0, place_of[p, planes - step + p], up_from if p > 0 else None, up_to))
        if p >= planes - step:
            edge = p == planes - 1
            jobs.append((1, place_of[p, p - planes + step], None if edge else down_from, down_to))
        if jobs:

            @pl.when(z == p)
            def _(jobs=jobs):
                for way, _, came, _ in jobs:
                    for k in range(tiles if came is not None else 0):
                        pull(came, way, k).start()
                for way, index, came, out in jobs:
                    for k in range(tiles):
                        at = slice(k * tile, (k + 1) * tile)
                        value = parts[index][at, :]
                        if came is not None:
                            pull(came, way, k).wait()
                            value = value + came_ref[way, at, :].astype(F32)
                        sent_ref[way, at, :] = value.astype(BF16)
                        push(out, way, k).start()
                for way, _, _, out in jobs:
                    for k in range(tiles):
                        push(out, way, k).wait()


def relay(planes, step, place_of, parts, up, down, tokens):
    vmem = pl.BlockSpec(memory_space=pltpu.VMEM)
    hbm = pl.BlockSpec(memory_space=pltpu.HBM)
    lines = up.shape[0]
    return pl.pallas_call(
        functools.partial(relay_kernel, planes, step, place_of),
        out_shape=[pltpu.HBM(up.shape, BF16)] * 2,
        in_specs=[vmem] * len(parts) + [hbm, hbm, vmem, vmem],
        out_specs=[hbm, hbm],
        scratch_shapes=[
            pltpu.VMEM((2, lines, 2 * FX), BF16),
            pltpu.VMEM((2, lines, 2 * FX), BF16),
            pltpu.SemaphoreType.DMA((2, 2, lines // min(512, lines))),
        ],
        compiler_params=vmem_params(10),
        cost_estimate=cost(60e9, 8e6),
        name="relay",
    )(*parts, in_hbm(up), in_hbm(down), *tokens)


def together(*values):
    return lax.optimization_barrier(values)


def block_order(planes):
    return np.array(
        [sorted(range(planes), key=lambda d: (-abs(d - z), -d)) for z in range(planes)], np.int32
    )


def body(
    planes, inner, slab,
    images, references, offsets, orientations, interp_mats, interp_index, owners, line_index, volume_in,
):
    number = images.shape[0]
    lines = volume_in.shape[0]
    group = inner * slab
    devices = planes * group
    rows_all = number * LIST * FY
    cap = max(2, 7 * rows_all // (4 * devices))
    span = cap + 16
    pad = -(-(cap + 1) // (2 * FX)) * 2 * FX
    half = lax.axis_index("slab") % 2

    local = references.shape[0]
    width = references.shape[1]
    mine = lax.dynamic_slice_in_dim(references, half * (width // 2), width // 2, axis=1)
    block = [mine]
    for e in range(1, inner):
        block.append(lax.ppermute(mine, "x", [(i, i ^ e) for i in range(inner)]))

    place_of = np.argsort(block_order(planes), axis=1).astype(np.int32)
    index, digits, real, imag = row_slots(
        place_of,
        owners.reshape(number, LIST * FY),
        line_index,
        images,
        devices,
        group,
        pad,
    )
    block, index = together(block, index)
    block = jnp.concatenate(block, axis=0)
    near = [block]
    for shift in range(1, planes):
        near.append(lax.ppermute(block, "z", [(p, (p + shift) % planes) for p in range(planes)]))
    def place(k, index):
        return placed_rows(k, group, cap, index, digits, real, imag)

    placed = [None] * planes
    placed[0], token = place(0, index)
    token, index = together(token, index)
    placed[1], token = place(1, index)

    def to_members(value):
        return lax.all_to_all(
            value.reshape(group, span, 2 * FX), ("x", "slab"), 0, 0, tiled=True
        ).reshape(group * span, 2 * FX)

    got = to_members(placed[0])
    near, token = together(near, token)
    near = jnp.concatenate(near, axis=0)
    far = lax.ppermute(near, "slab", [(i, i ^ 1) for i in range(slab)])
    table, evidence = weights_table(
        planes, inner, half.reshape(1).astype(I32), images, near, far, offsets, orientations,
        interp_index, token,
    )
    table, got, index = together(table, got, index)
    early = min(2, planes - 1)
    placed[early], token = place(early, index)
    later = token
    tables = lax.all_to_all(
        jnp.broadcast_to(table[None], (group,) + table.shape), ("x", "slab"), 0, 0, tiled=True
    ).reshape(group * number, FX)
    tables, placed[1], later = together(tables, placed[1], later)
    got = [got, to_members(placed[1])]

    def lines_of(k, base=None):
        return partial_lines(cap, pad, got[k], tables, interp_mats, lines, k == 0, base)

    part, short = lines_of(0)
    part, index = together(part, index)
    parts = [part]
    for k in range(early + 1, min(early + 2, planes)):
        placed[k], token = place(k, index)
    placed[early], token = together(placed[early], token)
    got.append(to_members(placed[early]))
    up = down = lax.ppermute(short, "z", sorted({(0, 1), (planes - 1, planes - 2)}))
    for s in range(2, planes):
        part = lines_of(s - 1)
        if s + 1 < planes:
            part, index = together(part, index)
            if placed[s + 1] is None:
                placed[s + 1], _ = place(s + 1, index)
            part, placed[s + 1] = together(part, placed[s + 1])
            got.append(to_members(placed[s + 1]))
        parts.append(part)
        up_send, down_send = relay(planes, s, place_of, parts, up, down, (token, later))
        up = lax.ppermute(up_send, "z", [(p, p + 1) for p in range(s)])
        down = lax.ppermute(down_send, "z", [(p, p - 1) for p in range(planes - s, planes)])
    last = lines_of(planes - 1, volume_in)
    volume = last + up.astype(F32) + down.astype(F32)
    return volume, evidence[:, 0]


def solution(mesh):
    dom, slab = mesh.shape["dom"], mesh.shape["slab"]
    planes = dom // INNER
    fine = Mesh(mesh.devices.reshape(planes, INNER, slab), ("z", "x", "slab"))
    every = ("z", "x", "slab")
    in_specs = (
        P(every, None),
        P(("z", "x"), None),
        P(every, None),
        P(every, None),
        P(),
        P(every, None),
        P(every, None, None),
        P(every, None),
        P(every, None),
    )
    out_specs = (P(every, None), P(every))
    return jax.shard_map(
        functools.partial(body, planes, INNER, slab),
        mesh=fine,
        in_specs=in_specs,
        out_specs=out_specs,
        check_vma=False,
    )
```

```python
import functools
import math

import jax
import jax.numpy as jnp
import numpy as np
from jax import lax
from jax.experimental import pallas as pl
from jax.experimental.pallas import tpu as pltpu
from jax.sharding import Mesh
from jax.sharding import PartitionSpec as P

FY = 256
FX = 128
TX = 4
TY = 4
LIST = 2
OFF = 8
INNER = 2
F32 = jnp.float32
BF16 = jnp.bfloat16
I32 = jnp.int32
STEP = 2.0 * math.pi / FY
SHIFTS = OFF + max(TX, TY) // 2
NSHIFT = 24


def vmem_params(mib):
    return pltpu.CompilerParams(vmem_limit_bytes=mib << 20)


def whole(shape):
    return pl.BlockSpec(shape, lambda *_: (0,) * len(shape))


def cost(flops, nbytes):
    return pl.CostEstimate(flops=int(flops), bytes_accessed=int(nbytes), transcendentals=0)


def iota(shape, axis):
    return lax.broadcasted_iota(I32, shape, axis)


def in_hbm(value):
    return pltpu.with_memory_space_constraint(value, pltpu.HBM)


def split(value):
    high = value.astype(BF16)
    return high, (value - high.astype(F32)).astype(BF16)


def slot_kernel(
    dests, group, pad, place_of, owner_ref, line_from, image_from,
    index_ref, digit_ref, real_ref, imag_ref, hot_ref, line_ref, image_ref, sems,
):
    number = owner_ref.shape[0]
    blocks = number * LIST
    planes = dests // group
    z = lax.axis_index("z")
    lines_in = pltpu.make_async_copy(line_from, line_ref, sems.at[0])
    lines_in.start()
    images_in = pltpu.make_async_copy(image_from, image_ref, sems.at[1])
    images_in.start()

    def widen(k, carry):
        for i in range(8):
            r = k * 8 + i
            at = pl.multiple_of(r * 2 * FX, 2 * FX)
            to = pl.ds(pl.multiple_of(r * number, number), number)
            real_ref[to, :] = image_ref[:, pl.ds(at, FX)].astype(F32)
            imag_ref[to, :] = image_ref[:, pl.ds(at + FX, FX)].astype(F32)
        return carry

    owner = owner_ref[...]
    plane = owner // group
    chunk = jnp.zeros_like(owner)
    for k in range(planes):
        at = functools.reduce(
            lambda value, p: jnp.where(z == p, int(place_of[p, k]), value), range(planes), 0
        )
        chunk = jnp.where(plane == k, at, chunk)
    dest = chunk * group + (owner & (group - 1))
    owner_rows = iota((dests, FY), 0)
    for b in range(blocks):
        n, l = b // LIST, b % LIST
        hot = owner_rows == dest[n : n + 1, l * FY : (l + 1) * FY]
        hot_ref[b * dests : (b + 1) * dests, :] = hot.astype(F32).astype(BF16)
    before = (iota((FY, FY), 0) < iota((FY, FY), 1)).astype(F32).astype(BF16)
    prefix = jnp.dot(hot_ref[...], before, preferred_element_type=F32)
    lines_in.wait()
    running = jnp.zeros((dests, 1), F32)
    lane = iota((1, FY), 1).astype(F32)
    ranks = iota((pad, FY), 0)
    total = jnp.zeros((4 * dests, pad), F32)
    for b in range(blocks):
        n, l = b // LIST, b % LIST
        hot = hot_ref[b * dests : (b + 1) * dests, :].astype(F32)
        part = prefix[b * dests : (b + 1) * dests, :]
        rank = jnp.sum(hot * (part + running), axis=0, keepdims=True).astype(I32)
        running = running + part[:, FY - 1 :] + hot[:, FY - 1 :]
        line = line_ref[n : n + 1, l * FY : (l + 1) * FY]
        digits = [
            hot * lane,
            hot * float(b),
            hot * (line & 255).astype(F32),
            hot * ((line >> 8) + 1).astype(F32),
        ]
        left = jnp.concatenate(digits, axis=0).astype(BF16)
        right = (ranks == rank).astype(F32).astype(BF16)
        total = total + lax.dot_general(
            left, right, (((1,), (1,)), ((), ())), preferred_element_type=F32
        )
    digit_ref[...] = total
    row = total[:dests].astype(I32) * number + (total[dests : 2 * dests].astype(I32) >> 1)
    index_ref[...] = jnp.where(iota((dests, pad), 1) == pad - 1, running.astype(I32), row)
    images_in.wait()
    lax.fori_loop(0, FY // 8, widen, 0)


def row_slots(place_of, owners, lines, images, dests, group, pad):
    number, width = images.shape
    return pl.pallas_call(
        functools.partial(slot_kernel, dests, group, pad, place_of),
        out_shape=(
            jax.ShapeDtypeStruct((dests, pad), I32),
            jax.ShapeDtypeStruct((4 * dests, pad), F32),
            pltpu.VMEM((number * FY, FX), F32),
            pltpu.VMEM((number * FY, FX), F32),
        ),
        in_specs=[pl.BlockSpec(memory_space=pltpu.VMEM)]
        + [pl.BlockSpec(memory_space=pltpu.HBM)] * 2,
        scratch_shapes=[
            pltpu.VMEM((number * LIST * dests, FY), BF16),
            pltpu.VMEM(lines.shape, I32),
            pltpu.VMEM(images.shape, BF16),
            pltpu.SemaphoreType.DMA((2,)),
        ],
        compiler_params=vmem_params(20),
        cost_estimate=cost(3e9, 12e6),
        name="slots",
    )(owners, in_hbm(lines), in_hbm(images))


def place_kernel(
    chunk, cap, index_ref, digit_ref, real_ref, imag_ref, out_ref, token_ref, left_ref, right_ref,
    held, sems,
):
    group, pad = index_ref.shape
    dests = digit_ref.shape[0] // 4
    words = pad // (2 * FX)
    span = cap + 16
    zeros = jnp.zeros((group * span, FX), F32)

    left_ref[...] = zeros
    right_ref[...] = zeros
    token_ref[...] = jnp.zeros_like(token_ref)
    def member(d, carry):
        start = d * span

        def some(i, inner):
            spots = [index_ref[d, i * 16 + j] for j in range(16)]
            lefts = [real_ref[pl.ds(at, 1), :] for at in spots]
            rights = [imag_ref[pl.ds(at, 1), :] for at in spots]
            for j in range(16):
                left_ref[pl.ds(start + i * 16 + j, 1), :] = lefts[j]
                right_ref[pl.ds(start + i * 16 + j, 1), :] = rights[j]
            return inner

        lax.fori_loop(0, (index_ref[d, pad - 1] + 15) // 16, some, 0)
        return carry

    lax.fori_loop(0, group, member, 0)
    copies = []
    for d in range(group):
        start = d * span
        for which in range(4):
            row = which * dests + chunk * group + d
            for word in range(words):
                to = start + cap + which * words + word
                lane = word * 2 * FX
                left_ref[to : to + 1, :] = digit_ref[row : row + 1, lane : lane + FX]
                right_ref[to : to + 1, :] = digit_ref[row : row + 1, lane + FX : lane + 2 * FX]
        at = slice(start, start + span)
        held[at, :FX] = left_ref[at, :].astype(BF16)
        held[at, FX:] = right_ref[at, :].astype(BF16)
        copies.append(pltpu.make_async_copy(held.at[at], out_ref.at[at], sems.at[d]))
        copies[-1].start()
    for copy in copies:
        copy.wait()


def placed_rows(chunk, group, cap, index, digits, real, imag):
    pad = index.shape[1]
    span = cap + 16
    vmem = pl.BlockSpec(memory_space=pltpu.VMEM)
    return pl.pallas_call(
        functools.partial(place_kernel, chunk, cap),
        grid=(1,),
        out_shape=(pltpu.HBM((group * span, 2 * FX), BF16), jax.ShapeDtypeStruct((8, FX), F32)),
        in_specs=[
            pl.BlockSpec((group, pad), lambda i: (chunk, 0), memory_space=pltpu.SMEM),
            vmem,
            vmem,
            vmem,
        ],
        out_specs=(pl.BlockSpec(memory_space=pltpu.HBM), vmem),
        scratch_shapes=[pltpu.VMEM((group * span, FX), F32)] * 2
        + [pltpu.VMEM((group * span, 2 * FX), BF16), pltpu.SemaphoreType.DMA((group,))],
        compiler_params=vmem_params(12),
        cost_estimate=cost(1e5, 1e5),
        name="place",
    )(index, digits, real, imag)


def rotate(real, imag, cosine, sine):
    return real * cosine - imag * sine, real * sine + imag * cosine


def score_kernel(
    planes, inner, half_ref, turn_ref, image_from, near_ref, far_ref, offset_ref, orient_ref,
    interp_ref, token_ref, table_ref, evidence_ref, image_ref, sems,
):
    number = image_ref.shape[0]
    refs = near_ref.shape[0]
    rows_half = FY // 2
    group = 16
    half = half_ref[0]
    copies = []
    for k in range(4):
        side = half if k < 2 else 1 - half
        quarter = FY * FX // 2
        at = pl.ds(pl.multiple_of((side * 2 + k % 2) * quarter, quarter), quarter)
        copies.append(
            pltpu.make_async_copy(image_from.at[:, at], image_ref.at[:, at], sems.at[k])
        )
        copies[-1].start()
    off_x = offset_ref[:, 0:1]
    off_y = offset_ref[:, 1:2]
    lane = iota((number, FX), 1)

    def wave(units):
        angle = STEP * (units & (FY - 1)).astype(F32)
        return jnp.cos(angle), jnp.sin(angle)

    col_cos, col_sin = wave(-lane * off_x)
    one_cos, one_sin = wave(jnp.broadcast_to(-off_y, (number, FX)))
    ref_lane = iota((1, FX), 1)
    x1_cos, x1_sin = wave(jnp.broadcast_to(ref_lane, (refs, FX)))
    x2_cos, x2_sin = wave(jnp.broadcast_to(2 * ref_lane, (refs, FX)))

    def shifts(real, imag, c1, s1, c2, s2):
        rc, rs, ic, is_ = real * c1, real * s1, imag * c1, imag * s1
        pairs = [
            (real * c2 + imag * s2, imag * c2 - real * s2),
            (rc + is_, ic - rs),
            (real, imag),
            (rc - is_, ic + rs),
        ]
        return pairs

    def stacked(pairs):
        return jnp.concatenate(
            [jnp.concatenate([p.astype(BF16), q.astype(BF16)], axis=1) for p, q in pairs],
            axis=0,
        )

    def run(ref, first, total, waits):
        start_cos, start_sin = wave(-(lane * off_x + first * off_y))

        def block(k, carry):
            total, cosine, sine = carry
            lefts, rights = [], []
            for i in range(group):
                r = first + k * group + i
                at = pl.multiple_of(r * 2 * FX, 2 * FX)
                at_ref = pl.multiple_of((k * group + i) * 2 * FX, 2 * FX)
                real = image_ref[:, pl.ds(at, FX)].astype(F32)
                imag = image_ref[:, pl.ds(at + FX, FX)].astype(F32)
                real, imag = rotate(real, imag, cosine, sine)
                cosine, sine = rotate(cosine, sine, one_cos, one_sin)
                lefts.append(
                    stacked(
                        shifts(
                            real, imag, turn_ref[0, r], turn_ref[1, r], turn_ref[2, r], turn_ref[3, r]
                        )
                    )
                )
                real = ref[:, pl.ds(at_ref, FX)].astype(F32)
                imag = ref[:, pl.ds(at_ref + FX, FX)].astype(F32)
                rights.append(stacked(shifts(real, imag, x1_cos, -x1_sin, x2_cos, -x2_sin)))
            total = total + lax.dot_general(
                jnp.concatenate(lefts, axis=1),
                jnp.concatenate(rights, axis=1),
                (((1,), (1,)), ((), ())),
                preferred_element_type=F32,
            )
            return total, cosine, sine

        carry = (total, start_cos, start_sin)
        turns = rows_half // group // len(waits)
        for k, wait in enumerate(waits):
            wait.wait()
            carry = lax.fori_loop(k * turns, (k + 1) * turns, block, carry)
        return carry[0]

    total = jnp.zeros((TY * number, TX * refs), F32)
    total = run(near_ref, half * rows_half, total, copies[:2])
    total = run(far_ref, (1 - half) * rows_half, total, copies[2:])
    total = total * (1.0 / math.sqrt(FY * 2 * FX))
    parts = [total[b * number : (b + 1) * number, :] for b in range(TY)]
    top = functools.reduce(jnp.maximum, parts)
    top = jnp.max(top, axis=1, keepdims=True)
    mass = sum(jnp.sum(jnp.exp(part - top), axis=1, keepdims=True) for part in parts)
    evidence = top + jnp.log(mass)
    evidence_ref[...] = jnp.broadcast_to(evidence, (number, FX))
    spot = iota((number, TX * refs), 1)
    shift_of = spot // refs
    spot = spot & (refs - 1)
    local = refs // (planes * inner)
    plane = lax.axis_index("z") - spot // (inner * local)
    plane = jnp.where(plane < 0, plane + planes, plane)
    column = lax.axis_index("x") ^ ((spot // local) & (inner - 1))
    name = (plane * inner + column) * local + (spot & (local - 1))
    slot = iota((number, FX), 1)
    table = jnp.where(slot == 32, off_x.astype(F32), 0.0)
    table = jnp.where(slot == 33, off_y.astype(F32), table)
    for l in range(LIST):
        table = jnp.where(slot == 34 + l, interp_ref[:, l : l + 1].astype(F32), table)
        for b in range(TY):
            weights = jnp.exp(parts[b] - evidence)
            for a in range(TX):
                chosen = (name == orient_ref[:, l : l + 1]) & (shift_of == a)
                value = jnp.sum(jnp.where(chosen, weights, 0.0), axis=1, keepdims=True)
                table = jnp.where(slot == l * 16 + b * TX + a, value, table)
    table_ref[...] = table


def weights_table(
    planes, inner, half, images, near, far, offsets, orientations, interp_index, token
):
    number = images.shape[0]
    turn = np.arange(FY) * STEP
    turns = np.stack([np.cos(turn), np.sin(turn), np.cos(2 * turn), np.sin(2 * turn)])
    smem = pl.BlockSpec(memory_space=pltpu.SMEM)
    vmem = pl.BlockSpec(memory_space=pltpu.VMEM)
    return pl.pallas_call(
        functools.partial(score_kernel, planes, inner),
        out_shape=[jax.ShapeDtypeStruct((number, FX), F32)] * 2,
        in_specs=[smem, smem, pl.BlockSpec(memory_space=pltpu.HBM)] + [vmem] * 6,
        scratch_shapes=[pltpu.VMEM(images.shape, BF16), pltpu.SemaphoreType.DMA((4,))],
        compiler_params=vmem_params(14),
        cost_estimate=cost(1e9, 5e6),
        name="scores",
    )(
        half, jnp.asarray(turns, F32), in_hbm(images), near, far, offsets, orientations,
        interp_index, token,
    )


def wave_table():
    shift = np.arange(NSHIFT)[:, None] - SHIFTS
    angle = STEP * ((shift * np.arange(FX)[None, :]) % FY)
    table = np.concatenate(
        [
            np.concatenate([np.cos(angle), np.sin(angle)], axis=1),
            np.concatenate([-np.sin(angle), np.cos(angle)], axis=1),
        ],
        axis=0,
    ).astype(np.float32)
    high = table.astype(jnp.bfloat16)
    low = (table - high.astype(np.float32)).astype(jnp.bfloat16)
    return np.concatenate([high, high, low], axis=0)


def gather_kernel(cap, pad, first, row_ref, table_ref, wave_ref, mats_ref, *refs):
    base_ref = refs[0] if first is None else None
    out_ref, mixed_ref, line_ref = refs[1 if first is None else 0], refs[-2], refs[-1]
    lines = out_ref.shape[0]
    members = table_ref.shape[0]
    count = mats_ref.shape[0]
    span = cap + 16
    group = row_ref.shape[0] // span
    words = pad // (2 * FX)
    low_count = count // 2
    table_high, table_low = split(table_ref[:, :64])
    picks = jnp.concatenate([table_high, table_low], axis=1)
    number = members // group
    mats = jnp.concatenate(
        [mats_ref[:low_count].reshape(low_count * FX, FX), mats_ref[low_count:].reshape(low_count * FX, FX)],
        axis=1,
    )
    def block(s, carry):
        at = pl.multiple_of(s * span, 16)
        extra = row_ref[pl.ds(at + cap, 16), :].astype(F32)
        digit = [
            jnp.concatenate(
                [extra[which * words + word : which * words + word + 1] for word in range(words)],
                axis=1,
            )[:, :cap].astype(I32)
            for which in range(4)
        ]
        r = digit[0]
        member = s * number + (digit[1] >> 1)
        front = (digit[1] & 1) == 0
        line_ref[s] = digit[2] + (digit[3] - 1) * 256
        hot = (iota((members, cap), 0) == member).astype(F32).astype(BF16)
        got = lax.dot_general(picks, hot, (((0,), (0,)), ((), ())), preferred_element_type=F32)
        got = got[:64] + got[64:]
        weight = jnp.where(front, got[0:16], got[16:32])
        off_x = got[32:33].astype(I32)
        off_y = got[33:34].astype(I32)
        interp = jnp.where(front, got[34:35], got[35:36])
        sub = iota((8, cap), 0)
        units = r * ((sub & 3) - TY // 2 - off_y) - jnp.where(sub >= 4, FY // 4, 0)
        wave = jnp.cos(STEP * (units & (FY - 1)).astype(F32))
        gate_real = sum(weight[b * TX : (b + 1) * TX] * wave[b : b + 1] for b in range(TY))
        gate_imag = sum(weight[b * TX : (b + 1) * TX] * wave[4 + b : 5 + b] for b in range(TY))
        spot = iota((NSHIFT, cap), 0) + off_x
        coef_real = jnp.zeros((NSHIFT, cap), F32)
        coef_imag = jnp.zeros((NSHIFT, cap), F32)
        for a in range(TX):
            here = spot == a - TX // 2 + SHIFTS
            coef_real = jnp.where(here, gate_real[a : a + 1], coef_real)
            coef_imag = jnp.where(here, gate_imag[a : a + 1], coef_imag)
        high, low = split(jnp.concatenate([coef_real, coef_imag], axis=0))
        coef = jnp.concatenate([high, low, high], axis=0)
        phase = lax.dot_general(
            coef, wave_ref[...], (((0,), (0,)), ((), ())), preferred_element_type=F32
        )
        values = row_ref[pl.ds(at, cap), :].astype(F32)
        real, imag = rotate(values[:, :FX], values[:, FX:], phase[:, :FX], phase[:, FX:])
        slices = jnp.concatenate([real, imag], axis=0).astype(BF16)
        column = jnp.transpose(jnp.broadcast_to(interp, (8, cap)))[:, 0:1]
        column = jnp.broadcast_to(column, (cap, FX)).astype(I32)
        column = jnp.concatenate([column, column], axis=0)
        which = jnp.where(column >= low_count, column - low_count, column)
        zero = jnp.zeros_like(slices)
        pieces = [jnp.where(which == q, slices, zero) for q in range(low_count)]
        mixed = jnp.dot(jnp.concatenate(pieces, axis=1), mats, preferred_element_type=F32)
        mixed = jnp.where(column >= low_count, mixed[:, FX:], mixed[:, :FX]).astype(BF16)
        to = pl.ds(pl.multiple_of(s * cap, 16), cap)
        mixed_ref[to, :FX] = mixed[:cap]
        mixed_ref[to, FX:] = mixed[cap:]
        return carry

    lax.fori_loop(0, group, block, 0, unroll=2 if first else 2)
    line = jnp.concatenate([line_ref[s] for s in range(group)], axis=1)
    tile = min(512, lines // 2)
    rows = iota((tile, group * cap), 0)
    for at in range(0, lines, tile):
        hot = jnp.where(rows == line - at, 1.0, 0.0).astype(BF16)
        value = jnp.dot(hot, mixed_ref[...], preferred_element_type=F32)
        if base_ref is not None:
            value = value + base_ref[at : at + tile, :]
        out_ref[at : at + tile, :] = value
        if first:
            refs[1][at : at + tile, :] = value.astype(BF16)


def partial_lines(cap, pad, rows, table, mats, lines, first, base=None):
    group = rows.shape[0] // (cap + 16)
    shape = jax.ShapeDtypeStruct((lines, 2 * FX), F32)
    short = jax.ShapeDtypeStruct((lines, 2 * FX), BF16)
    vmem = pl.BlockSpec(memory_space=pltpu.VMEM)
    extra = () if base is None else (base,)
    return pl.pallas_call(
        functools.partial(gather_kernel, cap, pad, None if extra else first),
        out_shape=(shape, short) if first else shape,
        in_specs=[vmem] * (4 + len(extra)),
        scratch_shapes=[
            pltpu.VMEM((group * cap, 2 * FX), BF16),
            pltpu.VMEM((group, 1, cap), I32),
        ],
        compiler_params=vmem_params(20),
        cost_estimate=cost(1e6, 1e5),
        name="lines",
    )(rows, table, jnp.asarray(wave_table()), mats, *extra)


def relay_kernel(planes, step, place_of, *refs):
    up_from, down_from, _, _, up_to, down_to, came_ref, sent_ref, sems = refs[-9:]
    parts = refs[:-9]
    z = lax.axis_index("z")
    lines = up_to.shape[0]
    tile = min(512, lines)
    tiles = lines // tile

    def pull(came, way, k):
        at = pl.ds(k * tile, tile)
        return pltpu.make_async_copy(came.at[at], came_ref.at[way, at], sems.at[0, way, k])

    def push(out, way, k):
        at = pl.ds(k * tile, tile)
        return pltpu.make_async_copy(sent_ref.at[way, at], out.at[at], sems.at[1, way, k])

    for p in range(planes):
        jobs = []
        if p < step:
            jobs.append((0, place_of[p, planes - step + p], up_from if p > 0 else None, up_to))
        if p >= planes - step:
            edge = p == planes - 1
            jobs.append((1, place_of[p, p - planes + step], None if edge else down_from, down_to))
        if jobs:

            @pl.when(z == p)
            def _(jobs=jobs):
                for way, _, came, _ in jobs:
                    for k in range(tiles if came is not None else 0):
                        pull(came, way, k).start()
                for way, index, came, out in jobs:
                    for k in range(tiles):
                        at = slice(k * tile, (k + 1) * tile)
                        value = parts[index][at, :]
                        if came is not None:
                            pull(came, way, k).wait()
                            value = value + came_ref[way, at, :].astype(F32)
                        sent_ref[way, at, :] = value.astype(BF16)
                        push(out, way, k).start()
                for way, _, _, out in jobs:
                    for k in range(tiles):
                        push(out, way, k).wait()


def relay(planes, step, place_of, parts, up, down, tokens):
    vmem = pl.BlockSpec(memory_space=pltpu.VMEM)
    hbm = pl.BlockSpec(memory_space=pltpu.HBM)
    lines = up.shape[0]
    return pl.pallas_call(
        functools.partial(relay_kernel, planes, step, place_of),
        out_shape=[pltpu.HBM(up.shape, BF16)] * 2,
        in_specs=[vmem] * len(parts) + [hbm, hbm, vmem, vmem],
        out_specs=[hbm, hbm],
        scratch_shapes=[
            pltpu.VMEM((2, lines, 2 * FX), BF16),
            pltpu.VMEM((2, lines, 2 * FX), BF16),
            pltpu.SemaphoreType.DMA((2, 2, lines // min(512, lines))),
        ],
        compiler_params=vmem_params(10),
        cost_estimate=cost(60e9, 8e6),
        name="relay",
    )(*parts, in_hbm(up), in_hbm(down), *tokens)


def together(*values):
    return lax.optimization_barrier(values)


def block_order(planes):
    return np.array(
        [sorted(range(planes), key=lambda d: (-abs(d - z), -d)) for z in range(planes)], np.int32
    )


def body(
    planes, inner, slab,
    images, references, offsets, orientations, interp_mats, interp_index, owners, line_index, volume_in,
):
    number = images.shape[0]
    lines = volume_in.shape[0]
    group = inner * slab
    devices = planes * group
    rows_all = number * LIST * FY
    cap = max(2, 7 * rows_all // (4 * devices))
    span = cap + 16
    pad = -(-(cap + 1) // (2 * FX)) * 2 * FX
    half = lax.axis_index("slab") % 2

    local = references.shape[0]
    width = references.shape[1]
    mine = lax.dynamic_slice_in_dim(references, half * (width // 2), width // 2, axis=1)
    block = [mine]
    for e in range(1, inner):
        block.append(lax.ppermute(mine, "x", [(i, i ^ e) for i in range(inner)]))

    place_of = np.argsort(block_order(planes), axis=1).astype(np.int32)
    index, digits, real, imag = row_slots(
        place_of,
        owners.reshape(number, LIST * FY),
        line_index,
        images,
        devices,
        group,
        pad,
    )
    block, index = together(block, index)
    block = jnp.concatenate(block, axis=0)
    near = [block]
    for shift in range(1, planes):
        near.append(lax.ppermute(block, "z", [(p, (p + shift) % planes) for p in range(planes)]))
    def place(k, index):
        return placed_rows(k, group, cap, index, digits, real, imag)

    placed = [None] * planes
    placed[0], token = place(0, index)
    token, index = together(token, index)
    placed[1], token = place(1, index)

    def to_members(value):
        return lax.all_to_all(
            value.reshape(group, span, 2 * FX), ("x", "slab"), 0, 0, tiled=True
        ).reshape(group * span, 2 * FX)

    got = to_members(placed[0])
    near, token = together(near, token)
    near = jnp.concatenate(near, axis=0)
    far = lax.ppermute(near, "slab", [(i, i ^ 1) for i in range(slab)])
    table, evidence = weights_table(
        planes, inner, half.reshape(1).astype(I32), images, near, far, offsets, orientations,
        interp_index, token,
    )
    table, got, index = together(table, got, index)
    early = min(2, planes - 1)
    placed[early], token = place(early, index)
    later = token
    tables = lax.all_to_all(
        jnp.broadcast_to(table[None], (group,) + table.shape), ("x", "slab"), 0, 0, tiled=True
    ).reshape(group * number, FX)
    tables, placed[1], later = together(tables, placed[1], later)
    got = [got, to_members(placed[1])]

    def lines_of(k, base=None):
        return partial_lines(cap, pad, got[k], tables, interp_mats, lines, k == 0, base)

    part, short = lines_of(0)
    part, index = together(part, index)
    parts = [part]
    for k in range(early + 1, min(early + 2, planes)):
        placed[k], token = place(k, index)
    placed[early], token = together(placed[early], token)
    got.append(to_members(placed[early]))
    up = down = lax.ppermute(short, "z", sorted({(0, 1), (planes - 1, planes - 2)}))
    for s in range(2, planes):
        part = lines_of(s - 1)
        if s + 1 < planes:
            part, index = together(part, index)
            if placed[s + 1] is None:
                placed[s + 1], _ = place(s + 1, index)
            part, placed[s + 1] = together(part, placed[s + 1])
            got.append(to_members(placed[s + 1]))
        parts.append(part)
        up_send, down_send = relay(planes, s, place_of, parts, up, down, (token, later))
        up = lax.ppermute(up_send, "z", [(p, p + 1) for p in range(s)])
        down = lax.ppermute(down_send, "z", [(p, p - 1) for p in range(planes - s, planes)])
    last = lines_of(planes - 1, volume_in)
    volume = last + up.astype(F32) + down.astype(F32)
    return volume, evidence[:, 0]


def solution(mesh):
    dom, slab = mesh.shape["dom"], mesh.shape["slab"]
    planes = dom // INNER
    fine = Mesh(mesh.devices.reshape(planes, INNER, slab), ("z", "x", "slab"))
    every = ("z", "x", "slab")
    in_specs = (
        P(every, None),
        P(("z", "x"), None),
        P(every, None),
        P(every, None),
        P(),
        P(every, None),
        P(every, None, None),
        P(every, None),
        P(every, None),
    )
    out_specs = (P(every, None), P(every))
    return jax.shard_map(
        functools.partial(body, planes, INNER, slab),
        mesh=fine,
        in_specs=in_specs,
        out_specs=out_specs,
        check_vma=False,
    )
```

```python
import functools
import math

import jax
import jax.numpy as jnp
import numpy as np
from jax import lax
from jax.experimental import pallas as pl
from jax.experimental.pallas import tpu as pltpu
from jax.sharding import Mesh
from jax.sharding import PartitionSpec as P

FY = 256
FX = 128
TX = 4
TY = 4
LIST = 2
OFF = 8
INNER = 2
F32 = jnp.float32
BF16 = jnp.bfloat16
I32 = jnp.int32
STEP = 2.0 * math.pi / FY
SHIFTS = OFF + max(TX, TY) // 2
NSHIFT = 24


def vmem_params(mib):
    return pltpu.CompilerParams(vmem_limit_bytes=mib << 20)


def whole(shape):
    return pl.BlockSpec(shape, lambda *_: (0,) * len(shape))


def cost(flops, nbytes):
    return pl.CostEstimate(flops=int(flops), bytes_accessed=int(nbytes), transcendentals=0)


def iota(shape, axis):
    return lax.broadcasted_iota(I32, shape, axis)


def in_hbm(value):
    return pltpu.with_memory_space_constraint(value, pltpu.HBM)


def split(value):
    high = value.astype(BF16)
    return high, (value - high.astype(F32)).astype(BF16)


def slot_kernel(
    dests, group, pad, place_of, owner_ref, line_from, image_from,
    index_ref, digit_ref, real_ref, imag_ref, hot_ref, line_ref, image_ref, sems,
):
    number = owner_ref.shape[0]
    blocks = number * LIST
    planes = dests // group
    z = lax.axis_index("z")
    lines_in = pltpu.make_async_copy(line_from, line_ref, sems.at[0])
    lines_in.start()
    images_in = pltpu.make_async_copy(image_from, image_ref, sems.at[1])
    images_in.start()

    def widen(k, carry):
        for i in range(8):
            r = k * 8 + i
            at = pl.multiple_of(r * 2 * FX, 2 * FX)
            to = pl.ds(pl.multiple_of(r * number, number), number)
            real_ref[to, :] = image_ref[:, pl.ds(at, FX)].astype(F32)
            imag_ref[to, :] = image_ref[:, pl.ds(at + FX, FX)].astype(F32)
        return carry

    owner = owner_ref[...]
    plane = owner // group
    chunk = jnp.zeros_like(owner)
    for k in range(planes):
        at = functools.reduce(
            lambda value, p: jnp.where(z == p, int(place_of[p, k]), value), range(planes), 0
        )
        chunk = jnp.where(plane == k, at, chunk)
    dest = chunk * group + (owner & (group - 1))
    owner_rows = iota((dests, FY), 0)
    for b in range(blocks):
        n, l = b // LIST, b % LIST
        hot = owner_rows == dest[n : n + 1, l * FY : (l + 1) * FY]
        hot_ref[b * dests : (b + 1) * dests, :] = hot.astype(F32).astype(BF16)
    before = (iota((FY, FY), 0) < iota((FY, FY), 1)).astype(F32).astype(BF16)
    prefix = jnp.dot(hot_ref[...], before, preferred_element_type=F32)
    lines_in.wait()
    running = jnp.zeros((dests, 1), F32)
    lane = iota((1, FY), 1).astype(F32)
    ranks = iota((pad, FY), 0)
    total = jnp.zeros((4 * dests, pad), F32)
    for b in range(blocks):
        n, l = b // LIST, b % LIST
        hot = hot_ref[b * dests : (b + 1) * dests, :].astype(F32)
        part = prefix[b * dests : (b + 1) * dests, :]
        rank = jnp.sum(hot * (part + running), axis=0, keepdims=True).astype(I32)
        running = running + part[:, FY - 1 :] + hot[:, FY - 1 :]
        line = line_ref[n : n + 1, l * FY : (l + 1) * FY]
        digits = [
            hot * lane,
            hot * float(b),
            hot * (line & 255).astype(F32),
            hot * ((line >> 8) + 1).astype(F32),
        ]
        left = jnp.concatenate(digits, axis=0).astype(BF16)
        right = (ranks == rank).astype(F32).astype(BF16)
        total = total + lax.dot_general(
            left, right, (((1,), (1,)), ((), ())), preferred_element_type=F32
        )
    digit_ref[...] = total
    row = total[:dests].astype(I32) * number + (total[dests : 2 * dests].astype(I32) >> 1)
    index_ref[...] = jnp.where(iota((dests, pad), 1) == pad - 1, running.astype(I32), row)
    images_in.wait()
    lax.fori_loop(0, FY // 8, widen, 0)


def row_slots(place_of, owners, lines, images, dests, group, pad):
    number, width = images.shape
    return pl.pallas_call(
        functools.partial(slot_kernel, dests, group, pad, place_of),
        out_shape=(
            jax.ShapeDtypeStruct((dests, pad), I32),
            jax.ShapeDtypeStruct((4 * dests, pad), F32),
            pltpu.VMEM((number * FY, FX), F32),
            pltpu.VMEM((number * FY, FX), F32),
        ),
        in_specs=[pl.BlockSpec(memory_space=pltpu.VMEM)]
        + [pl.BlockSpec(memory_space=pltpu.HBM)] * 2,
        scratch_shapes=[
            pltpu.VMEM((number * LIST * dests, FY), BF16),
            pltpu.VMEM(lines.shape, I32),
            pltpu.VMEM(images.shape, BF16),
            pltpu.SemaphoreType.DMA((2,)),
        ],
        compiler_params=vmem_params(20),
        cost_estimate=cost(3e9, 12e6),
        name="slots",
    )(owners, in_hbm(lines), in_hbm(images))


def place_kernel(
    chunk, cap, index_ref, digit_ref, real_ref, imag_ref, out_ref, token_ref, left_ref, right_ref,
    held, sems,
):
    group = out_ref.shape[0] // (cap + 16)
    pad = index_ref.shape[0] // group
    dests = digit_ref.shape[0] // 4
    words = pad // (2 * FX)
    span = cap + 16
    zeros = jnp.zeros((group * span, FX), F32)

    left_ref[...] = zeros
    right_ref[...] = zeros
    token_ref[...] = jnp.zeros_like(token_ref)
    def member(d, carry):
        start = d * span
        base = d * pad

        def some(i, inner):
            at = base + i * 32
            to = start + i * 32
            spots = [index_ref[at + j] for j in range(32)]
            lefts = [real_ref[pl.ds(spot, 1), :] for spot in spots]
            rights = [imag_ref[pl.ds(spot, 1), :] for spot in spots]
            for j in range(32):
                left_ref[pl.ds(to + j, 1), :] = lefts[j]
                right_ref[pl.ds(to + j, 1), :] = rights[j]
            return inner

        lax.fori_loop(0, (index_ref[base + pad - 1] + 31) // 32, some, 0)
        return carry

    lax.fori_loop(0, group, member, 0)
    copies = []
    for d in range(group):
        start = d * span
        for which in range(4):
            row = which * dests + chunk * group + d
            for word in range(words):
                to = start + cap + which * words + word
                lane = word * 2 * FX
                left_ref[to : to + 1, :] = digit_ref[row : row + 1, lane : lane + FX]
                right_ref[to : to + 1, :] = digit_ref[row : row + 1, lane + FX : lane + 2 * FX]
        at = slice(start, start + span)
        held[at, :FX] = left_ref[at, :].astype(BF16)
        held[at, FX:] = right_ref[at, :].astype(BF16)
        copies.append(pltpu.make_async_copy(held.at[at], out_ref.at[at], sems.at[d]))
        copies[-1].start()
    for copy in copies:
        copy.wait()


def placed_rows(chunk, group, cap, index, digits, real, imag):
    pad = digits.shape[1]
    span = cap + 16
    vmem = pl.BlockSpec(memory_space=pltpu.VMEM)
    return pl.pallas_call(
        functools.partial(place_kernel, chunk, cap),
        grid=(1,),
        out_shape=(pltpu.HBM((group * span, 2 * FX), BF16), jax.ShapeDtypeStruct((8, FX), F32)),
        in_specs=[
            pl.BlockSpec((group * pad,), lambda i: (chunk,), memory_space=pltpu.SMEM),
            vmem,
            vmem,
            vmem,
        ],
        out_specs=(pl.BlockSpec(memory_space=pltpu.HBM), vmem),
        scratch_shapes=[pltpu.VMEM((group * span, FX), F32)] * 2
        + [pltpu.VMEM((group * span, 2 * FX), BF16), pltpu.SemaphoreType.DMA((group,))],
        compiler_params=vmem_params(12),
        cost_estimate=cost(1e5, 1e5),
        name="place",
    )(index, digits, real, imag)


def rotate(real, imag, cosine, sine):
    return real * cosine - imag * sine, real * sine + imag * cosine


def score_kernel(
    planes, inner, half_ref, turn_ref, image_from, near_ref, far_ref, offset_ref, orient_ref,
    interp_ref, token_ref, table_ref, evidence_ref, image_ref, sems,
):
    number = image_ref.shape[0]
    refs = near_ref.shape[0]
    rows_half = FY // 2
    group = 16
    half = half_ref[0]
    copies = []
    for k in range(4):
        side = half if k < 2 else 1 - half
        quarter = FY * FX // 2
        at = pl.ds(pl.multiple_of((side * 2 + k % 2) * quarter, quarter), quarter)
        copies.append(
            pltpu.make_async_copy(image_from.at[:, at], image_ref.at[:, at], sems.at[k])
        )
        copies[-1].start()
    off_x = offset_ref[:, 0:1]
    off_y = offset_ref[:, 1:2]
    lane = iota((number, FX), 1)

    def wave(units):
        angle = STEP * (units & (FY - 1)).astype(F32)
        return jnp.cos(angle), jnp.sin(angle)

    col_cos, col_sin = wave(-lane * off_x)
    one_cos, one_sin = wave(jnp.broadcast_to(-off_y, (number, FX)))
    ref_lane = iota((1, FX), 1)
    x1_cos, x1_sin = wave(jnp.broadcast_to(ref_lane, (refs, FX)))
    x2_cos, x2_sin = wave(jnp.broadcast_to(2 * ref_lane, (refs, FX)))

    def shifts(real, imag, c1, s1, c2, s2):
        rc, rs, ic, is_ = real * c1, real * s1, imag * c1, imag * s1
        pairs = [
            (real * c2 + imag * s2, imag * c2 - real * s2),
            (rc + is_, ic - rs),
            (real, imag),
            (rc - is_, ic + rs),
        ]
        return pairs

    def stacked(pairs):
        return jnp.concatenate(
            [jnp.concatenate([p.astype(BF16), q.astype(BF16)], axis=1) for p, q in pairs],
            axis=0,
        )

    def run(ref, first, total, waits):
        start_cos, start_sin = wave(-(lane * off_x + first * off_y))

        def block(k, carry):
            total, cosine, sine = carry
            lefts, rights = [], []
            for i in range(group):
                r = first + k * group + i
                at = pl.multiple_of(r * 2 * FX, 2 * FX)
                at_ref = pl.multiple_of((k * group + i) * 2 * FX, 2 * FX)
                real = image_ref[:, pl.ds(at, FX)].astype(F32)
                imag = image_ref[:, pl.ds(at + FX, FX)].astype(F32)
                real, imag = rotate(real, imag, cosine, sine)
                cosine, sine = rotate(cosine, sine, one_cos, one_sin)
                lefts.append(
                    stacked(
                        shifts(
                            real, imag, turn_ref[0, r], turn_ref[1, r], turn_ref[2, r], turn_ref[3, r]
                        )
                    )
                )
                real = ref[:, pl.ds(at_ref, FX)].astype(F32)
                imag = ref[:, pl.ds(at_ref + FX, FX)].astype(F32)
                rights.append(stacked(shifts(real, imag, x1_cos, -x1_sin, x2_cos, -x2_sin)))
            total = total + lax.dot_general(
                jnp.concatenate(lefts, axis=1),
                jnp.concatenate(rights, axis=1),
                (((1,), (1,)), ((), ())),
                preferred_element_type=F32,
            )
            return total, cosine, sine

        carry = (total, start_cos, start_sin)
        turns = rows_half // group // len(waits)
        for k, wait in enumerate(waits):
            wait.wait()
            carry = lax.fori_loop(k * turns, (k + 1) * turns, block, carry)
        return carry[0]

    total = jnp.zeros((TY * number, TX * refs), F32)
    total = run(near_ref, half * rows_half, total, copies[:2])
    total = run(far_ref, (1 - half) * rows_half, total, copies[2:])
    total = total * (1.0 / math.sqrt(FY * 2 * FX))
    parts = [total[b * number : (b + 1) * number, :] for b in range(TY)]
    top = functools.reduce(jnp.maximum, parts)
    top = jnp.max(top, axis=1, keepdims=True)
    mass = sum(jnp.sum(jnp.exp(part - top), axis=1, keepdims=True) for part in parts)
    evidence = top + jnp.log(mass)
    evidence_ref[...] = jnp.broadcast_to(evidence, (number, FX))
    spot = iota((number, TX * refs), 1)
    shift_of = spot // refs
    spot = spot & (refs - 1)
    local = refs // (planes * inner)
    plane = lax.axis_index("z") - spot // (inner * local)
    plane = jnp.where(plane < 0, plane + planes, plane)
    column = lax.axis_index("x") ^ ((spot // local) & (inner - 1))
    name = (plane * inner + column) * local + (spot & (local - 1))
    slot = iota((number, FX), 1)
    table = jnp.where(slot == 32, off_x.astype(F32), 0.0)
    table = jnp.where(slot == 33, off_y.astype(F32), table)
    for l in range(LIST):
        table = jnp.where(slot == 34 + l, interp_ref[:, l : l + 1].astype(F32), table)
        for b in range(TY):
            weights = jnp.exp(parts[b] - evidence)
            for a in range(TX):
                chosen = (name == orient_ref[:, l : l + 1]) & (shift_of == a)
                value = jnp.sum(jnp.where(chosen, weights, 0.0), axis=1, keepdims=True)
                table = jnp.where(slot == l * 16 + b * TX + a, value, table)
    table_ref[...] = table


def weights_table(
    planes, inner, half, images, near, far, offsets, orientations, interp_index, token
):
    number = images.shape[0]
    turn = np.arange(FY) * STEP
    turns = np.stack([np.cos(turn), np.sin(turn), np.cos(2 * turn), np.sin(2 * turn)])
    smem = pl.BlockSpec(memory_space=pltpu.SMEM)
    vmem = pl.BlockSpec(memory_space=pltpu.VMEM)
    return pl.pallas_call(
        functools.partial(score_kernel, planes, inner),
        out_shape=[jax.ShapeDtypeStruct((number, FX), F32)] * 2,
        in_specs=[smem, smem, pl.BlockSpec(memory_space=pltpu.HBM)] + [vmem] * 6,
        scratch_shapes=[pltpu.VMEM(images.shape, BF16), pltpu.SemaphoreType.DMA((4,))],
        compiler_params=vmem_params(14),
        cost_estimate=cost(1e9, 5e6),
        name="scores",
    )(
        half, jnp.asarray(turns, F32), in_hbm(images), near, far, offsets, orientations,
        interp_index, token,
    )


def wave_table():
    shift = np.arange(NSHIFT)[:, None] - SHIFTS
    angle = STEP * ((shift * np.arange(FX)[None, :]) % FY)
    table = np.concatenate(
        [
            np.concatenate([np.cos(angle), np.sin(angle)], axis=1),
            np.concatenate([-np.sin(angle), np.cos(angle)], axis=1),
        ],
        axis=0,
    ).astype(np.float32)
    high = table.astype(jnp.bfloat16)
    low = (table - high.astype(np.float32)).astype(jnp.bfloat16)
    return np.concatenate([high, high, low], axis=0)


def gather_kernel(cap, pad, first, row_ref, table_ref, wave_ref, mats_ref, *refs):
    base_ref = refs[0] if first is None else None
    out_ref, mixed_ref, line_ref = refs[1 if first is None else 0], refs[-2], refs[-1]
    lines = out_ref.shape[0]
    members = table_ref.shape[0]
    count = mats_ref.shape[0]
    span = cap + 16
    group = row_ref.shape[0] // span
    words = pad // (2 * FX)
    low_count = count // 2
    table_high, table_low = split(table_ref[:, :64])
    picks = jnp.concatenate([table_high, table_low], axis=1)
    number = members // group
    mats = jnp.concatenate(
        [mats_ref[:low_count].reshape(low_count * FX, FX), mats_ref[low_count:].reshape(low_count * FX, FX)],
        axis=1,
    )
    def block(s, carry):
        at = pl.multiple_of(s * span, 16)
        extra = row_ref[pl.ds(at + cap, 16), :].astype(F32)
        digit = [
            jnp.concatenate(
                [extra[which * words + word : which * words + word + 1] for word in range(words)],
                axis=1,
            )[:, :cap].astype(I32)
            for which in range(4)
        ]
        r = digit[0]
        member = s * number + (digit[1] >> 1)
        front = (digit[1] & 1) == 0
        line_ref[s] = digit[2] + (digit[3] - 1) * 256
        hot = (iota((members, cap), 0) == member).astype(F32).astype(BF16)
        got = lax.dot_general(picks, hot, (((0,), (0,)), ((), ())), preferred_element_type=F32)
        got = got[:64] + got[64:]
        weight = jnp.where(front, got[0:16], got[16:32])
        off_x = got[32:33].astype(I32)
        off_y = got[33:34].astype(I32)
        interp = jnp.where(front, got[34:35], got[35:36])
        sub = iota((8, cap), 0)
        units = r * ((sub & 3) - TY // 2 - off_y) - jnp.where(sub >= 4, FY // 4, 0)
        wave = jnp.cos(STEP * (units & (FY - 1)).astype(F32))
        gate_real = sum(weight[b * TX : (b + 1) * TX] * wave[b : b + 1] for b in range(TY))
        gate_imag = sum(weight[b * TX : (b + 1) * TX] * wave[4 + b : 5 + b] for b in range(TY))
        spot = iota((NSHIFT, cap), 0) + off_x
        coef_real = jnp.zeros((NSHIFT, cap), F32)
        coef_imag = jnp.zeros((NSHIFT, cap), F32)
        for a in range(TX):
            here = spot == a - TX // 2 + SHIFTS
            coef_real = jnp.where(here, gate_real[a : a + 1], coef_real)
            coef_imag = jnp.where(here, gate_imag[a : a + 1], coef_imag)
        high, low = split(jnp.concatenate([coef_real, coef_imag], axis=0))
        coef = jnp.concatenate([high, low, high], axis=0)
        phase = lax.dot_general(
            coef, wave_ref[...], (((0,), (0,)), ((), ())), preferred_element_type=F32
        )
        values = row_ref[pl.ds(at, cap), :].astype(F32)
        real, imag = rotate(values[:, :FX], values[:, FX:], phase[:, :FX], phase[:, FX:])
        slices = jnp.concatenate([real, imag], axis=0).astype(BF16)
        column = jnp.transpose(jnp.broadcast_to(interp, (8, cap)))[:, 0:1]
        column = jnp.broadcast_to(column, (cap, FX)).astype(I32)
        column = jnp.concatenate([column, column], axis=0)
        which = jnp.where(column >= low_count, column - low_count, column)
        zero = jnp.zeros_like(slices)
        pieces = [jnp.where(which == q, slices, zero) for q in range(low_count)]
        mixed = jnp.dot(jnp.concatenate(pieces, axis=1), mats, preferred_element_type=F32)
        mixed = jnp.where(column >= low_count, mixed[:, FX:], mixed[:, :FX]).astype(BF16)
        to = pl.ds(pl.multiple_of(s * cap, 16), cap)
        mixed_ref[to, :FX] = mixed[:cap]
        mixed_ref[to, FX:] = mixed[cap:]
        return carry

    lax.fori_loop(0, group, block, 0, unroll=2 if first else 2)
    line = jnp.concatenate([line_ref[s] for s in range(group)], axis=1)
    tile = min(512, lines // 2)
    rows = iota((tile, group * cap), 0)
    for at in range(0, lines, tile):
        hot = jnp.where(rows == line - at, 1.0, 0.0).astype(BF16)
        value = jnp.dot(hot, mixed_ref[...], preferred_element_type=F32)
        if base_ref is not None:
            value = value + base_ref[at : at + tile, :]
        out_ref[at : at + tile, :] = value
        if first:
            refs[1][at : at + tile, :] = value.astype(BF16)


def partial_lines(cap, pad, rows, table, mats, lines, first, base=None):
    group = rows.shape[0] // (cap + 16)
    shape = jax.ShapeDtypeStruct((lines, 2 * FX), F32)
    short = jax.ShapeDtypeStruct((lines, 2 * FX), BF16)
    vmem = pl.BlockSpec(memory_space=pltpu.VMEM)
    extra = () if base is None else (base,)
    return pl.pallas_call(
        functools.partial(gather_kernel, cap, pad, None if extra else first),
        out_shape=(shape, short) if first else shape,
        in_specs=[vmem] * (4 + len(extra)),
        scratch_shapes=[
            pltpu.VMEM((group * cap, 2 * FX), BF16),
            pltpu.VMEM((group, 1, cap), I32),
        ],
        compiler_params=vmem_params(20),
        cost_estimate=cost(1e6, 1e5),
        name="lines",
    )(in_hbm(rows), table, jnp.asarray(wave_table()), mats, *extra)


def relay_kernel(planes, step, place_of, *refs):
    up_from, down_from, _, _, up_to, down_to, came_ref, sent_ref, sems = refs[-9:]
    parts = refs[:-9]
    z = lax.axis_index("z")
    lines = up_to.shape[0]
    tile = min(512, lines)
    tiles = lines // tile

    def pull(came, way, k):
        at = pl.ds(k * tile, tile)
        return pltpu.make_async_copy(came.at[at], came_ref.at[way, at], sems.at[0, way, k])

    def push(out, way, k):
        at = pl.ds(k * tile, tile)
        return pltpu.make_async_copy(sent_ref.at[way, at], out.at[at], sems.at[1, way, k])

    for p in range(planes):
        jobs = []
        if p < step:
            jobs.append((0, place_of[p, planes - step + p], up_from if p > 0 else None, up_to))
        if p >= planes - step:
            edge = p == planes - 1
            jobs.append((1, place_of[p, p - planes + step], None if edge else down_from, down_to))
        if jobs:

            @pl.when(z == p)
            def _(jobs=jobs):
                for way, _, came, _ in jobs:
                    for k in range(tiles if came is not None else 0):
                        pull(came, way, k).start()
                for way, index, came, out in jobs:
                    for k in range(tiles):
                        at = slice(k * tile, (k + 1) * tile)
                        value = parts[index][at, :]
                        if came is not None:
                            pull(came, way, k).wait()
                            value = value + came_ref[way, at, :].astype(F32)
                        sent_ref[way, at, :] = value.astype(BF16)
                        push(out, way, k).start()
                for way, _, _, out in jobs:
                    for k in range(tiles):
                        push(out, way, k).wait()


def relay(planes, step, place_of, parts, up, down, tokens):
    vmem = pl.BlockSpec(memory_space=pltpu.VMEM)
    hbm = pl.BlockSpec(memory_space=pltpu.HBM)
    lines = up.shape[0]
    return pl.pallas_call(
        functools.partial(relay_kernel, planes, step, place_of),
        out_shape=[pltpu.HBM(up.shape, BF16)] * 2,
        in_specs=[vmem] * len(parts) + [hbm, hbm, vmem, vmem],
        out_specs=[hbm, hbm],
        scratch_shapes=[
            pltpu.VMEM((2, lines, 2 * FX), BF16),
            pltpu.VMEM((2, lines, 2 * FX), BF16),
            pltpu.SemaphoreType.DMA((2, 2, lines // min(512, lines))),
        ],
        compiler_params=vmem_params(10),
        cost_estimate=cost(60e9, 8e6),
        name="relay",
    )(*parts, in_hbm(up), in_hbm(down), *tokens)


def together(*values):
    return lax.optimization_barrier(values)


def block_order(planes):
    return np.array(
        [sorted(range(planes), key=lambda d: (-abs(d - z), -d)) for z in range(planes)], np.int32
    )


def body(
    planes, inner, slab,
    images, references, offsets, orientations, interp_mats, interp_index, owners, line_index, volume_in,
):
    number = images.shape[0]
    lines = volume_in.shape[0]
    group = inner * slab
    devices = planes * group
    rows_all = number * LIST * FY
    cap = max(2, 7 * rows_all // (4 * devices))
    span = cap + 16
    pad = -(-(cap + 1) // (2 * FX)) * 2 * FX
    half = lax.axis_index("slab") % 2

    local = references.shape[0]
    width = references.shape[1]
    mine = lax.dynamic_slice_in_dim(references, half * (width // 2), width // 2, axis=1)
    block = [mine]
    for e in range(1, inner):
        block.append(lax.ppermute(mine, "x", [(i, i ^ e) for i in range(inner)]))

    place_of = np.argsort(block_order(planes), axis=1).astype(np.int32)
    index, digits, real, imag = row_slots(
        place_of,
        owners.reshape(number, LIST * FY),
        line_index,
        images,
        devices,
        group,
        pad,
    )
    block, index = together(block, index)
    block = jnp.concatenate(block, axis=0)
    near = [block]
    for shift in range(1, planes):
        near.append(lax.ppermute(block, "z", [(p, (p + shift) % planes) for p in range(planes)]))
    index = index.reshape(devices * pad)

    def place(k, index):
        return placed_rows(k, group, cap, index, digits, real, imag)

    placed = [None] * planes
    placed[0], token = place(0, index)
    token, index = together(token, index)
    placed[1], token = place(1, index)

    def to_members(value):
        return lax.all_to_all(
            value.reshape(group, span, 2 * FX), ("x", "slab"), 0, 0, tiled=True
        ).reshape(group * span, 2 * FX)

    got = to_members(placed[0])
    near, token = together(near, token)
    near = jnp.concatenate(near, axis=0)
    far = lax.ppermute(near, "slab", [(i, i ^ 1) for i in range(slab)])
    table, evidence = weights_table(
        planes, inner, half.reshape(1).astype(I32), images, near, far, offsets, orientations,
        interp_index, token,
    )
    table, got, index = together(table, got, index)
    early = min(2, planes - 1)
    placed[early], token = place(early, index)
    later = token
    tables = lax.all_to_all(
        jnp.broadcast_to(table[None], (group,) + table.shape), ("x", "slab"), 0, 0, tiled=True
    ).reshape(group * number, FX)
    tables, placed[1], later = together(tables, placed[1], later)
    got = [got, to_members(placed[1])]

    def lines_of(k, base=None):
        return partial_lines(cap, pad, got[k], tables, interp_mats, lines, k == 0, base)

    part, short = lines_of(0)
    part, index = together(part, index)
    parts = [part]
    for k in range(early + 1, min(early + 2, planes)):
        placed[k], token = place(k, index)
    placed[early], token = together(placed[early], token)
    got.append(to_members(placed[early]))
    up = down = lax.ppermute(short, "z", sorted({(0, 1), (planes - 1, planes - 2)}))
    for s in range(2, planes):
        part = lines_of(s - 1)
        if s + 1 < planes:
            part, index = together(part, index)
            if placed[s + 1] is None:
                placed[s + 1], _ = place(s + 1, index)
            part, placed[s + 1] = together(part, placed[s + 1])
            got.append(to_members(placed[s + 1]))
        parts.append(part)
        up_send, down_send = relay(planes, s, place_of, parts, up, down, (token, later))
        up = lax.ppermute(up_send, "z", [(p, p + 1) for p in range(s)])
        down = lax.ppermute(down_send, "z", [(p, p - 1) for p in range(planes - s, planes)])
    last = lines_of(planes - 1, volume_in)
    volume = last + up.astype(F32) + down.astype(F32)
    return volume, evidence[:, 0]


def solution(mesh):
    dom, slab = mesh.shape["dom"], mesh.shape["slab"]
    planes = dom // INNER
    fine = Mesh(mesh.devices.reshape(planes, INNER, slab), ("z", "x", "slab"))
    every = ("z", "x", "slab")
    in_specs = (
        P(every, None),
        P(("z", "x"), None),
        P(every, None),
        P(every, None),
        P(),
        P(every, None),
        P(every, None, None),
        P(every, None),
        P(every, None),
    )
    out_specs = (P(every, None), P(every))
    return jax.shard_map(
        functools.partial(body, planes, INNER, slab),
        mesh=fine,
        in_specs=in_specs,
        out_specs=out_specs,
        check_vma=False,
    )
```

```python
import functools
import math

import jax
import jax.numpy as jnp
import numpy as np
from jax import lax
from jax.experimental import pallas as pl
from jax.experimental.pallas import tpu as pltpu
from jax.sharding import Mesh
from jax.sharding import PartitionSpec as P

FY = 256
FX = 128
TX = 4
TY = 4
LIST = 2
OFF = 8
INNER = 2
F32 = jnp.float32
BF16 = jnp.bfloat16
I32 = jnp.int32
STEP = 2.0 * math.pi / FY
SHIFTS = OFF + max(TX, TY) // 2
NSHIFT = 24


def vmem_params(mib):
    return pltpu.CompilerParams(vmem_limit_bytes=mib << 20)


def whole(shape):
    return pl.BlockSpec(shape, lambda *_: (0,) * len(shape))


def cost(flops, nbytes):
    return pl.CostEstimate(flops=int(flops), bytes_accessed=int(nbytes), transcendentals=0)


def iota(shape, axis):
    return lax.broadcasted_iota(I32, shape, axis)


def in_hbm(value):
    return pltpu.with_memory_space_constraint(value, pltpu.HBM)


def split(value):
    high = value.astype(BF16)
    return high, (value - high.astype(F32)).astype(BF16)


def slot_kernel(
    dests, group, pad, place_of, owner_ref, line_from, image_from,
    index_ref, digit_ref, real_ref, imag_ref, hot_ref, line_ref, image_ref, sems,
):
    number = owner_ref.shape[0]
    blocks = number * LIST
    planes = dests // group
    z = lax.axis_index("z")
    lines_in = pltpu.make_async_copy(line_from, line_ref, sems.at[0])
    lines_in.start()
    images_in = pltpu.make_async_copy(image_from, image_ref, sems.at[1])
    images_in.start()

    def widen(k, carry):
        for i in range(8):
            r = k * 8 + i
            at = pl.multiple_of(r * 2 * FX, 2 * FX)
            to = pl.ds(pl.multiple_of(r * number, number), number)
            real_ref[to, :] = image_ref[:, pl.ds(at, FX)].astype(F32)
            imag_ref[to, :] = image_ref[:, pl.ds(at + FX, FX)].astype(F32)
        return carry

    owner = owner_ref[...]
    plane = owner // group
    chunk = jnp.zeros_like(owner)
    for k in range(planes):
        at = functools.reduce(
            lambda value, p: jnp.where(z == p, int(place_of[p, k]), value), range(planes), 0
        )
        chunk = jnp.where(plane == k, at, chunk)
    dest = chunk * group + (owner & (group - 1))
    owner_rows = iota((dests, FY), 0)
    for b in range(blocks):
        n, l = b // LIST, b % LIST
        hot = owner_rows == dest[n : n + 1, l * FY : (l + 1) * FY]
        hot_ref[b * dests : (b + 1) * dests, :] = hot.astype(F32).astype(BF16)
    before = (iota((FY, FY), 0) < iota((FY, FY), 1)).astype(F32).astype(BF16)
    prefix = jnp.dot(hot_ref[...], before, preferred_element_type=F32)
    lines_in.wait()
    running = jnp.zeros((dests, 1), F32)
    lane = iota((1, FY), 1).astype(F32)
    ranks = iota((pad, FY), 0)
    total = jnp.zeros((4 * dests, pad), F32)
    for b in range(blocks):
        n, l = b // LIST, b % LIST
        hot = hot_ref[b * dests : (b + 1) * dests, :].astype(F32)
        part = prefix[b * dests : (b + 1) * dests, :]
        rank = jnp.sum(hot * (part + running), axis=0, keepdims=True).astype(I32)
        running = running + part[:, FY - 1 :] + hot[:, FY - 1 :]
        line = line_ref[n : n + 1, l * FY : (l + 1) * FY]
        digits = [
            hot * lane,
            hot * float(b),
            hot * (line & 255).astype(F32),
            hot * ((line >> 8) + 1).astype(F32),
        ]
        left = jnp.concatenate(digits, axis=0).astype(BF16)
        right = (ranks == rank).astype(F32).astype(BF16)
        total = total + lax.dot_general(
            left, right, (((1,), (1,)), ((), ())), preferred_element_type=F32
        )
    digit_ref[...] = total
    row = total[:dests].astype(I32) * number + (total[dests : 2 * dests].astype(I32) >> 1)
    index_ref[...] = jnp.where(iota((dests, pad), 1) == pad - 1, running.astype(I32), row)
    images_in.wait()
    lax.fori_loop(0, FY // 8, widen, 0)


def row_slots(place_of, owners, lines, images, dests, group, pad):
    number, width = images.shape
    return pl.pallas_call(
        functools.partial(slot_kernel, dests, group, pad, place_of),
        out_shape=(
            jax.ShapeDtypeStruct((dests, pad), I32),
            jax.ShapeDtypeStruct((4 * dests, pad), F32),
            pltpu.VMEM((number * FY, FX), F32),
            pltpu.VMEM((number * FY, FX), F32),
        ),
        in_specs=[pl.BlockSpec(memory_space=pltpu.VMEM)]
        + [pl.BlockSpec(memory_space=pltpu.HBM)] * 2,
        scratch_shapes=[
            pltpu.VMEM((number * LIST * dests, FY), BF16),
            pltpu.VMEM(lines.shape, I32),
            pltpu.VMEM(images.shape, BF16),
            pltpu.SemaphoreType.DMA((2,)),
        ],
        compiler_params=vmem_params(20),
        cost_estimate=cost(3e9, 12e6),
        name="slots",
    )(owners, in_hbm(lines), in_hbm(images))


def place_kernel(
    chunk, cap, index_ref, digit_ref, real_ref, imag_ref, out_ref, token_ref, left_ref, right_ref,
    held, sems,
):
    group = out_ref.shape[0] // (cap + 16)
    pad = index_ref.shape[0] // group
    dests = digit_ref.shape[0] // 4
    words = pad // (2 * FX)
    span = cap + 16
    zeros = jnp.zeros((group * span, FX), F32)

    left_ref[...] = zeros
    right_ref[...] = zeros
    token_ref[...] = jnp.zeros_like(token_ref)
    def member(d, carry):
        start = d * span
        base = d * pad

        def some(i, inner):
            at = base + i * 32
            to = start + i * 32
            spots = [index_ref[at + j] for j in range(32)]
            lefts = [real_ref[pl.ds(spot, 1), :] for spot in spots]
            rights = [imag_ref[pl.ds(spot, 1), :] for spot in spots]
            for j in range(32):
                left_ref[pl.ds(to + j, 1), :] = lefts[j]
                right_ref[pl.ds(to + j, 1), :] = rights[j]
            return inner

        lax.fori_loop(0, (index_ref[base + pad - 1] + 31) // 32, some, 0)
        return carry

    lax.fori_loop(0, group, member, 0)
    copies = []
    for d in range(group):
        start = d * span
        for which in range(4):
            row = which * dests + chunk * group + d
            for word in range(words):
                to = start + cap + which * words + word
                lane = word * 2 * FX
                left_ref[to : to + 1, :] = digit_ref[row : row + 1, lane : lane + FX]
                right_ref[to : to + 1, :] = digit_ref[row : row + 1, lane + FX : lane + 2 * FX]
        at = slice(start, start + span)
        held[at, :FX] = left_ref[at, :].astype(BF16)
        held[at, FX:] = right_ref[at, :].astype(BF16)
        copies.append(pltpu.make_async_copy(held.at[at], out_ref.at[at], sems.at[d]))
        copies[-1].start()
    for copy in copies:
        copy.wait()


def placed_rows(chunk, group, cap, index, digits, real, imag):
    pad = digits.shape[1]
    span = cap + 16
    vmem = pl.BlockSpec(memory_space=pltpu.VMEM)
    return pl.pallas_call(
        functools.partial(place_kernel, chunk, cap),
        grid=(1,),
        out_shape=(pltpu.HBM((group * span, 2 * FX), BF16), jax.ShapeDtypeStruct((8, FX), F32)),
        in_specs=[
            pl.BlockSpec((group * pad,), lambda i: (chunk,), memory_space=pltpu.SMEM),
            vmem,
            vmem,
            vmem,
        ],
        out_specs=(pl.BlockSpec(memory_space=pltpu.HBM), vmem),
        scratch_shapes=[pltpu.VMEM((group * span, FX), F32)] * 2
        + [pltpu.VMEM((group * span, 2 * FX), BF16), pltpu.SemaphoreType.DMA((group,))],
        compiler_params=vmem_params(12),
        cost_estimate=cost(1e5, 1e5),
        name="place",
    )(index, digits, real, imag)


def rotate(real, imag, cosine, sine):
    return real * cosine - imag * sine, real * sine + imag * cosine


def score_kernel(
    planes, inner, half_ref, turn_ref, image_from, near_ref, far_ref, offset_ref, orient_ref,
    interp_ref, token_ref, table_ref, evidence_ref, image_ref, sems,
):
    number = image_ref.shape[0]
    refs = near_ref.shape[0]
    rows_half = FY // 2
    group = 16
    half = half_ref[0]
    copies = []
    for k in range(4):
        side = half if k < 2 else 1 - half
        quarter = FY * FX // 2
        at = pl.ds(pl.multiple_of((side * 2 + k % 2) * quarter, quarter), quarter)
        copies.append(
            pltpu.make_async_copy(image_from.at[:, at], image_ref.at[:, at], sems.at[k])
        )
        copies[-1].start()
    off_x = offset_ref[:, 0:1]
    off_y = offset_ref[:, 1:2]
    lane = iota((number, FX), 1)

    def wave(units):
        angle = STEP * (units & (FY - 1)).astype(F32)
        return jnp.cos(angle), jnp.sin(angle)

    col_cos, col_sin = wave(-lane * off_x)
    one_cos, one_sin = wave(jnp.broadcast_to(-off_y, (number, FX)))
    ref_lane = iota((1, FX), 1)
    x1_cos, x1_sin = wave(jnp.broadcast_to(ref_lane, (refs, FX)))
    x2_cos, x2_sin = wave(jnp.broadcast_to(2 * ref_lane, (refs, FX)))

    def shifts(real, imag, c1, s1, c2, s2):
        rc, rs, ic, is_ = real * c1, real * s1, imag * c1, imag * s1
        pairs = [
            (real * c2 + imag * s2, imag * c2 - real * s2),
            (rc + is_, ic - rs),
            (real, imag),
            (rc - is_, ic + rs),
        ]
        return pairs

    def stacked(pairs):
        return jnp.concatenate(
            [jnp.concatenate([p.astype(BF16), q.astype(BF16)], axis=1) for p, q in pairs],
            axis=0,
        )

    def run(ref, first, total, waits):
        start_cos, start_sin = wave(-(lane * off_x + first * off_y))

        def block(k, carry):
            total, cosine, sine = carry
            lefts, rights = [], []
            for i in range(group):
                r = first + k * group + i
                at = pl.multiple_of(r * 2 * FX, 2 * FX)
                at_ref = pl.multiple_of((k * group + i) * 2 * FX, 2 * FX)
                real = image_ref[:, pl.ds(at, FX)].astype(F32)
                imag = image_ref[:, pl.ds(at + FX, FX)].astype(F32)
                real, imag = rotate(real, imag, cosine, sine)
                cosine, sine = rotate(cosine, sine, one_cos, one_sin)
                lefts.append(
                    stacked(
                        shifts(
                            real, imag, turn_ref[0, r], turn_ref[1, r], turn_ref[2, r], turn_ref[3, r]
                        )
                    )
                )
                real = ref[:, pl.ds(at_ref, FX)].astype(F32)
                imag = ref[:, pl.ds(at_ref + FX, FX)].astype(F32)
                rights.append(stacked(shifts(real, imag, x1_cos, -x1_sin, x2_cos, -x2_sin)))
            total = total + lax.dot_general(
                jnp.concatenate(lefts, axis=1),
                jnp.concatenate(rights, axis=1),
                (((1,), (1,)), ((), ())),
                preferred_element_type=F32,
            )
            return total, cosine, sine

        carry = (total, start_cos, start_sin)
        turns = rows_half // group // len(waits)
        for k, wait in enumerate(waits):
            wait.wait()
            carry = lax.fori_loop(k * turns, (k + 1) * turns, block, carry)
        return carry[0]

    total = jnp.zeros((TY * number, TX * refs), F32)
    total = run(near_ref, half * rows_half, total, copies[:2])
    total = run(far_ref, (1 - half) * rows_half, total, copies[2:])
    total = total * (1.0 / math.sqrt(FY * 2 * FX))
    parts = [total[b * number : (b + 1) * number, :] for b in range(TY)]
    top = functools.reduce(jnp.maximum, parts)
    top = jnp.max(top, axis=1, keepdims=True)
    mass = sum(jnp.sum(jnp.exp(part - top), axis=1, keepdims=True) for part in parts)
    evidence = top + jnp.log(mass)
    evidence_ref[...] = jnp.broadcast_to(evidence, (number, FX))
    spot = iota((number, TX * refs), 1)
    shift_of = spot // refs
    spot = spot & (refs - 1)
    local = refs // (planes * inner)
    plane = lax.axis_index("z") - spot // (inner * local)
    plane = jnp.where(plane < 0, plane + planes, plane)
    column = lax.axis_index("x") ^ ((spot // local) & (inner - 1))
    name = (plane * inner + column) * local + (spot & (local - 1))
    slot = iota((number, FX), 1)
    table = jnp.where(slot == 32, off_x.astype(F32), 0.0)
    table = jnp.where(slot == 33, off_y.astype(F32), table)
    for l in range(LIST):
        table = jnp.where(slot == 34 + l, interp_ref[:, l : l + 1].astype(F32), table)
        for b in range(TY):
            weights = jnp.exp(parts[b] - evidence)
            for a in range(TX):
                chosen = (name == orient_ref[:, l : l + 1]) & (shift_of == a)
                value = jnp.sum(jnp.where(chosen, weights, 0.0), axis=1, keepdims=True)
                table = jnp.where(slot == l * 16 + b * TX + a, value, table)
    table_ref[...] = table


def weights_table(
    planes, inner, half, images, near, far, offsets, orientations, interp_index, token
):
    number = images.shape[0]
    turn = np.arange(FY) * STEP
    turns = np.stack([np.cos(turn), np.sin(turn), np.cos(2 * turn), np.sin(2 * turn)])
    smem = pl.BlockSpec(memory_space=pltpu.SMEM)
    vmem = pl.BlockSpec(memory_space=pltpu.VMEM)
    return pl.pallas_call(
        functools.partial(score_kernel, planes, inner),
        out_shape=[jax.ShapeDtypeStruct((number, FX), F32)] * 2,
        in_specs=[smem, smem, pl.BlockSpec(memory_space=pltpu.HBM)] + [vmem] * 6,
        scratch_shapes=[pltpu.VMEM(images.shape, BF16), pltpu.SemaphoreType.DMA((4,))],
        compiler_params=vmem_params(14),
        cost_estimate=cost(1e9, 5e6),
        name="scores",
    )(
        half, jnp.asarray(turns, F32), in_hbm(images), near, far, offsets, orientations,
        interp_index, token,
    )


def wave_table():
    shift = np.arange(NSHIFT)[:, None] - SHIFTS
    angle = STEP * ((shift * np.arange(FX)[None, :]) % FY)
    table = np.concatenate(
        [
            np.concatenate([np.cos(angle), np.sin(angle)], axis=1),
            np.concatenate([-np.sin(angle), np.cos(angle)], axis=1),
        ],
        axis=0,
    ).astype(np.float32)
    high = table.astype(jnp.bfloat16)
    low = (table - high.astype(np.float32)).astype(jnp.bfloat16)
    return np.concatenate([high, high, low], axis=0)


def gather_kernel(cap, pad, first, row_ref, table_ref, wave_ref, mats_ref, *refs):
    base_ref = refs[0] if first is None else None
    out_ref, mixed_ref, line_ref = refs[1 if first is None else 0], refs[-2], refs[-1]
    lines = out_ref.shape[0]
    members = table_ref.shape[0]
    count = mats_ref.shape[0]
    span = cap + 16
    group = row_ref.shape[0] // span
    words = pad // (2 * FX)
    low_count = count // 2
    table_high, table_low = split(table_ref[:, :64])
    picks = jnp.concatenate([table_high, table_low], axis=1)
    number = members // group
    mats = jnp.concatenate(
        [mats_ref[:low_count].reshape(low_count * FX, FX), mats_ref[low_count:].reshape(low_count * FX, FX)],
        axis=1,
    )
    def block(s, carry):
        at = pl.multiple_of(s * span, 16)
        extra = row_ref[pl.ds(at + cap, 16), :].astype(F32)
        digit = [
            jnp.concatenate(
                [extra[which * words + word : which * words + word + 1] for word in range(words)],
                axis=1,
            )[:, :cap].astype(I32)
            for which in range(4)
        ]
        r = digit[0]
        member = s * number + (digit[1] >> 1)
        front = (digit[1] & 1) == 0
        line_ref[s] = digit[2] + (digit[3] - 1) * 256
        hot = (iota((members, cap), 0) == member).astype(F32).astype(BF16)
        got = lax.dot_general(picks, hot, (((0,), (0,)), ((), ())), preferred_element_type=F32)
        got = got[:64] + got[64:]
        weight = jnp.where(front, got[0:16], got[16:32])
        off_x = got[32:33].astype(I32)
        off_y = got[33:34].astype(I32)
        interp = jnp.where(front, got[34:35], got[35:36])
        sub = iota((8, cap), 0)
        units = r * ((sub & 3) - TY // 2 - off_y) - jnp.where(sub >= 4, FY // 4, 0)
        wave = jnp.cos(STEP * (units & (FY - 1)).astype(F32))
        gate_real = sum(weight[b * TX : (b + 1) * TX] * wave[b : b + 1] for b in range(TY))
        gate_imag = sum(weight[b * TX : (b + 1) * TX] * wave[4 + b : 5 + b] for b in range(TY))
        spot = iota((NSHIFT, cap), 0) + off_x
        coef_real = jnp.zeros((NSHIFT, cap), F32)
        coef_imag = jnp.zeros((NSHIFT, cap), F32)
        for a in range(TX):
            here = spot == a - TX // 2 + SHIFTS
            coef_real = jnp.where(here, gate_real[a : a + 1], coef_real)
            coef_imag = jnp.where(here, gate_imag[a : a + 1], coef_imag)
        high, low = split(jnp.concatenate([coef_real, coef_imag], axis=0))
        coef = jnp.concatenate([high, low, high], axis=0)
        phase = lax.dot_general(
            coef, wave_ref[...], (((0,), (0,)), ((), ())), preferred_element_type=F32
        )
        values = row_ref[pl.ds(at, cap), :].astype(F32)
        real, imag = rotate(values[:, :FX], values[:, FX:], phase[:, :FX], phase[:, FX:])
        slices = jnp.concatenate([real, imag], axis=0).astype(BF16)
        column = jnp.transpose(jnp.broadcast_to(interp, (8, cap)))[:, 0:1]
        column = jnp.broadcast_to(column, (cap, FX)).astype(I32)
        column = jnp.concatenate([column, column], axis=0)
        which = jnp.where(column >= low_count, column - low_count, column)
        zero = jnp.zeros_like(slices)
        pieces = [jnp.where(which == q, slices, zero) for q in range(low_count)]
        mixed = jnp.dot(jnp.concatenate(pieces, axis=1), mats, preferred_element_type=F32)
        mixed = jnp.where(column >= low_count, mixed[:, FX:], mixed[:, :FX]).astype(BF16)
        to = pl.ds(pl.multiple_of(s * cap, 16), cap)
        mixed_ref[to, :FX] = mixed[:cap]
        mixed_ref[to, FX:] = mixed[cap:]
        return carry

    lax.fori_loop(0, group, block, 0, unroll=2 if first else 2)
    line = jnp.concatenate([line_ref[s] for s in range(group)], axis=1)
    tile = min(512, lines // 2)
    rows = iota((tile, group * cap), 0)
    for at in range(0, lines, tile):
        hot = jnp.where(rows == line - at, 1.0, 0.0).astype(BF16)
        value = jnp.dot(hot, mixed_ref[...], preferred_element_type=F32)
        if base_ref is not None:
            value = value + base_ref[at : at + tile, :]
        out_ref[at : at + tile, :] = value
        if first:
            refs[1][at : at + tile, :] = value.astype(BF16)


def partial_lines(cap, pad, rows, table, mats, lines, first, base=None):
    group = rows.shape[0] // (cap + 16)
    shape = jax.ShapeDtypeStruct((lines, 2 * FX), F32)
    short = jax.ShapeDtypeStruct((lines, 2 * FX), BF16)
    vmem = pl.BlockSpec(memory_space=pltpu.VMEM)
    extra = () if base is None else (base,)
    return pl.pallas_call(
        functools.partial(gather_kernel, cap, pad, None if extra else first),
        out_shape=(shape, short) if first else shape,
        in_specs=[vmem] * (4 + len(extra)),
        scratch_shapes=[
            pltpu.VMEM((group * cap, 2 * FX), BF16),
            pltpu.VMEM((group, 1, cap), I32),
        ],
        compiler_params=vmem_params(20),
        cost_estimate=cost(1e6, 1e5),
        name="lines",
    )(in_hbm(rows), table, jnp.asarray(wave_table()), mats, *extra)


def relay_kernel(planes, step, place_of, *refs):
    up_from, down_from, _, _, up_to, down_to, came_ref, sent_ref, sems = refs[-9:]
    parts = refs[:-9]
    z = lax.axis_index("z")
    lines = up_to.shape[0]
    tile = min(512, lines)
    tiles = lines // tile

    def pull(came, way, k):
        at = pl.ds(k * tile, tile)
        return pltpu.make_async_copy(came.at[at], came_ref.at[way, at], sems.at[0, way, k])

    def push(out, way, k):
        at = pl.ds(k * tile, tile)
        return pltpu.make_async_copy(sent_ref.at[way, at], out.at[at], sems.at[1, way, k])

    for p in range(planes):
        jobs = []
        if p < step:
            jobs.append((0, place_of[p, planes - step + p], up_from if p > 0 else None, up_to))
        if p >= planes - step:
            edge = p == planes - 1
            jobs.append((1, place_of[p, p - planes + step], None if edge else down_from, down_to))
        if jobs:

            @pl.when(z == p)
            def _(jobs=jobs):
                for way, _, came, _ in jobs:
                    for k in range(tiles if came is not None else 0):
                        pull(came, way, k).start()
                for way, index, came, out in jobs:
                    for k in range(tiles):
                        at = slice(k * tile, (k + 1) * tile)
                        value = parts[index][at, :]
                        if came is not None:
                            pull(came, way, k).wait()
                            value = value + came_ref[way, at, :].astype(F32)
                        sent_ref[way, at, :] = value.astype(BF16)
                        push(out, way, k).start()
                for way, _, _, out in jobs:
                    for k in range(tiles):
                        push(out, way, k).wait()


def relay(planes, step, place_of, parts, up, down, tokens):
    vmem = pl.BlockSpec(memory_space=pltpu.VMEM)
    hbm = pl.BlockSpec(memory_space=pltpu.HBM)
    lines = up.shape[0]
    return pl.pallas_call(
        functools.partial(relay_kernel, planes, step, place_of),
        out_shape=[pltpu.HBM(up.shape, BF16)] * 2,
        in_specs=[vmem] * len(parts) + [hbm, hbm, vmem, vmem],
        out_specs=[hbm, hbm],
        scratch_shapes=[
            pltpu.VMEM((2, lines, 2 * FX), BF16),
            pltpu.VMEM((2, lines, 2 * FX), BF16),
            pltpu.SemaphoreType.DMA((2, 2, lines // min(512, lines))),
        ],
        compiler_params=vmem_params(10),
        cost_estimate=cost(60e9, 8e6),
        name="relay",
    )(*parts, in_hbm(up), in_hbm(down), *tokens)


def finish_kernel(last_ref, up_from, down_from, volume_to, came_ref, sum_ref, sems):
    lines = last_ref.shape[0]
    tiles = sems.shape[1]
    tile = lines // tiles

    def copies(k):
        at = pl.ds(k * tile, tile)
        return (
            pltpu.make_async_copy(up_from.at[at], came_ref.at[0, at], sems.at[0, k]),
            pltpu.make_async_copy(down_from.at[at], came_ref.at[1, at], sems.at[1, k]),
            pltpu.make_async_copy(sum_ref.at[at], volume_to.at[at], sems.at[2, k]),
        )

    for k in range(tiles):
        up, down, _ = copies(k)
        up.start()
        down.start()
    for k in range(tiles):
        up, down, out = copies(k)
        up.wait()
        down.wait()
        at = slice(k * tile, (k + 1) * tile)
        came = came_ref[0, at, :].astype(F32) + came_ref[1, at, :].astype(F32)
        sum_ref[at, :] = last_ref[at, :] + came
        out.start()
    for k in range(tiles):
        copies(k)[2].wait()


def finish(last, up, down):
    hbm = pl.BlockSpec(memory_space=pltpu.HBM)
    return pl.pallas_call(
        finish_kernel,
        out_shape=pltpu.HBM(last.shape, F32),
        in_specs=[pl.BlockSpec(memory_space=pltpu.VMEM), hbm, hbm],
        out_specs=hbm,
        scratch_shapes=[
            pltpu.VMEM((2,) + up.shape, BF16),
            pltpu.VMEM(last.shape, F32),
            pltpu.SemaphoreType.DMA((3, 4)),
        ],
        compiler_params=vmem_params(12),
        cost_estimate=cost(1e6, 8e6),
        name="finish",
    )(last, in_hbm(up), in_hbm(down))


def together(*values):
    return lax.optimization_barrier(values)


def block_order(planes):
    return np.array(
        [sorted(range(planes), key=lambda d: (-abs(d - z), -d)) for z in range(planes)], np.int32
    )


def body(
    planes, inner, slab,
    images, references, offsets, orientations, interp_mats, interp_index, owners, line_index, volume_in,
):
    number = images.shape[0]
    lines = volume_in.shape[0]
    group = inner * slab
    devices = planes * group
    rows_all = number * LIST * FY
    cap = max(2, 7 * rows_all // (4 * devices))
    span = cap + 16
    pad = -(-(cap + 1) // (2 * FX)) * 2 * FX
    half = lax.axis_index("slab") % 2

    local = references.shape[0]
    width = references.shape[1]
    mine = lax.dynamic_slice_in_dim(references, half * (width // 2), width // 2, axis=1)
    block = [mine]
    for e in range(1, inner):
        block.append(lax.ppermute(mine, "x", [(i, i ^ e) for i in range(inner)]))

    place_of = np.argsort(block_order(planes), axis=1).astype(np.int32)
    index, digits, real, imag = row_slots(
        place_of,
        owners.reshape(number, LIST * FY),
        line_index,
        images,
        devices,
        group,
        pad,
    )
    block, index = together(block, index)
    block = jnp.concatenate(block, axis=0)
    near = [block]
    for shift in range(1, planes):
        near.append(lax.ppermute(block, "z", [(p, (p + shift) % planes) for p in range(planes)]))
    index = index.reshape(devices * pad)

    def place(k, index):
        return placed_rows(k, group, cap, index, digits, real, imag)

    placed = [None] * planes
    placed[0], token = place(0, index)
    token, index = together(token, index)
    placed[1], token = place(1, index)

    def to_members(value):
        return lax.all_to_all(
            value.reshape(group, span, 2 * FX), ("x", "slab"), 0, 0, tiled=True
        ).reshape(group * span, 2 * FX)

    got = to_members(placed[0])
    near, token = together(near, token)
    near = jnp.concatenate(near, axis=0)
    far = lax.ppermute(near, "slab", [(i, i ^ 1) for i in range(slab)])
    table, evidence = weights_table(
        planes, inner, half.reshape(1).astype(I32), images, near, far, offsets, orientations,
        interp_index, token,
    )
    table, got, index = together(table, got, index)
    early = min(2, planes - 1)
    placed[early], token = place(early, index)
    later = token
    tables = lax.all_to_all(
        jnp.broadcast_to(table[None], (group,) + table.shape), ("x", "slab"), 0, 0, tiled=True
    ).reshape(group * number, FX)
    tables, placed[1], later = together(tables, placed[1], later)
    got = [got, to_members(placed[1])]

    def lines_of(k, base=None):
        return partial_lines(cap, pad, got[k], tables, interp_mats, lines, k == 0, base)

    part, short = lines_of(0)
    part, index = together(part, index)
    parts = [part]
    for k in range(early + 1, min(early + 2, planes)):
        placed[k], token = place(k, index)
    placed[early], token = together(placed[early], token)
    got.append(to_members(placed[early]))
    up = down = lax.ppermute(short, "z", sorted({(0, 1), (planes - 1, planes - 2)}))
    for s in range(2, planes):
        part = lines_of(s - 1)
        if s + 1 < planes:
            part, index = together(part, index)
            if placed[s + 1] is None:
                placed[s + 1], _ = place(s + 1, index)
            part, placed[s + 1] = together(part, placed[s + 1])
            got.append(to_members(placed[s + 1]))
        parts.append(part)
        up_send, down_send = relay(planes, s, place_of, parts, up, down, (token, later))
        up = lax.ppermute(up_send, "z", [(p, p + 1) for p in range(s)])
        down = lax.ppermute(down_send, "z", [(p, p - 1) for p in range(planes - s, planes)])
    last = lines_of(planes - 1, volume_in)
    volume = finish(last, up, down)
    return volume, evidence[:, 0]


def solution(mesh):
    dom, slab = mesh.shape["dom"], mesh.shape["slab"]
    planes = dom // INNER
    fine = Mesh(mesh.devices.reshape(planes, INNER, slab), ("z", "x", "slab"))
    every = ("z", "x", "slab")
    in_specs = (
        P(every, None),
        P(("z", "x"), None),
        P(every, None),
        P(every, None),
        P(),
        P(every, None),
        P(every, None, None),
        P(every, None),
        P(every, None),
    )
    out_specs = (P(every, None), P(every))
    return jax.shard_map(
        functools.partial(body, planes, INNER, slab),
        mesh=fine,
        in_specs=in_specs,
        out_specs=out_specs,
        check_vma=False,
    )
```
